128 devices in a mesh: batch: 16 (over y, z), proto: 8 (over x, core).
Axes of the slice: x: 4, y: 4, z: 4, core: 2. Of those that a mesh axis runs over, the one named last changes fastest.
Arguments:
- embeddings: bfloat16 [16384, 1024], P('batch'), may hold values from -6 to 6
- pairing: int32 [16384], P('batch'), may hold values from 0 to 1023, as said below
- w_in: bfloat16 [1024, 512], replicated, may hold values from -0.1875 to 0.1875
- w_out: bfloat16 [512, 128], replicated, may hold values from -0.25 to 0.25
- prototypes: bfloat16 [32768, 128], P('proto'), may hold values from -1.8 to 1.8
Outputs:
- grad_in: float32 [1024, 512], replicated
- grad_out: float32 [512, 128], replicated
- grad_proto: float32 [32768, 128], P('proto')
The draws below stay inside these ranges and needn't reach their ends.
Inputs may be any that keep to these rules, and one draw needn't show every extreme that they name: Within every aligned block of 1024 rows the views come in pairs: pairing[pairing[i]] = i and pairing[i] != i, both counted within the block.
All inputs are finite; a program needn't handle non-finite values.
Results may differ from the reference program's by a relative error of at most 0.007.
Values may be sent and summed in bfloat16 or wider, within the bound.
A program may use at most 64 MiB of HBM per device.

```python
import math
import jax
import jax.numpy as jnp
from jax import lax

E = 1024
H = 512
Z = 128
K = 32768
R_DEV = 1024
ITERS = 3
ROWS = 16384


def draw_pairing(key, part):

    def one_block(block_key):
        order = jax.random.permutation(block_key, R_DEV).astype(jnp.int32)
        partners = order.reshape(R_DEV // 2, 2)[:, ::-1].reshape(R_DEV)
        return jnp.zeros((R_DEV,), jnp.int32).at[order].set(partners)
    keys = jax.random.split(jax.random.fold_in(key, 11), ROWS // R_DEV)
    return jax.vmap(one_block)(keys).reshape(ROWS).astype(jnp.int32)


def draw_prototypes(key, part):
    base_key = jax.random.fold_in(key, 23)
    first, second = jax.random.split(base_key)
    values = jnp.clip(jax.random.normal(first, (K, Z), jnp.float32), -6.0, 6.0)
    scale = jnp.exp(jax.random.uniform(second, (K, 1), jnp.float32, math.log(0.03), math.log(0.3)))
    return (values * scale).astype(jnp.bfloat16)


def block_levels(rng, dims, pieces, smallest, largest):
    def one(position, blocks):
        heights = jax.random.uniform(jax.random.fold_in(jax.random.fold_in(rng, 6), position), (blocks,), jnp.float32, smallest / len(pieces), largest / len(pieces))
        return jnp.repeat(jnp.exp(heights), dims[position] // blocks).reshape((-1,) + (1,) * (len(dims) - position - 1))

    gain = one(*pieces[0])
    for cut in pieces[1:]:
        gain = gain * one(*cut)
    return gain


def scatter_about(stream_key, extent, deviation, bound, cuts=(), kind=jnp.bfloat16):
    loudness = block_levels(stream_key, extent, cuts, -0.22, 0.18) if cuts else 1.0
    result = jax.random.normal(stream_key, extent, jnp.float32) * deviation * loudness
    return jnp.minimum(jnp.maximum(result, -bound), bound).astype(kind)


def setup_inputs(seed: int = 0) -> dict:
    seeds = jax.random.split(jax.random.key(seed), 6)
    return {
        "embeddings": scatter_about(seeds[0], (ROWS, E), 1.0, 6.0, ((0, 16),)),
        "pairing": draw_pairing(jax.random.fold_in(seeds[5], 71), 0),
        "w_in": scatter_about(seeds[2], (E, H), E ** -0.5, 0.1875),
        "w_out": scatter_about(seeds[3], (H, Z), H ** -0.5, 0.25),
        "prototypes": draw_prototypes(jax.random.fold_in(seeds[5], 71), 0),
    }


norm_eps = 1e-06
code_temp = 0.05
pred_temp = 0.1
loss_scale = 64.0

def head_forward(rows_in, w_in, w_out):
    pre_act = jnp.dot(rows_in, w_in, preferred_element_type=jnp.float32)
    hidden = jax.nn.gelu(pre_act).astype(jnp.bfloat16)
    raw_out = jnp.dot(hidden, w_out, preferred_element_type=jnp.float32)
    inv_norm = lax.rsqrt(lax.optimization_barrier(jnp.sum(raw_out * raw_out, axis=1, keepdims=True)) + norm_eps)
    return (pre_act, hidden, raw_out, inv_norm, (raw_out * inv_norm).astype(jnp.bfloat16))

def head_backward(rows_in, w_out, pre_act, hidden, raw_out, inv_norm, view_grad):
    along = lax.optimization_barrier(jnp.sum(raw_out * view_grad, axis=1, keepdims=True))
    d_raw = (inv_norm * view_grad - raw_out * (inv_norm * inv_norm * inv_norm) * along).astype(jnp.bfloat16)
    grad_out = lax.dot_general(hidden, d_raw, (((0,), (0,)), ((), ())), preferred_element_type=jnp.float32)
    d_hidden = lax.dot_general(d_raw, w_out, (((1,), (1,)), ((), ())), preferred_element_type=jnp.float32)
    _, pullback = jax.vjp(jax.nn.gelu, pre_act)
    d_pre = pullback(d_hidden)[0].astype(jnp.bfloat16)
    grad_in = lax.dot_general(rows_in, d_pre, (((0,), (0,)), ((), ())), preferred_element_type=jnp.float32)
    return (grad_in, grad_out)

def unit_rows(prototypes):
    proto_f = prototypes.astype(jnp.float32)
    proto_inv = lax.rsqrt(lax.optimization_barrier(jnp.sum(proto_f * proto_f, axis=1, keepdims=True)) + norm_eps)
    return (proto_f, proto_inv, (proto_f * proto_inv).astype(jnp.bfloat16))

def scores_of(rows_in, unit):
    return lax.dot_general(rows_in, unit, (((1,), (1,)), ((), ())), preferred_element_type=jnp.float32)

def reference(embeddings, pairing, w_in, w_out, prototypes):
    pre_act, hidden, raw_out, inv_norm, views = head_forward(embeddings, w_in, w_out)
    proto_f, proto_inv, unit = unit_rows(prototypes)
    block_rows = min(R_DEV, 512)
    count = ROWS // block_rows
    offsets = jnp.arange(ROWS, dtype=jnp.int32) // R_DEV * R_DEV
    mate_index = (offsets + pairing).astype(jnp.int32)
    mates = views[mate_index]
    view_blocks = views.reshape(count, block_rows, Z)
    row_scale = jnp.ones((ROWS,), jnp.float32)
    col_scale = jnp.ones((K,), jnp.float32)
    for sweep in range(ITERS):

        def add_columns(running, pair):
            block, scale = pair
            found = lax.optimization_barrier(jnp.sum(scale[:, None] * jnp.exp(scores_of(block, unit) / code_temp), axis=0))
            return (running + found, None)
        col_total, _ = lax.scan(add_columns, jnp.zeros((K,), jnp.float32), (view_blocks, row_scale.reshape(count, block_rows)))
        col_scale = 1.0 / col_total

        def add_rows(block, col_scale=col_scale):
            return lax.optimization_barrier(jnp.sum(jnp.exp(scores_of(block, unit) / code_temp) * col_scale[None, :], axis=1))
        row_scale = (1.0 / lax.map(add_rows, view_blocks)).reshape(ROWS)

    def add_totals(block):
        return lax.optimization_barrier(jnp.sum(jnp.exp(scores_of(block, unit) / pred_temp), axis=1))
    totals = lax.map(add_totals, view_blocks).reshape(ROWS)
    mate_scale = row_scale[mate_index]

    def finish(running, pair):
        block, mate_block, mate_row, total = pair
        scores = scores_of(block, unit)
        mate_scores = scores_of(mate_block, unit)
        predicted = jnp.exp(scores / pred_temp) / total[:, None]
        codes = mate_row[:, None] * jnp.exp(mate_scores / code_temp) * col_scale[None, :]
        d_scores = ((predicted - codes) * (loss_scale / pred_temp)).astype(jnp.bfloat16)
        view_part = jnp.dot(d_scores, unit, preferred_element_type=jnp.float32)
        running = running + lax.dot_general(d_scores, block, (((0,), (0,)), ((), ())), preferred_element_type=jnp.float32)
        return (running, view_part)
    unit_grad, view_parts = lax.scan(finish, jnp.zeros((K, Z), jnp.float32), (view_blocks, mates.reshape(count, block_rows, Z), mate_scale.reshape(count, block_rows), totals.reshape(count, block_rows)))
    view_grad = view_parts.reshape(ROWS, Z)
    along = lax.optimization_barrier(jnp.sum(proto_f * unit_grad, axis=1, keepdims=True))
    grad_proto = proto_inv * unit_grad - proto_f * (proto_inv * proto_inv * proto_inv) * along
    grad_in, grad_out = head_backward(embeddings, w_out, pre_act, hidden, raw_out, inv_norm, view_grad)
    return (grad_in, grad_out, grad_proto)
```

```python
import math

import jax
import jax.numpy as jnp
from jax import lax
from jax.experimental import pallas as pl
from jax.experimental.pallas import tpu as pltpu
from jax.sharding import PartitionSpec as P

ITERS = 3
norm_eps = 1e-06
loss_gain = 64.0 / 0.1
half_log2 = 10.0 * math.log2(math.e)
gelu_a = math.sqrt(2.0 / math.pi)
gelu_b = 0.044715

F32, BF16 = jnp.float32, jnp.bfloat16
MESH = pl.DeviceIdType.MESH
NB, NP = 16, 8
R, E, H, Z, W = 1024, 1024, 512, 128, 4096
RC = R // NP
CC = W // NB
WV = W // 128


def dot(a, b):
    return jnp.dot(a, b, preferred_element_type=F32)


def dot_t(a, b):
    return lax.dot_general(a, b, (((1,), (1,)), ((), ())), preferred_element_type=F32)


def dot_tl(a, b):
    return lax.dot_general(a, b, (((0,), (0,)), ((), ())), preferred_element_type=F32)


def iota(shape, dim):
    return lax.broadcasted_iota(jnp.int32, shape, dim)


def onehot(mask):
    return jnp.where(mask, 1.0, 0.0).astype(BF16)


def aligned(i, n):
    return pl.ds(pl.multiple_of(i * n, n), n)


def as_row(x):
    return jnp.concatenate([x[k : k + 1, :] for k in range(x.shape[0])], axis=1)


def kernel(
    emb, pairing, w_in, w_out, proto,
    gin, gout, gproto,
    pre, hidden, raw, perm, perm_t, views, views_t, unit, eh, dsc,
    tot_acc, row_b, tot_b, raw_own, c_ref,
    col_send, col_recv, row_send, row_recv,
    vun, vg_send, vg_recv, vg_own, dr_send, dr_all, d_raw, d_pre,
    ug_send, ug_recv, ug_own, gp_send,
    go_f, go_send, go_recv, goa_send, gi_f, gi_send, gi_recv, gx_send,
    col_sem, row_sem, vg_sem, dr_sem, ug_sem, gp_sem, go_sem, goa_sem, gi_sem, gx_sem, gb_sem, gc_sem,
):
    b = lax.axis_index("batch")
    p = lax.axis_index("proto")
    x, core = p // 2, p % 2

    def batch_peer(k):
        return (lax.rem(b + k, NB), p)

    def batch_source(k):
        return lax.rem(b + NB - k, NB)

    def proto_peer(k):
        return (b, lax.rem(p + k, NP))

    def proto_source(k):
        return lax.rem(p + NP - k, NP)

    def copy(src, dst, sem, k, device):
        return pltpu.make_async_remote_copy(
            src_ref=src, dst_ref=dst, send_sem=sem.at[0, k], recv_sem=sem.at[1, k],
            device_id=device, device_id_type=MESH,
        )

    barrier = pltpu.get_barrier_semaphore()

    @pl.loop(1, NB)
    def _(k):
        pl.semaphore_signal(barrier, inc=1, device_id=batch_peer(k), device_id_type=MESH)

    @pl.loop(1, NP)
    def _(k):
        pl.semaphore_signal(barrier, inc=1, device_id=proto_peer(k), device_id_type=MESH)

    @pl.loop(0, R // 256)
    def _(i):
        rows = aligned(i, 256)
        v = dot(emb[rows, :], w_in[...])
        pre[rows, :] = v
        hid = (0.5 * v * (1.0 + jnp.tanh(gelu_a * (v + gelu_b * (v * v * v))))).astype(BF16)
        hidden[rows, :] = hid
        out = dot(hid, w_out[...])
        raw[rows, :] = out
        inv = lax.rsqrt(jnp.sum(out * out, axis=1, keepdims=True) + norm_eps)
        vun[rows, :] = (out * inv).astype(BF16)

    mate = pairing[...]
    lead = mate > iota((8, 128), 0) * 128 + iota((8, 128), 1)
    lead_f = jnp.where(lead, 1.0, 0.0)
    within = dot(lead_f, jnp.where(iota((128, 128), 0) < iota((128, 128), 1), 1.0, 0.0))
    chunk = dot(lead_f, jnp.ones((128, 128), F32))
    before = [jnp.zeros((1, 128), F32)]
    for k in range(7):
        before.append(before[-1] + chunk[k : k + 1, :])
    rank = within + jnp.concatenate(before, axis=0)
    high = jnp.floor(rank * (1.0 / 32.0))
    low = rank - 32.0 * high
    mate_row = as_row(mate)

    @pl.loop(0, 8)
    def _(i):
        perm[aligned(i, 128), :] = onehot(mate_row == iota((128, R), 0) + i * 128)

    halves = jnp.concatenate([as_row(high), as_row(low), jnp.zeros((14, R), F32)], axis=0).astype(BF16)
    of_mate = dot(halves, perm[...])
    lead_row = as_row(lead_f)
    rank_row = jnp.where(lead_row > 0.5, as_row(rank), 32.0 * of_mate[0:1, :] + of_mate[1:2, :])
    pos = rank_row + 64.0 * jnp.floor(rank_row * (1.0 / 64.0)) + jnp.where(lead_row > 0.5, 0.0, 64.0)
    pos = pos.astype(jnp.int32)

    @pl.loop(0, 8)
    def _(i):
        perm[aligned(i, 128), :] = onehot(pos == iota((128, R), 0) + i * 128)

    views[...] = dot(perm[...], vun[...]).astype(BF16)

    @pl.loop(0, W // 256)
    def _(i):
        rows = aligned(i, 256)
        f = proto[rows, :].astype(F32)
        inv = lax.rsqrt(jnp.sum(f * f, axis=1, keepdims=True) + norm_eps)
        unit[rows, :] = (f * inv).astype(BF16)

    tot_acc[...] = jnp.zeros_like(tot_acc)

    @pl.loop(0, W // 512)
    def _(j):
        cols = aligned(j, 512)
        u = unit[cols, :]

        def some_rows(i, acc):
            rows = aligned(i, 256)
            e = jnp.exp2(dot_t(views[rows, :], u) * half_log2)
            eh[rows, cols] = e
            tot_acc[rows, :] += (e[:, 0:128] + e[:, 128:256]) + (e[:, 256:384] + e[:, 384:512])
            return acc + jnp.sum((e * e).reshape(32, 8, 512), axis=0)

        acc = lax.fori_loop(0, R // 256, some_rows, jnp.zeros((8, 512), F32))
        line = jnp.sum(acc, axis=0, keepdims=True)
        for m in range(4):
            col_send[0, pl.ds(j * 4 + m, 1), :] = line[:, m * 128 : m * 128 + 128]

    pl.semaphore_wait(barrier, NB - 1 + NP - 1)

    def start_columns(it):
        @pl.loop(1, NB)
        def _(k):
            copy(col_send.at[it], col_recv.at[it, k], col_sem.at[it], k, batch_peer(k)).start()

    def finish_columns(it):
        @pl.loop(1, NB)
        def _(k):
            copy(col_send.at[it], col_recv.at[it, k], col_sem.at[it], k, batch_peer(k)).wait_recv()

        total = col_send[it]
        for k in range(1, NB):
            total = total + col_recv[it, k]
        c_ref[...] = 1.0 / total

    def start_rows(slot):
        @pl.loop(1, NP)
        def _(k):
            copy(row_send.at[slot], row_recv.at[slot, k], row_sem.at[slot], k, proto_peer(k)).start()

    def finish_rows(slot):
        @pl.loop(1, NP)
        def _(k):
            copy(row_send.at[slot], row_recv.at[slot, k], row_sem.at[slot], k, proto_peer(k)).wait_recv()

        total = row_send[slot]
        for k in range(1, NP):
            total = total + row_recv[slot, k]
        return 1.0 / total

    def to_lines(src, slot):
        for q in range(8):
            row_send[slot, q : q + 1, :] = jnp.sum(src[q * 128 : q * 128 + 128, :].T, axis=0, keepdims=True)

    def spread(lines, dst):
        for q in range(8):
            dst[q * 128 : q * 128 + 128, :] = jnp.broadcast_to(lines[q : q + 1, :], (128, 128)).T

    def column_sweep(it):
        def some_rows(i, acc):
            rows = aligned(i, 8)
            r = row_b[rows, :]
            out = []
            for j in range(WV):
                e = eh[rows, j * 128 : j * 128 + 128]
                out.append(acc[j] + (e * e) * r)
            return tuple(out)

        acc = lax.fori_loop(0, R // 8, some_rows, tuple(jnp.zeros((8, 128), F32) for _ in range(WV)))
        for j in range(WV):
            col_send[it, j : j + 1, :] = jnp.sum(acc[j], axis=0, keepdims=True)

    def row_sweep():
        c = [jnp.broadcast_to(c_ref[j : j + 1, :], (8, 128)) for j in range(WV)]

        @pl.loop(0, R // 8)
        def _(i):
            rows = aligned(i, 8)
            part = [jnp.zeros((8, 128), F32) for _ in range(4)]
            for j in range(WV):
                e = eh[rows, j * 128 : j * 128 + 128]
                part[j % 4] = part[j % 4] + (e * e) * c[j]
            row_b[rows, :] = (part[0] + part[1]) + (part[2] + part[3])

    start_columns(0)

    to_lines(tot_acc, ITERS)
    start_rows(ITERS)
    views_t[...] = views[...].astype(F32).T.astype(BF16)

    @pl.loop(0, R // 256)
    def _(i):
        rows = aligned(i, 256)
        v = pre[rows, :]
        t = jnp.tanh(gelu_a * (v + gelu_b * (v * v * v)))
        pre[rows, :] = 0.5 * (1.0 + t) + 0.5 * v * (1.0 - t * t) * (gelu_a * (1.0 + 3.0 * gelu_b * (v * v)))

    finish_columns(0)
    row_sweep()
    to_lines(row_b, 0)
    start_rows(0)

    for q in range(8):
        at = jnp.broadcast_to(pos[:, q * 128 : q * 128 + 128], (128, 128)).astype(F32).T
        for k in range(8):
            here = (iota((128, 128), 1) + k * 128).astype(F32)
            perm_t[q * 128 : q * 128 + 128, k * 128 : k * 128 + 128] = onehot(at == here)

    spread(finish_rows(0), row_b)
    column_sweep(1)
    start_columns(1)

    own = perm[aligned(p, RC), :]
    r0 = raw[...]
    r1 = r0.astype(BF16)
    r0 = r0 - r1.astype(F32)
    r2 = r0.astype(BF16)
    r3 = (r0 - r2.astype(F32)).astype(BF16)
    raw_own[...] = dot(own, r1) + dot(own, r2) + dot(own, r3)
    spread(finish_rows(ITERS) * loss_gain, tot_b)

    finish_columns(1)
    row_sweep()
    to_lines(row_b, 1)
    start_rows(1)
    spread(finish_rows(1), row_b)
    column_sweep(2)
    start_columns(2)
    finish_columns(2)
    row_sweep()
    to_lines(row_b, 2)
    start_rows(2)
    spread(finish_rows(2) * loss_gain, row_b)

    def view_copy(k):
        return copy(vg_send.at[k], vg_recv.at[k], vg_sem, k, proto_peer(k))

    @pl.loop(1, NP + 1)
    def _(k):
        q = lax.rem(p + k, NP)
        top, low_half = aligned(2 * q, 64), aligned(2 * q + 1, 64)
        t_top, t_low = tot_b[top, :], tot_b[low_half, :]
        r_top, r_low = row_b[top, :], row_b[low_half, :]

        @pl.loop(0, WV)
        def _(j):
            cols = aligned(j, 128)
            c = c_ref[pl.ds(j, 1), :]
            e_top, e_low = eh[top, cols], eh[low_half, cols]
            dsc[top, cols] = (e_top * t_top - (e_low * e_low) * c * r_low).astype(BF16)
            dsc[low_half, cols] = (e_low * t_low - (e_top * e_top) * c * r_top).astype(BF16)

        part = dot(dsc[aligned(q, RC), :], unit[...])
        vg_send[lax.rem(k, NP)] = part.astype(BF16)

        @pl.when(k < NP)
        def _():
            view_copy(k).start()

        @pl.when(k == NP)
        def _():
            vg_own[...] = part

    def unit_copy(k):
        return copy(ug_send.at[k], ug_recv.at[k], ug_sem, k, batch_peer(k))

    @pl.loop(1, NB + 1)
    def _(k):
        q = lax.rem(b + k, NB)
        part = dot(views_t[...], dsc[:, aligned(q, CC)])

        @pl.when(k < NB)
        def _():
            ug_send[k] = part.astype(BF16)
            unit_copy(k).start()

        @pl.when(k == NB)
        def _():
            ug_own[...] = part

    view_grad = vg_own[...]
    for k in range(1, NP):
        view_copy(k).wait_recv()
        view_grad = view_grad + vg_recv[k].astype(F32)
    out = raw_own[...]
    inv = lax.rsqrt(jnp.sum(out * out, axis=1, keepdims=True) + norm_eps)
    along = jnp.sum(out * view_grad, axis=1, keepdims=True)
    mine = (inv * view_grad - out * (inv * inv * inv) * along).astype(BF16)
    dr_send[...] = mine
    dr_all[aligned(p, RC), :] = mine

    def raw_copy(k, owner):
        return copy(dr_send, dr_all.at[aligned(owner, RC), :], dr_sem, k, proto_peer(k))

    @pl.loop(1, NP)
    def _(k):
        raw_copy(k, p).start()

    @pl.loop(1, NP)
    def _(k):
        raw_copy(k, proto_source(k)).wait_recv()

    d_raw[...] = dot(perm_t[...], dr_all[...]).astype(BF16)

    go = dot_tl(hidden[...], d_raw[...]).reshape(NB, H // NB, Z)
    go_f[...] = go
    go_send[...] = go.astype(BF16)

    def out_copy(k):
        return copy(go_send.at[lax.rem(b + k, NB)], go_recv.at[k], go_sem, k, batch_peer(k))

    @pl.loop(1, NB)
    def _(k):
        out_copy(k).start()

    @pl.loop(0, R // 256)
    def _(i):
        rows = aligned(i, 256)
        d_pre[rows, :] = (pre[rows, :] * dot_t(d_raw[rows, :], w_out[...])).astype(BF16)

    part_of = core * 4 + x
    gi = dot_tl(emb[:, aligned(part_of, 128)], d_pre[...]).reshape(8, 16, H)
    gi_f[...] = gi
    gi_send[...] = gi.astype(BF16)

    def half(q):
        return aligned(q % 2, 256)

    def in_copy(k):
        q = lax.rem(b + k, NB)
        return copy(gi_send.at[q // 2, :, half(q)], gi_recv.at[k], gi_sem, k, batch_peer(k))

    @pl.loop(1, NB)
    def _(k):
        in_copy(k).start()

    @pl.loop(1, NB)
    def _(k):
        in_copy(k).wait_recv()

    total = gi_f[b // 2, :, half(b)]
    for k in range(1, NB):
        total = total + gi_recv[k].astype(F32)
    total = total.astype(BF16)
    gx_send[...] = total
    gin[part_of, b // 2, :, half(b)] = total

    def along_x(k, owner):
        peer = (b, lax.rem(x + k, 4) * 2 + core)
        return copy(gx_send, gin.at[core * 4 + owner, b // 2, :, half(b)], gx_sem, k, peer)

    @pl.loop(1, 4)
    def _(k):
        along_x(k, x).start()

    grad = ug_own[...]
    for k in range(1, NB):
        unit_copy(k).wait_recv()
        grad = grad + ug_recv[k].astype(F32)
    grad = grad.T
    f = proto[aligned(b, CC), :].astype(F32)
    inv = lax.rsqrt(jnp.sum(f * f, axis=1, keepdims=True) + norm_eps)
    along = jnp.sum(f * grad, axis=1, keepdims=True)
    grad = (inv * grad - f * (inv * inv * inv) * along).astype(BF16)
    gp_send[...] = grad
    gproto[aligned(b, CC), :] = grad

    def proto_copy(k, owner):
        return copy(gp_send, gproto.at[aligned(owner, CC), :], gp_sem, k, batch_peer(k))

    @pl.loop(1, NB)
    def _(k):
        proto_copy(k, b).start()

    total = go_f[b]
    for k in range(1, NB):
        out_copy(k).wait_recv()
        total = total + go_recv[k].astype(F32)
    total = total.astype(BF16)
    goa_send[...] = total
    gout[b] = total

    def out_all(k, owner):
        return copy(goa_send, gout.at[owner], goa_sem, k, batch_peer(k))

    @pl.loop(1, NB)
    def _(k):
        out_all(k, b).start()

    @pl.loop(1, 4)
    def _(k):
        along_x(k, lax.rem(x + 4 - k, 4)).wait_recv()

    def plane(q, c):
        return gin.at[pl.ds(c * 4, 4), q // 2, :, half(q)]

    def along_batch(k, owner):
        return copy(plane(owner, core), plane(owner, core), gb_sem, k, batch_peer(k))

    @pl.loop(1, NB)
    def _(k):
        along_batch(k, b).start()

    def to_core(k, c):
        q = batch_source(k)
        return copy(plane(q, c), plane(q, c), gc_sem, k, (b, x * 2 + 1 - core))

    to_core(0, core).start()

    @pl.loop(1, NB)
    def _(k):
        along_batch(k, batch_source(k)).wait_recv()
        to_core(k, core).start()

    @pl.loop(0, NB)
    def _(k):
        to_core(k, 1 - core).wait_recv()
        to_core(k, core).wait_send()

    @pl.loop(1, NB)
    def _(k):
        proto_copy(k, batch_source(k)).wait_recv()
        out_all(k, batch_source(k)).wait_recv()
        for it in range(ITERS):
            copy(col_send.at[it], col_recv.at[it, k], col_sem.at[it], k, batch_peer(k)).wait_send()
        unit_copy(k).wait_send()
        proto_copy(k, b).wait_send()
        out_copy(k).wait_send()
        out_all(k, b).wait_send()
        in_copy(k).wait_send()
        along_batch(k, b).wait_send()

    @pl.loop(1, NP)
    def _(k):
        for slot in range(ITERS + 1):
            copy(row_send.at[slot], row_recv.at[slot, k], row_sem.at[slot], k, proto_peer(k)).wait_send()
        view_copy(k).wait_send()
        raw_copy(k, p).wait_send()

    @pl.loop(1, 4)
    def _(k):
        along_x(k, x).wait_send()


def body(embeddings, pairing, w_in, w_out, prototypes):
    vmem = pl.BlockSpec(memory_space=pltpu.VMEM)
    out = lambda *shape: jax.ShapeDtypeStruct(shape, BF16)
    dma = lambda *shape: pltpu.SemaphoreType.DMA(shape)
    v = pltpu.VMEM
    grad_in, grad_out, grad_proto = pl.pallas_call(
        kernel,
        name="swav_step",
        out_shape=(out(NP, 8, 16, H), out(NB, H // NB, Z), out(W, Z)),
        in_specs=[vmem] * 5,
        out_specs=(vmem,) * 3,
        scratch_shapes=[
            v((R, H), F32), v((R, H), BF16), v((R, Z), F32), v((R, R), BF16), v((R, R), BF16),
            v((R, Z), BF16), v((Z, R), BF16), v((W, Z), BF16), v((R, W), F32), v((R, W), BF16),
            v((R, 128), F32), v((R, 128), F32), v((R, 128), F32), v((RC, Z), F32), v((WV, 128), F32),
            v((ITERS, WV, 128), F32), v((ITERS, NB, WV, 128), F32),
            v((ITERS + 1, 8, 128), F32), v((ITERS + 1, NP, 8, 128), F32),
            v((R, Z), BF16), v((NP, RC, Z), BF16), v((NP, RC, Z), BF16), v((RC, Z), F32),
            v((RC, Z), BF16), v((R, Z), BF16), v((R, Z), BF16), v((R, H), BF16),
            v((NB, Z, CC), BF16), v((NB, Z, CC), BF16), v((Z, CC), F32), v((CC, Z), BF16),
            v((NB, H // NB, Z), F32), v((NB, H // NB, Z), BF16), v((NB, H // NB, Z), BF16), v((H // NB, Z), BF16),
            v((8, 16, H), F32), v((8, 16, H), BF16), v((NB, 16, 256), BF16), v((16, 256), BF16),
            dma(ITERS, 2, NB), dma(ITERS + 1, 2, NP), dma(2, NP), dma(2, NP), dma(2, NB), dma(2, NB),
            dma(2, NB), dma(2, NB), dma(2, NB), dma(2, 4), dma(2, NB), dma(2, NB),
        ],
        compiler_params=pltpu.CompilerParams(
            collective_id=0, has_side_effects=True, vmem_limit_bytes=60 << 20
        ),
    )(embeddings, pairing.reshape(8, 128), w_in, w_out, prototypes)
    return (
        grad_in.reshape(E, H).astype(F32),
        grad_out.reshape(H, Z).astype(F32),
        grad_proto.astype(F32),
    )


def solution(mesh):
    return jax.shard_map(
        body,
        mesh=mesh,
        in_specs=(P("batch", None), P("batch"), P(), P(), P("proto", None)),
        out_specs=(P(), P(), P("proto", None)),
        check_vma=False,
    )
```

```python
import math

import jax
import jax.numpy as jnp
from jax import lax
from jax.experimental import pallas as pl
from jax.experimental.pallas import tpu as pltpu
from jax.sharding import PartitionSpec as P

ITERS = 3
norm_eps = 1e-06
loss_gain = 64.0 / 0.1
half_log2 = 10.0 * math.log2(math.e)
gelu_a = math.sqrt(2.0 / math.pi)
gelu_b = 0.044715

F32, BF16 = jnp.float32, jnp.bfloat16
MESH = pl.DeviceIdType.MESH
NB, NP = 16, 8
R, E, H, Z, W = 1024, 1024, 512, 128, 4096
RC = R // NP
CC = W // NB
WV = W // 128


def dot(a, b):
    return jnp.dot(a, b, preferred_element_type=F32)


def dot_t(a, b):
    return lax.dot_general(a, b, (((1,), (1,)), ((), ())), preferred_element_type=F32)


def dot_tl(a, b):
    return lax.dot_general(a, b, (((0,), (0,)), ((), ())), preferred_element_type=F32)


def iota(shape, dim):
    return lax.broadcasted_iota(jnp.int32, shape, dim)


def onehot(mask):
    return jnp.where(mask, 1.0, 0.0).astype(BF16)


def aligned(i, n):
    return pl.ds(pl.multiple_of(i * n, n), n)


def as_row(x):
    return jnp.concatenate([x[k : k + 1, :] for k in range(x.shape[0])], axis=1)


def kernel(
    emb, pairing, w_in, w_out, proto,
    gin, gout, gproto,
    pre, hidden, raw, perm, perm_t, views, views_t, unit, eh, dsc,
    tot_acc, row_b, tot_b, raw_own, c_ref,
    col_line, col_send, col_recv, row_send, row_recv,
    vun, vg_send, vg_recv, vg_own, dr_send, dr_all, d_raw, d_pre,
    ug_send, ug_recv, ug_own, gp_send,
    go_f, go_send, go_recv, goa_send, gi_f, gi_send, gi_recv, gx_send,
    col_sem, row_sem, vg_sem, dr_sem, ug_sem, gp_sem, go_sem, goa_sem, gi_sem, gx_sem, gb_sem, gc_sem,
):
    b = lax.axis_index("batch")
    p = lax.axis_index("proto")
    x, core = p // 2, p % 2

    def batch_peer(k):
        return (lax.rem(b + k, NB), p)

    def batch_source(k):
        return lax.rem(b + NB - k, NB)

    def proto_peer(k):
        return (b, lax.rem(p + k, NP))

    def proto_source(k):
        return lax.rem(p + NP - k, NP)

    def copy(src, dst, sem, k, device):
        return pltpu.make_async_remote_copy(
            src_ref=src, dst_ref=dst, send_sem=sem.at[0, k], recv_sem=sem.at[1, k],
            device_id=device, device_id_type=MESH,
        )

    barrier = pltpu.get_barrier_semaphore()

    @pl.loop(1, NB)
    def _(k):
        pl.semaphore_signal(barrier, inc=1, device_id=batch_peer(k), device_id_type=MESH)

    @pl.loop(1, NP)
    def _(k):
        pl.semaphore_signal(barrier, inc=1, device_id=proto_peer(k), device_id_type=MESH)

    @pl.loop(0, R // 256)
    def _(i):
        rows = aligned(i, 256)
        v = dot(emb[rows, :], w_in[...])
        pre[rows, :] = v
        hid = (0.5 * v * (1.0 + jnp.tanh(gelu_a * (v + gelu_b * (v * v * v))))).astype(BF16)
        hidden[rows, :] = hid
        out = dot(hid, w_out[...])
        raw[rows, :] = out
        inv = lax.rsqrt(jnp.sum(out * out, axis=1, keepdims=True) + norm_eps)
        vun[rows, :] = (out * inv).astype(BF16)

    mate = pairing[...]
    lead = mate > iota((8, 128), 0) * 128 + iota((8, 128), 1)
    lead_f = jnp.where(lead, 1.0, 0.0)
    within = dot(lead_f, jnp.where(iota((128, 128), 0) < iota((128, 128), 1), 1.0, 0.0))
    chunk = dot(lead_f, jnp.ones((128, 128), F32))
    before = [jnp.zeros((1, 128), F32)]
    for k in range(7):
        before.append(before[-1] + chunk[k : k + 1, :])
    rank = within + jnp.concatenate(before, axis=0)
    high = jnp.floor(rank * (1.0 / 32.0))
    low = rank - 32.0 * high
    mate_row = as_row(mate)

    @pl.loop(0, 8)
    def _(i):
        perm[aligned(i, 128), :] = onehot(mate_row == iota((128, R), 0) + i * 128)

    halves = jnp.concatenate([as_row(high), as_row(low), jnp.zeros((14, R), F32)], axis=0).astype(BF16)
    of_mate = dot(halves, perm[...])
    lead_row = as_row(lead_f)
    rank_row = jnp.where(lead_row > 0.5, as_row(rank), 32.0 * of_mate[0:1, :] + of_mate[1:2, :])
    pos = rank_row + 64.0 * jnp.floor(rank_row * (1.0 / 64.0)) + jnp.where(lead_row > 0.5, 0.0, 64.0)
    pos = pos.astype(jnp.int32)

    @pl.loop(0, 8)
    def _(i):
        perm[aligned(i, 128), :] = onehot(pos == iota((128, R), 0) + i * 128)

    views[...] = dot(perm[...], vun[...]).astype(BF16)

    @pl.loop(0, W // 256)
    def _(i):
        rows = aligned(i, 256)
        f = proto[rows, :].astype(F32)
        inv = lax.rsqrt(jnp.sum(f * f, axis=1, keepdims=True) + norm_eps)
        unit[rows, :] = (f * inv).astype(BF16)

    tot_acc[...] = jnp.zeros_like(tot_acc)

    @pl.loop(0, W // 512)
    def _(j):
        cols = aligned(j, 512)
        u = unit[cols, :]

        def some_rows(i, acc):
            rows = aligned(i, 128)
            e = jnp.exp2(dot_t(views[rows, :], u) * half_log2)
            eh[rows, cols] = e
            tot_acc[rows, :] += (e[:, 0:128] + e[:, 128:256]) + (e[:, 256:384] + e[:, 384:512])
            return acc + jnp.sum((e * e).reshape(16, 8, 512), axis=0)

        acc = lax.fori_loop(0, R // 128, some_rows, jnp.zeros((8, 512), F32), unroll=8)
        line = jnp.sum(acc, axis=0, keepdims=True)
        for m in range(4):
            col_line[pl.ds(j * 4 + m, 1), :] = line[:, m * 128 : m * 128 + 128]

    pl.semaphore_wait(barrier, NB - 1 + NP - 1)

    def start_columns(it):
        col_send[it] = col_line[...].astype(BF16)

        @pl.loop(1, NB)
        def _(k):
            copy(col_send.at[it], col_recv.at[it, k], col_sem.at[it], k, batch_peer(k)).start()

    def finish_columns(it):
        @pl.loop(1, NB)
        def _(k):
            copy(col_send.at[it], col_recv.at[it, k], col_sem.at[it], k, batch_peer(k)).wait_recv()

        total = col_send[it].astype(F32)
        for k in range(1, NB):
            total = total + col_recv[it, k].astype(F32)
        c_ref[...] = 1.0 / total

    def start_rows(slot):
        @pl.loop(1, NP)
        def _(k):
            copy(row_send.at[slot], row_recv.at[slot, k], row_sem.at[slot], k, proto_peer(k)).start()

    def finish_rows(slot):
        @pl.loop(1, NP)
        def _(k):
            copy(row_send.at[slot], row_recv.at[slot, k], row_sem.at[slot], k, proto_peer(k)).wait_recv()

        total = row_send[slot]
        for k in range(1, NP):
            total = total + row_recv[slot, k]
        return 1.0 / total

    def to_lines(src, slot):
        for q in range(8):
            row_send[slot, q : q + 1, :] = jnp.sum(src[q * 128 : q * 128 + 128, :].T, axis=0, keepdims=True)

    def spread(lines, dst):
        for q in range(8):
            dst[q * 128 : q * 128 + 128, :] = jnp.broadcast_to(lines[q : q + 1, :], (128, 128)).T

    def column_sweep():
        def some_rows(i, acc):
            rows = aligned(i, 8)
            r = row_b[rows, :]
            out = []
            for j in range(WV):
                e = eh[rows, j * 128 : j * 128 + 128]
                out.append(acc[j] + (e * e) * r)
            return tuple(out)

        acc = lax.fori_loop(0, R // 8, some_rows, tuple(jnp.zeros((8, 128), F32) for _ in range(WV)))
        for j in range(WV):
            col_line[j : j + 1, :] = jnp.sum(acc[j], axis=0, keepdims=True)

    def row_sweep():
        c = [jnp.broadcast_to(c_ref[j : j + 1, :], (8, 128)) for j in range(WV)]

        @pl.loop(0, R // 8)
        def _(i):
            rows = aligned(i, 8)
            part = [jnp.zeros((8, 128), F32) for _ in range(4)]
            for j in range(WV):
                e = eh[rows, j * 128 : j * 128 + 128]
                part[j % 4] = part[j % 4] + (e * e) * c[j]
            row_b[rows, :] = (part[0] + part[1]) + (part[2] + part[3])

    start_columns(0)

    to_lines(tot_acc, ITERS)
    start_rows(ITERS)
    views_t[...] = views[...].astype(F32).T.astype(BF16)

    @pl.loop(0, R // 256)
    def _(i):
        rows = aligned(i, 256)
        v = pre[rows, :]
        t = jnp.tanh(gelu_a * (v + gelu_b * (v * v * v)))
        pre[rows, :] = 0.5 * (1.0 + t) + 0.5 * v * (1.0 - t * t) * (gelu_a * (1.0 + 3.0 * gelu_b * (v * v)))

    finish_columns(0)
    row_sweep()
    to_lines(row_b, 0)
    start_rows(0)

    for q in range(8):
        at = jnp.broadcast_to(pos[:, q * 128 : q * 128 + 128], (128, 128)).astype(F32).T
        for k in range(8):
            here = (iota((128, 128), 1) + k * 128).astype(F32)
            perm_t[q * 128 : q * 128 + 128, k * 128 : k * 128 + 128] = onehot(at == here)

    spread(finish_rows(0), row_b)
    column_sweep()
    start_columns(1)

    own = perm[aligned(p, RC), :]
    r0 = raw[...]
    r1 = r0.astype(BF16)
    r0 = r0 - r1.astype(F32)
    r2 = r0.astype(BF16)
    r3 = (r0 - r2.astype(F32)).astype(BF16)
    raw_own[...] = dot(own, r1) + dot(own, r2) + dot(own, r3)
    spread(finish_rows(ITERS) * loss_gain, tot_b)

    finish_columns(1)
    row_sweep()
    to_lines(row_b, 1)
    start_rows(1)
    spread(finish_rows(1), row_b)
    column_sweep()
    start_columns(2)
    finish_columns(2)
    row_sweep()
    to_lines(row_b, 2)
    start_rows(2)
    spread(finish_rows(2) * loss_gain, row_b)

    def view_copy(k):
        return copy(vg_send.at[k], vg_recv.at[k], vg_sem, k, proto_peer(k))

    @pl.loop(1, NP + 1)
    def _(k):
        q = lax.rem(p + k, NP)

        @pl.loop(0, 4)
        def _(h):
            top, low = aligned(q * 8 + h, 16), aligned(q * 8 + h + 4, 16)
            t_top, t_low = tot_b[top, :], tot_b[low, :]
            r_top, r_low = row_b[top, :], row_b[low, :]
            for j in range(WV):
                cols = slice(j * 128, j * 128 + 128)
                c = c_ref[j : j + 1, :]
                e_top, e_low = eh[top, cols], eh[low, cols]
                dsc[top, cols] = (e_top * t_top - (e_low * e_low) * c * r_low).astype(BF16)
                dsc[low, cols] = (e_low * t_low - (e_top * e_top) * c * r_top).astype(BF16)

        part = dot(dsc[aligned(q, RC), :], unit[...])
        vg_send[lax.rem(k, NP)] = part.astype(BF16)

        @pl.when(k < NP)
        def _():
            view_copy(k).start()

        @pl.when(k == NP)
        def _():
            vg_own[...] = part

    def unit_copy(k):
        return copy(ug_send.at[k], ug_recv.at[k], ug_sem, k, batch_peer(k))

    @pl.loop(1, NB + 1)
    def _(k):
        q = lax.rem(b + k, NB)
        part = dot(views_t[...], dsc[:, aligned(q, CC)])

        @pl.when(k < NB)
        def _():
            ug_send[k] = part.astype(BF16)
            unit_copy(k).start()

        @pl.when(k == NB)
        def _():
            ug_own[...] = part

    view_grad = vg_own[...]
    for k in range(1, NP):
        view_copy(k).wait_recv()
        view_grad = view_grad + vg_recv[k].astype(F32)
    out = raw_own[...]
    inv = lax.rsqrt(jnp.sum(out * out, axis=1, keepdims=True) + norm_eps)
    along = jnp.sum(out * view_grad, axis=1, keepdims=True)
    mine = (inv * view_grad - out * (inv * inv * inv) * along).astype(BF16)
    dr_send[...] = mine
    dr_all[aligned(p, RC), :] = mine

    def raw_copy(k, owner):
        return copy(dr_send, dr_all.at[aligned(owner, RC), :], dr_sem, k, proto_peer(k))

    @pl.loop(1, NP)
    def _(k):
        raw_copy(k, p).start()

    @pl.loop(1, NP)
    def _(k):
        raw_copy(k, proto_source(k)).wait_recv()

    d_raw[...] = dot(perm_t[...], dr_all[...]).astype(BF16)

    @pl.loop(0, R // 256)
    def _(i):
        rows = aligned(i, 256)
        d_pre[rows, :] = (pre[rows, :] * dot_t(d_raw[rows, :], w_out[...])).astype(BF16)

    part_of = core * 4 + x
    gi = dot_tl(emb[:, aligned(part_of, 128)], d_pre[...]).reshape(8, 16, H)
    gi_f[...] = gi
    gi_send[...] = gi.astype(BF16)

    def half(q):
        return aligned(q % 2, 256)

    def in_copy(k):
        q = lax.rem(b + k, NB)
        return copy(gi_send.at[q // 2, :, half(q)], gi_recv.at[k], gi_sem, k, batch_peer(k))

    @pl.loop(1, NB)
    def _(k):
        in_copy(k).start()

    grad = ug_own[...]
    for k in range(1, NB):
        unit_copy(k).wait_recv()
        grad = grad + ug_recv[k].astype(F32)
    grad = grad.T
    f = proto[aligned(b, CC), :].astype(F32)
    inv = lax.rsqrt(jnp.sum(f * f, axis=1, keepdims=True) + norm_eps)
    along = jnp.sum(f * grad, axis=1, keepdims=True)
    grad = (inv * grad - f * (inv * inv * inv) * along).astype(BF16)
    gp_send[...] = grad
    gproto[aligned(b, CC), :] = grad

    def proto_copy(k, owner):
        return copy(gp_send, gproto.at[aligned(owner, CC), :], gp_sem, k, batch_peer(k))

    @pl.loop(1, NB // 2)
    def _(k):
        proto_copy(k, b).start()

    go = dot_tl(hidden[...], d_raw[...]).reshape(NB, H // NB, Z)
    go_f[...] = go
    go_send[...] = go.astype(BF16)

    def out_copy(k):
        return copy(go_send.at[lax.rem(b + k, NB)], go_recv.at[k], go_sem, k, batch_peer(k))

    @pl.loop(1, NB)
    def _(k):
        out_copy(k).start()

    @pl.loop(1, NB)
    def _(k):
        in_copy(k).wait_recv()

    total = gi_f[b // 2, :, half(b)]
    for k in range(1, NB):
        total = total + gi_recv[k].astype(F32)
    total = total.astype(BF16)
    gx_send[...] = total
    gin[part_of, b // 2, :, half(b)] = total

    def along_x(k, owner):
        peer = (b, lax.rem(x + k, 4) * 2 + core)
        return copy(gx_send, gin.at[core * 4 + owner, b // 2, :, half(b)], gx_sem, k, peer)

    @pl.loop(1, 4)
    def _(k):
        along_x(k, x).start()

    total = go_f[b]
    for k in range(1, NB):
        out_copy(k).wait_recv()
        total = total + go_recv[k].astype(F32)
    total = total.astype(BF16)
    goa_send[...] = total
    gout[b] = total

    def out_all(k, owner):
        return copy(goa_send, gout.at[owner], goa_sem, k, batch_peer(k))

    @pl.loop(1, NB)
    def _(k):
        out_all(k, b).start()

    @pl.loop(1, 4)
    def _(k):
        along_x(k, lax.rem(x + 4 - k, 4)).wait_recv()

    def plane(q, c):
        return gin.at[pl.ds(c * 4, 4), q // 2, :, half(q)]

    def along_batch(k, owner):
        return copy(plane(owner, core), plane(owner, core), gb_sem, k, batch_peer(k))

    @pl.loop(1, NB)
    def _(k):
        along_batch(k, b).start()

    @pl.loop(NB // 2, NB)
    def _(k):
        proto_copy(k, b).start()

    def to_core(k, c):
        q = batch_source(k)
        return copy(plane(q, c), plane(q, c), gc_sem, k, (b, x * 2 + 1 - core))

    to_core(0, core).start()

    @pl.loop(1, NB)
    def _(k):
        along_batch(k, batch_source(k)).wait_recv()
        to_core(k, core).start()

    @pl.loop(0, NB)
    def _(k):
        to_core(k, 1 - core).wait_recv()
        to_core(k, core).wait_send()

    @pl.loop(1, NB)
    def _(k):
        proto_copy(k, batch_source(k)).wait_recv()
        out_all(k, batch_source(k)).wait_recv()
        for it in range(ITERS):
            copy(col_send.at[it], col_recv.at[it, k], col_sem.at[it], k, batch_peer(k)).wait_send()
        unit_copy(k).wait_send()
        proto_copy(k, b).wait_send()
        out_copy(k).wait_send()
        out_all(k, b).wait_send()
        in_copy(k).wait_send()
        along_batch(k, b).wait_send()

    @pl.loop(1, NP)
    def _(k):
        for slot in range(ITERS + 1):
            copy(row_send.at[slot], row_recv.at[slot, k], row_sem.at[slot], k, proto_peer(k)).wait_send()
        view_copy(k).wait_send()
        raw_copy(k, p).wait_send()

    @pl.loop(1, 4)
    def _(k):
        along_x(k, x).wait_send()


def body(embeddings, pairing, w_in, w_out, prototypes):
    vmem = pl.BlockSpec(memory_space=pltpu.VMEM)
    out = lambda *shape: jax.ShapeDtypeStruct(shape, BF16)
    dma = lambda *shape: pltpu.SemaphoreType.DMA(shape)
    v = pltpu.VMEM
    grad_in, grad_out, grad_proto = pl.pallas_call(
        kernel,
        name="swav_step",
        out_shape=(out(NP, 8, 16, H), out(NB, H // NB, Z), out(W, Z)),
        in_specs=[vmem] * 5,
        out_specs=(vmem,) * 3,
        scratch_shapes=[
            v((R, H), F32), v((R, H), BF16), v((R, Z), F32), v((R, R), BF16), v((R, R), BF16),
            v((R, Z), BF16), v((Z, R), BF16), v((W, Z), BF16), v((R, W), F32), v((R, W), BF16),
            v((R, 128), F32), v((R, 128), F32), v((R, 128), F32), v((RC, Z), F32), v((WV, 128), F32),
            v((WV, 128), F32), v((ITERS, WV, 128), BF16), v((ITERS, NB, WV, 128), BF16),
            v((ITERS + 1, 8, 128), F32), v((ITERS + 1, NP, 8, 128), F32),
            v((R, Z), BF16), v((NP, RC, Z), BF16), v((NP, RC, Z), BF16), v((RC, Z), F32),
            v((RC, Z), BF16), v((R, Z), BF16), v((R, Z), BF16), v((R, H), BF16),
            v((NB, Z, CC), BF16), v((NB, Z, CC), BF16), v((Z, CC), F32), v((CC, Z), BF16),
            v((NB, H // NB, Z), F32), v((NB, H // NB, Z), BF16), v((NB, H // NB, Z), BF16), v((H // NB, Z), BF16),
            v((8, 16, H), F32), v((8, 16, H), BF16), v((NB, 16, 256), BF16), v((16, 256), BF16),
            dma(ITERS, 2, NB), dma(ITERS + 1, 2, NP), dma(2, NP), dma(2, NP), dma(2, NB), dma(2, NB),
            dma(2, NB), dma(2, NB), dma(2, NB), dma(2, 4), dma(2, NB), dma(2, NB),
        ],
        compiler_params=pltpu.CompilerParams(
            collective_id=0, has_side_effects=True, vmem_limit_bytes=60 << 20
        ),
    )(embeddings, pairing.reshape(8, 128), w_in, w_out, prototypes)
    return (
        grad_in.reshape(E, H).astype(F32),
        grad_out.reshape(H, Z).astype(F32),
        grad_proto.astype(F32),
    )


def solution(mesh):
    return jax.shard_map(
        body,
        mesh=mesh,
        in_specs=(P("batch", None), P("batch"), P(), P(), P("proto", None)),
        out_specs=(P(), P(), P("proto", None)),
        check_vma=False,
    )
```

```python
import math

import jax
import jax.numpy as jnp
from jax import lax
from jax.experimental import pallas as pl
from jax.experimental.pallas import tpu as pltpu
from jax.sharding import PartitionSpec as P

ITERS = 3
norm_eps = 1e-06
loss_gain = 64.0 / 0.1
half_log2 = 10.0 * math.log2(math.e)
gelu_a = math.sqrt(2.0 / math.pi)
gelu_b = 0.044715

F32, BF16 = jnp.float32, jnp.bfloat16
MESH = pl.DeviceIdType.MESH
NB, NP = 16, 8
R, E, H, Z, W = 1024, 1024, 512, 128, 4096
RC = R // NP
CC = W // NB
WV = W // 128


def dot(a, b):
    return jnp.dot(a, b, preferred_element_type=F32)


def dot_t(a, b):
    return lax.dot_general(a, b, (((1,), (1,)), ((), ())), preferred_element_type=F32)


def dot_tl(a, b):
    return lax.dot_general(a, b, (((0,), (0,)), ((), ())), preferred_element_type=F32)


def iota(shape, dim):
    return lax.broadcasted_iota(jnp.int32, shape, dim)


def onehot(mask):
    return jnp.where(mask, 1.0, 0.0).astype(BF16)


def aligned(i, n):
    return pl.ds(pl.multiple_of(i * n, n), n)


def as_row(x):
    return jnp.concatenate([x[k : k + 1, :] for k in range(x.shape[0])], axis=1)


def kernel(
    emb, pairing, w_in, w_out, proto,
    gin, gout, gproto,
    pre, hidden, raw, perm, perm_t, views, views_t, unit, eh, dsc,
    tot_acc, row_b, tot_b, raw_own, c_ref,
    col_line, col_send, col_recv, row_send, row_recv,
    vun, vg_send, vg_recv, vg_own, dr_send, dr_all, d_raw, d_pre,
    ua_send, ua_recv, ua_own, ub_send, ub_recv, ub_own, sa_send, sa_recv, sb_send, sb_recv,
    go_f, go_send, go_recv, goa_send, gi_f, gi_send, gi_recv, gx_send,
    col_sem, row_sem, vg_sem, dr_sem, up_sem, go_sem, goa_sem, gi_sem, ax_sem, ab_sem, ac_sem, bb_sem, bx_sem, bc_sem,
):
    b = lax.axis_index("batch")
    p = lax.axis_index("proto")
    x, core = p // 2, p % 2
    y, z = b // 4, b % 4

    def batch_peer(k):
        return (lax.rem(b + k, NB), p)

    def batch_source(k):
        return lax.rem(b + NB - k, NB)

    def proto_peer(k):
        return (b, lax.rem(p + k, NP))

    def proto_source(k):
        return lax.rem(p + NP - k, NP)

    def copy(src, dst, sem, k, device):
        return pltpu.make_async_remote_copy(
            src_ref=src, dst_ref=dst, send_sem=sem.at[0, k], recv_sem=sem.at[1, k],
            device_id=device, device_id_type=MESH,
        )

    barrier = pltpu.get_barrier_semaphore()

    @pl.loop(1, NB)
    def _(k):
        pl.semaphore_signal(barrier, inc=1, device_id=batch_peer(k), device_id_type=MESH)

    @pl.loop(1, NP)
    def _(k):
        pl.semaphore_signal(barrier, inc=1, device_id=proto_peer(k), device_id_type=MESH)

    @pl.loop(0, R // 256)
    def _(i):
        rows = aligned(i, 256)
        v = dot(emb[rows, :], w_in[...])
        pre[rows, :] = v
        hid = (0.5 * v * (1.0 + jnp.tanh(gelu_a * (v + gelu_b * (v * v * v))))).astype(BF16)
        hidden[rows, :] = hid
        out = dot(hid, w_out[...])
        raw[rows, :] = out
        inv = lax.rsqrt(jnp.sum(out * out, axis=1, keepdims=True) + norm_eps)
        vun[rows, :] = (out * inv).astype(BF16)

    mate = pairing[...]
    lead = mate > iota((8, 128), 0) * 128 + iota((8, 128), 1)
    lead_f = jnp.where(lead, 1.0, 0.0)
    within = dot(lead_f, jnp.where(iota((128, 128), 0) < iota((128, 128), 1), 1.0, 0.0))
    chunk = dot(lead_f, jnp.ones((128, 128), F32))
    before = [jnp.zeros((1, 128), F32)]
    for k in range(7):
        before.append(before[-1] + chunk[k : k + 1, :])
    rank = within + jnp.concatenate(before, axis=0)
    high = jnp.floor(rank * (1.0 / 32.0))
    low = rank - 32.0 * high
    mate_row = as_row(mate)

    @pl.loop(0, 8)
    def _(i):
        perm[aligned(i, 128), :] = onehot(mate_row == iota((128, R), 0) + i * 128)

    halves = jnp.concatenate([as_row(high), as_row(low), jnp.zeros((14, R), F32)], axis=0).astype(BF16)
    of_mate = dot(halves, perm[...])
    lead_row = as_row(lead_f)
    rank_row = jnp.where(lead_row > 0.5, as_row(rank), 32.0 * of_mate[0:1, :] + of_mate[1:2, :])
    pos = rank_row + 64.0 * jnp.floor(rank_row * (1.0 / 64.0)) + jnp.where(lead_row > 0.5, 0.0, 64.0)
    pos = pos.astype(jnp.int32)

    @pl.loop(0, 8)
    def _(i):
        perm[aligned(i, 128), :] = onehot(pos == iota((128, R), 0) + i * 128)

    views[...] = dot(perm[...], vun[...]).astype(BF16)

    @pl.loop(0, W // 256)
    def _(i):
        rows = aligned(i, 256)
        f = proto[rows, :].astype(F32)
        inv = lax.rsqrt(jnp.sum(f * f, axis=1, keepdims=True) + norm_eps)
        unit[rows, :] = (f * inv).astype(BF16)

    tot_acc[...] = jnp.zeros_like(tot_acc)

    @pl.loop(0, W // 512)
    def _(j):
        cols = aligned(j, 512)
        u = unit[cols, :]

        def some_rows(i, acc):
            rows = aligned(i, 128)
            e = jnp.exp2(dot_t(views[rows, :], u) * half_log2)
            eh[rows, cols] = e
            tot_acc[rows, :] += (e[:, 0:128] + e[:, 128:256]) + (e[:, 256:384] + e[:, 384:512])
            return acc + jnp.sum((e * e).reshape(16, 8, 512), axis=0)

        acc = lax.fori_loop(0, R // 128, some_rows, jnp.zeros((8, 512), F32), unroll=8)
        line = jnp.sum(acc, axis=0, keepdims=True)
        for m in range(4):
            col_line[pl.ds(j * 4 + m, 1), :] = line[:, m * 128 : m * 128 + 128]

    pl.semaphore_wait(barrier, NB - 1 + NP - 1)

    def start_columns(it):
        col_send[it] = col_line[...].astype(BF16)

        @pl.loop(1, NB)
        def _(k):
            copy(col_send.at[it], col_recv.at[it, k], col_sem.at[it], k, batch_peer(k)).start()

    def finish_columns(it):
        @pl.loop(1, NB)
        def _(k):
            copy(col_send.at[it], col_recv.at[it, k], col_sem.at[it], k, batch_peer(k)).wait_recv()

        total = col_send[it].astype(F32)
        for k in range(1, NB):
            total = total + col_recv[it, k].astype(F32)
        c_ref[...] = 1.0 / total

    def start_rows(slot):
        @pl.loop(1, NP)
        def _(k):
            copy(row_send.at[slot], row_recv.at[slot, k], row_sem.at[slot], k, proto_peer(k)).start()

    def finish_rows(slot):
        @pl.loop(1, NP)
        def _(k):
            copy(row_send.at[slot], row_recv.at[slot, k], row_sem.at[slot], k, proto_peer(k)).wait_recv()

        total = row_send[slot]
        for k in range(1, NP):
            total = total + row_recv[slot, k]
        return 1.0 / total

    def to_lines(src, slot):
        for q in range(8):
            row_send[slot, q : q + 1, :] = jnp.sum(src[q * 128 : q * 128 + 128, :].T, axis=0, keepdims=True)

    def spread(lines, dst):
        for q in range(8):
            dst[q * 128 : q * 128 + 128, :] = jnp.broadcast_to(lines[q : q + 1, :], (128, 128)).T

    def column_sweep():
        def some_rows(i, acc):
            rows = aligned(i, 8)
            r = row_b[rows, :]
            out = []
            for j in range(WV):
                e = eh[rows, j * 128 : j * 128 + 128]
                out.append(acc[j] + (e * e) * r)
            return tuple(out)

        acc = lax.fori_loop(0, R // 8, some_rows, tuple(jnp.zeros((8, 128), F32) for _ in range(WV)))
        for j in range(WV):
            col_line[j : j + 1, :] = jnp.sum(acc[j], axis=0, keepdims=True)

    def row_sweep():
        c = [jnp.broadcast_to(c_ref[j : j + 1, :], (8, 128)) for j in range(WV)]

        @pl.loop(0, R // 8)
        def _(i):
            rows = aligned(i, 8)
            part = [jnp.zeros((8, 128), F32) for _ in range(4)]
            for j in range(WV):
                e = eh[rows, j * 128 : j * 128 + 128]
                part[j % 4] = part[j % 4] + (e * e) * c[j]
            row_b[rows, :] = (part[0] + part[1]) + (part[2] + part[3])

    start_columns(0)

    to_lines(tot_acc, ITERS)
    start_rows(ITERS)
    views_t[...] = views[...].astype(F32).T.astype(BF16)

    @pl.loop(0, R // 256)
    def _(i):
        rows = aligned(i, 256)
        v = pre[rows, :]
        t = jnp.tanh(gelu_a * (v + gelu_b * (v * v * v)))
        pre[rows, :] = 0.5 * (1.0 + t) + 0.5 * v * (1.0 - t * t) * (gelu_a * (1.0 + 3.0 * gelu_b * (v * v)))

    finish_columns(0)
    row_sweep()
    to_lines(row_b, 0)
    start_rows(0)

    for q in range(8):
        at = jnp.broadcast_to(pos[:, q * 128 : q * 128 + 128], (128, 128)).astype(F32).T
        for k in range(8):
            here = (iota((128, 128), 1) + k * 128).astype(F32)
            perm_t[q * 128 : q * 128 + 128, k * 128 : k * 128 + 128] = onehot(at == here)

    spread(finish_rows(0), row_b)
    column_sweep()
    start_columns(1)

    own = perm[aligned(p, RC), :]
    r0 = raw[...]
    r1 = r0.astype(BF16)
    r0 = r0 - r1.astype(F32)
    r2 = r0.astype(BF16)
    r3 = (r0 - r2.astype(F32)).astype(BF16)
    raw_own[...] = dot(own, r1) + dot(own, r2) + dot(own, r3)
    spread(finish_rows(ITERS) * loss_gain, tot_b)

    finish_columns(1)
    row_sweep()
    to_lines(row_b, 1)
    start_rows(1)
    spread(finish_rows(1), row_b)
    column_sweep()
    start_columns(2)
    finish_columns(2)
    row_sweep()
    to_lines(row_b, 2)
    start_rows(2)
    spread(finish_rows(2) * loss_gain, row_b)

    def view_copy(k):
        return copy(vg_send.at[k], vg_recv.at[k], vg_sem, k, proto_peer(k))

    @pl.loop(1, NP + 1)
    def _(k):
        q = lax.rem(p + k, NP)

        @pl.loop(0, 4)
        def _(h):
            top, low = aligned(q * 8 + h, 16), aligned(q * 8 + h + 4, 16)
            t_top, t_low = tot_b[top, :], tot_b[low, :]
            r_top, r_low = row_b[top, :], row_b[low, :]
            for j in range(WV):
                cols = slice(j * 128, j * 128 + 128)
                c = c_ref[j : j + 1, :]
                e_top, e_low = eh[top, cols], eh[low, cols]
                dsc[top, cols] = (e_top * t_top - (e_low * e_low) * c * r_low).astype(BF16)
                dsc[low, cols] = (e_low * t_low - (e_top * e_top) * c * r_top).astype(BF16)

        part = dot(dsc[aligned(q, RC), :], unit[...])
        vg_send[lax.rem(k, NP)] = part.astype(BF16)

        @pl.when(k < NP)
        def _():
            view_copy(k).start()

        @pl.when(k == NP)
        def _():
            vg_own[...] = part

    def y_peer(k):
        return (lax.rem(y + k, 4) * 4 + z, p)

    def z_peer(k):
        return (y * 4 + lax.rem(z + k, 4), p)

    def back(i, k):
        return lax.rem(i + 4 - k, 4)

    def first_a(k):
        return copy(ua_send.at[k], ua_recv.at[k], up_sem.at[0], k, y_peer(k))

    def first_b(k):
        return copy(ub_send.at[k], ub_recv.at[k], up_sem.at[1], k, z_peer(k))

    @pl.loop(1, 5)
    def _(kk):
        k = lax.rem(kk, 4)
        to_y = lax.rem(y + k, 4)

        @pl.loop(0, 4)
        def _(m):
            to_z = lax.rem(z + m, 4)
            part = dot(views_t[...], dsc[:, aligned(to_y * 4 + to_z, CC)])
            ua_send[k, to_z] = part[:, :Z].astype(BF16)
            ub_send[m, to_y] = part[:, Z:].astype(BF16)

            @pl.when(k == 0)
            def _():
                ua_own[to_z] = part[:, :Z]

            @pl.when(m == 0)
            def _():
                ub_own[to_y] = part[:, Z:]

        @pl.when(kk < 4)
        def _():
            first_a(kk).start()

    @pl.loop(1, 4)
    def _(k):
        first_b(k).start()

    view_grad = vg_own[...]
    for k in range(1, NP):
        view_copy(k).wait_recv()
        view_grad = view_grad + vg_recv[k].astype(F32)
    out = raw_own[...]
    inv = lax.rsqrt(jnp.sum(out * out, axis=1, keepdims=True) + norm_eps)
    along = jnp.sum(out * view_grad, axis=1, keepdims=True)
    mine = (inv * view_grad - out * (inv * inv * inv) * along).astype(BF16)
    dr_send[...] = mine
    dr_all[aligned(p, RC), :] = mine

    def raw_copy(k, owner):
        return copy(dr_send, dr_all.at[aligned(owner, RC), :], dr_sem, k, proto_peer(k))

    @pl.loop(1, NP)
    def _(k):
        raw_copy(k, p).start()

    @pl.loop(1, NP)
    def _(k):
        raw_copy(k, proto_source(k)).wait_recv()

    d_raw[...] = dot(perm_t[...], dr_all[...]).astype(BF16)

    @pl.loop(0, R // 256)
    def _(i):
        rows = aligned(i, 256)
        d_pre[rows, :] = (pre[rows, :] * dot_t(d_raw[rows, :], w_out[...])).astype(BF16)

    part_of = core * 4 + x
    gi = dot_tl(emb[:, aligned(part_of, 128)], d_pre[...]).reshape(8, 16, H)
    for m in range(2):
        gi_m = jnp.concatenate([gi[:, :, m * 128 : m * 128 + 128], gi[:, :, m * 128 + 256 : m * 128 + 384]], axis=2)
        gi_f[:, m] = gi_m
        gi_send[:, m] = gi_m.astype(BF16)

    def in_copy(k):
        q = lax.rem(b + k, NB)
        return copy(gi_send.at[q // 2, q % 2], gi_recv.at[k], gi_sem, k, batch_peer(k))

    @pl.loop(1, NB)
    def _(k):
        in_copy(k).start()

    def second_a(k):
        return copy(sa_send.at[k], sa_recv.at[k], up_sem.at[2], k, z_peer(k))

    def second_b(k):
        return copy(sb_send.at[k], sb_recv.at[k], up_sem.at[3], k, y_peer(k))

    @pl.loop(1, 4)
    def _(k):
        first_a(k).wait_recv()
        first_b(k).wait_recv()

    def sum_a(i):
        return (ua_own[i] + ua_recv[1, i].astype(F32)) + (ua_recv[2, i].astype(F32) + ua_recv[3, i].astype(F32))

    def sum_b(i):
        return (ub_own[i] + ub_recv[1, i].astype(F32)) + (ub_recv[2, i].astype(F32) + ub_recv[3, i].astype(F32))

    @pl.loop(1, 4)
    def _(k):
        sa_send[k] = sum_a(lax.rem(z + k, 4)).astype(BF16)
        second_a(k).start()
        sb_send[k] = sum_b(lax.rem(y + k, 4)).astype(BF16)
        second_b(k).start()

    ua_own[z] = sum_a(z)
    ub_own[y] = sum_b(y)

    go = dot_tl(hidden[...], d_raw[...]).reshape(NB, H // NB, Z)
    go_f[...] = go
    go_send[...] = go.astype(BF16)

    def out_copy(k):
        return copy(go_send.at[lax.rem(b + k, NB)], go_recv.at[k], go_sem, k, batch_peer(k))

    @pl.loop(1, NB)
    def _(k):
        out_copy(k).start()

    @pl.loop(1, NB)
    def _(k):
        in_copy(k).wait_recv()

    total = gi_f[b // 2, b % 2]
    for k in range(1, NB):
        total = total + gi_recv[k].astype(F32)
    total = total.astype(BF16)
    gx_send[...] = total

    def tile(q, h):
        return pl.ds(pl.multiple_of((q % 2 + 2 * h) * 128, 128), 128)

    gin[part_of, b // 2, :, tile(b, 0)] = total[:, :128]
    gin[part_of, b // 2, :, tile(b, 1)] = total[:, 128:]

    def x_peer(k):
        return (b, lax.rem(x + k, 4) * 2 + core)

    other_core = (b, x * 2 + 1 - core)

    def a_along_x(k, owner):
        return copy(gx_send.at[:, pl.ds(0, 128)], gin.at[core * 4 + owner, b // 2, :, tile(b, 0)], ax_sem, k, x_peer(k))

    def b_along_batch(k, q):
        return copy(gx_send.at[:, pl.ds(128, 128)], gin.at[part_of, q // 2, :, tile(q, 1)], bb_sem, k, batch_peer(k))

    @pl.loop(1, 4)
    def _(k):
        a_along_x(k, x).start()

    @pl.loop(1, NB)
    def _(k):
        b_along_batch(k, b).start()

    @pl.loop(1, 4)
    def _(k):
        second_a(k).wait_recv()
        second_b(k).wait_recv()

    def finish_proto(own, recv, h):
        grad = own
        for k in range(1, 4):
            grad = grad + recv[k].astype(F32)
        grad = grad.T
        f = proto[aligned(b * 2 + h, Z), :].astype(F32)
        inv = lax.rsqrt(jnp.sum(f * f, axis=1, keepdims=True) + norm_eps)
        along = jnp.sum(f * grad, axis=1, keepdims=True)
        gproto[y, z, h] = (inv * grad - f * (inv * inv * inv) * along).astype(BF16)

    finish_proto(ua_own[z], sa_recv, 0)
    finish_proto(ub_own[y], sb_recv, 1)

    def third_a(k, i):
        return copy(gproto.at[y, i, 0], gproto.at[y, i, 0], up_sem.at[4], k, z_peer(k))

    def third_b(k, i):
        return copy(gproto.at[i, z, 1], gproto.at[i, z, 1], up_sem.at[5], k, y_peer(k))

    @pl.loop(1, 4)
    def _(k):
        third_a(k, z).start()
        third_b(k, y).start()

    @pl.loop(1, 4)
    def _(k):
        a_along_x(k, back(x, k)).wait_recv()

    def a_plane(q, c):
        return gin.at[pl.ds(c * 4, 4), q // 2, :, tile(q, 0)]

    def a_along_batch(k, q):
        return copy(a_plane(q, core), a_plane(q, core), ab_sem, k, batch_peer(k))

    def a_to_core(k, c):
        q = batch_source(k)
        return copy(a_plane(q, c), a_plane(q, c), ac_sem, k, other_core)

    @pl.loop(1, NB)
    def _(k):
        a_along_batch(k, b).start()

    a_to_core(0, core).start()

    def b_slab(i, c):
        return gin.at[c * 4 + i, :, :, pl.ds(256, 256)]

    def b_along_x(k, i):
        return copy(b_slab(i, core), b_slab(i, core), bx_sem, k, x_peer(k))

    def b_to_core(k, c):
        return copy(b_slab(back(x, k), c), b_slab(back(x, k), c), bc_sem, k, other_core)

    @pl.loop(1, NB)
    def _(k):
        b_along_batch(k, batch_source(k)).wait_recv()

    @pl.loop(1, 4)
    def _(k):
        b_along_x(k, x).start()

    b_to_core(0, core).start()

    @pl.loop(1, 4)
    def _(k):
        third_a(k, back(z, k)).wait_recv()
        third_b(k, back(y, k)).wait_recv()

    def fourth_a(k, i):
        return copy(gproto.at[i, :, 0], gproto.at[i, :, 0], up_sem.at[6], k, y_peer(k))

    def fourth_b(k, i):
        return copy(gproto.at[:, i, 1], gproto.at[:, i, 1], up_sem.at[7], k, z_peer(k))

    @pl.loop(1, 4)
    def _(k):
        fourth_a(k, y).start()
        fourth_b(k, z).start()

    total = go_f[b]
    for k in range(1, NB):
        out_copy(k).wait_recv()
        total = total + go_recv[k].astype(F32)
    total = total.astype(BF16)
    goa_send[...] = total
    gout[b] = total

    def out_all(k, owner):
        return copy(goa_send, gout.at[owner], goa_sem, k, batch_peer(k))

    @pl.loop(1, NB)
    def _(k):
        out_all(k, b).start()

    @pl.loop(1, NB)
    def _(k):
        a_along_batch(k, batch_source(k)).wait_recv()
        a_to_core(k, core).start()

    @pl.loop(1, 4)
    def _(k):
        b_along_x(k, back(x, k)).wait_recv()
        b_to_core(k, core).start()

    @pl.loop(0, NB)
    def _(k):
        a_to_core(k, 1 - core).wait_recv()
        a_to_core(k, core).wait_send()

    @pl.loop(0, 4)
    def _(k):
        b_to_core(k, 1 - core).wait_recv()
        b_to_core(k, core).wait_send()

    @pl.loop(1, NB)
    def _(k):
        out_all(k, batch_source(k)).wait_recv()
        for it in range(ITERS):
            copy(col_send.at[it], col_recv.at[it, k], col_sem.at[it], k, batch_peer(k)).wait_send()
        out_copy(k).wait_send()
        out_all(k, b).wait_send()
        in_copy(k).wait_send()
        a_along_batch(k, b).wait_send()
        b_along_batch(k, b).wait_send()

    @pl.loop(1, NP)
    def _(k):
        for slot in range(ITERS + 1):
            copy(row_send.at[slot], row_recv.at[slot, k], row_sem.at[slot], k, proto_peer(k)).wait_send()
        view_copy(k).wait_send()
        raw_copy(k, p).wait_send()

    @pl.loop(1, 4)
    def _(k):
        fourth_a(k, back(y, k)).wait_recv()
        fourth_b(k, back(z, k)).wait_recv()
        first_a(k).wait_send()
        first_b(k).wait_send()
        second_a(k).wait_send()
        second_b(k).wait_send()
        third_a(k, z).wait_send()
        third_b(k, y).wait_send()
        fourth_a(k, y).wait_send()
        fourth_b(k, z).wait_send()
        a_along_x(k, x).wait_send()
        b_along_x(k, x).wait_send()


def body(embeddings, pairing, w_in, w_out, prototypes):
    vmem = pl.BlockSpec(memory_space=pltpu.VMEM)
    out = lambda *shape: jax.ShapeDtypeStruct(shape, BF16)
    dma = lambda *shape: pltpu.SemaphoreType.DMA(shape)
    v = pltpu.VMEM
    grad_in, grad_out, grad_proto = pl.pallas_call(
        kernel,
        name="swav_step",
        out_shape=(out(NP, 8, 16, H), out(NB, H // NB, Z), out(4, 4, 2, Z, Z)),
        in_specs=[vmem] * 5,
        out_specs=(vmem,) * 3,
        scratch_shapes=[
            v((R, H), F32), v((R, H), BF16), v((R, Z), F32), v((R, R), BF16), v((R, R), BF16),
            v((R, Z), BF16), v((Z, R), BF16), v((W, Z), BF16), v((R, W), F32), v((R, W), BF16),
            v((R, 128), F32), v((R, 128), F32), v((R, 128), F32), v((RC, Z), F32), v((WV, 128), F32),
            v((WV, 128), F32), v((ITERS, WV, 128), BF16), v((ITERS, NB, WV, 128), BF16),
            v((ITERS + 1, 8, 128), F32), v((ITERS + 1, NP, 8, 128), F32),
            v((R, Z), BF16), v((NP, RC, Z), BF16), v((NP, RC, Z), BF16), v((RC, Z), F32),
            v((RC, Z), BF16), v((R, Z), BF16), v((R, Z), BF16), v((R, H), BF16),
            v((4, 4, Z, Z), BF16), v((4, 4, Z, Z), BF16), v((4, Z, Z), F32),
            v((4, 4, Z, Z), BF16), v((4, 4, Z, Z), BF16), v((4, Z, Z), F32),
            v((4, Z, Z), BF16), v((4, Z, Z), BF16), v((4, Z, Z), BF16), v((4, Z, Z), BF16),
            v((NB, H // NB, Z), F32), v((NB, H // NB, Z), BF16), v((NB, H // NB, Z), BF16), v((H // NB, Z), BF16),
            v((8, 2, 16, 256), F32), v((8, 2, 16, 256), BF16), v((NB, 16, 256), BF16), v((16, 256), BF16),
            dma(ITERS, 2, NB), dma(ITERS + 1, 2, NP), dma(2, NP), dma(2, NP), dma(8, 2, 4),
            dma(2, NB), dma(2, NB), dma(2, NB), dma(2, 4), dma(2, NB), dma(2, NB), dma(2, NB), dma(2, 4), dma(2, 4),
        ],
        compiler_params=pltpu.CompilerParams(
            collective_id=0, has_side_effects=True, vmem_limit_bytes=60 << 20
        ),
    )(embeddings, pairing.reshape(8, 128), w_in, w_out, prototypes)
    return (
        grad_in.reshape(E, H).astype(F32),
        grad_out.reshape(H, Z).astype(F32),
        grad_proto.reshape(W, Z).astype(F32),
    )


def solution(mesh):
    return jax.shard_map(
        body,
        mesh=mesh,
        in_specs=(P("batch", None), P("batch"), P(), P(), P("proto", None)),
        out_specs=(P(), P(), P("proto", None)),
        check_vma=False,
    )
```

```python
import math

import jax
import jax.numpy as jnp
from jax import lax
from jax.experimental import pallas as pl
from jax.experimental.pallas import tpu as pltpu
from jax.sharding import PartitionSpec as P

ITERS = 3
norm_eps = 1e-06
loss_gain = 64.0 / 0.1
half_log2 = 10.0 * math.log2(math.e)
gelu_a = math.sqrt(2.0 / math.pi)
gelu_b = 0.044715

F32, BF16 = jnp.float32, jnp.bfloat16
MESH = pl.DeviceIdType.MESH
NB, NP = 16, 8
R, E, H, Z, W = 1024, 1024, 512, 128, 4096
RC = R // NP
CC = W // NB
WV = W // 128


def dot(a, b):
    return jnp.dot(a, b, preferred_element_type=F32)


def dot_t(a, b):
    return lax.dot_general(a, b, (((1,), (1,)), ((), ())), preferred_element_type=F32)


def dot_tl(a, b):
    return lax.dot_general(a, b, (((0,), (0,)), ((), ())), preferred_element_type=F32)


def iota(shape, dim):
    return lax.broadcasted_iota(jnp.int32, shape, dim)


def onehot(mask):
    return jnp.where(mask, 1.0, 0.0).astype(BF16)


def aligned(i, n):
    return pl.ds(pl.multiple_of(i * n, n), n)


def as_row(x):
    return jnp.concatenate([x[k : k + 1, :] for k in range(x.shape[0])], axis=1)


def kernel(
    emb_hbm, pairing, w_in_hbm, w_out_hbm, proto,
    gin, gout, gproto,
    emb, w_in, w_out, pre, hidden, raw, perm, perm_t, views, views_t, unit, eh, dsc,
    tot_acc, row_b, row_n, tot_b, raw_own, c_ref,
    col_acc, col_line, col_send, col_recv, row_send, row_recv,
    vun, vg_send, vg_recv, vg_own, dr_send, dr_all, d_raw, d_pre,
    ua_send, ua_recv, ua_own, ub_send, ub_recv, ub_own, sa_send, sa_recv, sb_send, sb_recv,
    go_f, go_send, go_recv, goa_send, gi_f, gi_send, gi_recv, gx_send,
    col_sem, row_sem, vg_sem, dr_sem, up_sem, go_sem, goa_sem, gi_sem, ax_sem, ab_sem, ac_sem, bb_sem, bx_sem, bc_sem, in_sem,
):
    b = lax.axis_index("batch")
    p = lax.axis_index("proto")
    x, core = p // 2, p % 2
    y, z = b // 4, b % 4

    def batch_peer(k):
        return (lax.rem(b + k, NB), p)

    def batch_source(k):
        return lax.rem(b + NB - k, NB)

    def proto_peer(k):
        return (b, lax.rem(p + k, NP))

    def proto_source(k):
        return lax.rem(p + NP - k, NP)

    def copy(src, dst, sem, k, device):
        return pltpu.make_async_remote_copy(
            src_ref=src, dst_ref=dst, send_sem=sem.at[0, k], recv_sem=sem.at[1, k],
            device_id=device, device_id_type=MESH,
        )

    loads = [
        pltpu.make_async_copy(src, dst, in_sem.at[i])
        for i, (src, dst) in enumerate(((emb_hbm, emb), (w_in_hbm, w_in), (w_out_hbm, w_out)))
    ]
    for load in loads:
        load.start()

    barrier = pltpu.get_barrier_semaphore()

    @pl.loop(1, NB)
    def _(k):
        pl.semaphore_signal(barrier, inc=1, device_id=batch_peer(k), device_id_type=MESH)

    @pl.loop(1, NP)
    def _(k):
        pl.semaphore_signal(barrier, inc=1, device_id=proto_peer(k), device_id_type=MESH)

    mate = pairing[...]
    lead = mate > iota((8, 128), 0) * 128 + iota((8, 128), 1)
    lead_f = jnp.where(lead, 1.0, 0.0)
    within = dot(lead_f, jnp.where(iota((128, 128), 0) < iota((128, 128), 1), 1.0, 0.0))
    chunk = dot(lead_f, jnp.ones((128, 128), F32))
    before = [jnp.zeros((1, 128), F32)]
    for k in range(7):
        before.append(before[-1] + chunk[k : k + 1, :])
    rank = within + jnp.concatenate(before, axis=0)
    high = jnp.floor(rank * (1.0 / 32.0))
    low = rank - 32.0 * high
    mate_row = as_row(mate)

    @pl.loop(0, 8)
    def _(i):
        perm[aligned(i, 128), :] = onehot(mate_row == iota((128, R), 0) + i * 128)

    halves = jnp.concatenate([as_row(high), as_row(low), jnp.zeros((14, R), F32)], axis=0).astype(BF16)
    of_mate = dot(halves, perm[...])
    lead_row = as_row(lead_f)
    rank_row = jnp.where(lead_row > 0.5, as_row(rank), 32.0 * of_mate[0:1, :] + of_mate[1:2, :])
    pos = rank_row + 64.0 * jnp.floor(rank_row * (1.0 / 64.0)) + jnp.where(lead_row > 0.5, 0.0, 64.0)
    pos = pos.astype(jnp.int32)

    @pl.loop(0, 8)
    def _(i):
        perm[aligned(i, 128), :] = onehot(pos == iota((128, R), 0) + i * 128)

    @pl.loop(0, W // 256)
    def _(i):
        rows = aligned(i, 256)
        f = proto[rows, :].astype(F32)
        inv = lax.rsqrt(jnp.sum(f * f, axis=1, keepdims=True) + norm_eps)
        unit[rows, :] = (f * inv).astype(BF16)

    for load in loads:
        load.wait()

    @pl.loop(0, R // 256)
    def _(i):
        rows = aligned(i, 256)
        v = dot(emb[rows, :], w_in[...])
        pre[rows, :] = v
        hid = (0.5 * v * (1.0 + jnp.tanh(gelu_a * (v + gelu_b * (v * v * v))))).astype(BF16)
        hidden[rows, :] = hid
        out = dot(hid, w_out[...])
        raw[rows, :] = out
        inv = lax.rsqrt(jnp.sum(out * out, axis=1, keepdims=True) + norm_eps)
        vun[rows, :] = (out * inv).astype(BF16)

    views[...] = dot(perm[...], vun[...]).astype(BF16)

    def column_copy(it, h, k):
        return copy(col_send.at[it, h], col_recv.at[it, h, k], col_sem.at[it, h], k, batch_peer(k))

    def start_columns(it, h):
        col_send[it, h] = col_line[h * 16 : h * 16 + 16, :].astype(BF16)

        @pl.loop(1, NB)
        def _(k):
            column_copy(it, h, k).start()

    def finish_columns(it, h):
        @pl.loop(1, NB)
        def _(k):
            column_copy(it, h, k).wait_recv()

        total = col_send[it, h].astype(F32)
        for k in range(1, NB):
            total = total + col_recv[it, h, k].astype(F32)
        c_ref[h * 16 : h * 16 + 16, :] = 1.0 / total

    def row_copy(slot, k):
        return copy(row_send.at[slot], row_recv.at[slot, k], row_sem.at[slot], k, proto_peer(k))

    def start_rows(slot, src, first, count):
        for q in range(count):
            at = (first + q) * 128
            row_send[slot, q : q + 1, :] = jnp.sum(src[at : at + 128, :].T, axis=0, keepdims=True)

        @pl.loop(1, NP)
        def _(k):
            row_copy(slot, k).start()

    def finish_rows(slot):
        @pl.loop(1, NP)
        def _(k):
            row_copy(slot, k).wait_recv()

        total = row_send[slot]
        for k in range(1, NP):
            total = total + row_recv[slot, k]
        return 1.0 / total

    def spread(lines, dst, first, count):
        for q in range(count):
            at = (first + q) * 128
            dst[at : at + 128, :] = jnp.broadcast_to(lines[q : q + 1, :], (128, 128)).T.astype(dst.dtype)

    def pairwise(terms):
        while len(terms) > 1:
            terms = [terms[m] + terms[m + 1] for m in range(0, len(terms), 2)]
        return terms[0]

    def column_sweep(it, rows_half):
        for h in range(2):
            lines = range(h * 16, h * 16 + 16)

            def some_rows(i, acc):
                rows = [pl.ds(pl.multiple_of(i * 64 + m * 16, 16), 16) for m in range(4)]
                r = [row_n[at, :] for at in rows]
                out = []
                for j, a in zip(lines, acc):
                    part = pairwise([dsc[rows[m], j * 128 : j * 128 + 128] * r[m] for m in range(4)]).astype(F32)
                    out.append(a + (part[0:8] + part[8:16]))
                return tuple(out)

            if rows_half == 0:
                acc = tuple(jnp.zeros((8, 128), F32) for _ in lines)
            else:
                acc = tuple(col_acc[:, j * 128 : j * 128 + 128] for j in lines)
            acc = lax.fori_loop(rows_half * 8, rows_half * 8 + 8, some_rows, acc)
            if rows_half == 0:
                for j, a in zip(lines, acc):
                    col_acc[:, j * 128 : j * 128 + 128] = a
            else:
                for j, a in zip(lines, acc):
                    col_line[j : j + 1, :] = jnp.sum(a, axis=0, keepdims=True)
                start_columns(it, h)

    def row_sweep(h, first, last):
        lines = range(h * 16, h * 16 + 16)
        c = [jnp.broadcast_to(c_ref[j : j + 1, :], (16, 128)).astype(BF16) for j in lines]

        @pl.loop(first // 16, last // 16)
        def _(i):
            rows = aligned(i, 16)
            parts = []
            for g in range(0, 16, 4):
                some = [dsc[rows, (h * 16 + g + m) * 128 : (h * 16 + g + m + 1) * 128] * c[g + m] for m in range(4)]
                parts.append(pairwise(some).astype(F32))
            total = pairwise(parts)
            row_b[rows, :] = total if h == 0 else row_b[rows, :] + total

    def rows_of(it):
        finish_columns(it, 0)
        row_sweep(0, 0, R)
        finish_columns(it, 1)
        for h in range(2):
            row_sweep(1, h * 512, h * 512 + 512)
            start_rows(it * 2 + h, row_b, h * 4, 4)

    def columns_of(it):
        for h in range(2):
            spread(finish_rows(it * 2 - 2 + h), row_n, h * 4, 4)
            column_sweep(it, h)

    tot_acc[...] = jnp.zeros_like(tot_acc)
    row_send[...] = jnp.zeros_like(row_send)

    def some_columns(j):
        cols = aligned(j, 512)
        u = unit[cols, :]

        def some_rows(i, acc):
            rows = aligned(i, 128)
            e = jnp.exp2(dot_t(views[rows, :], u) * half_log2)
            eh[rows, cols] = e
            tot_acc[rows, :] += (e[:, 0:128] + e[:, 128:256]) + (e[:, 256:384] + e[:, 384:512])
            e = e * e
            dsc[rows, cols] = e.astype(BF16)
            return acc + jnp.sum(e.reshape(16, 8, 512), axis=0)

        acc = lax.fori_loop(0, R // 128, some_rows, jnp.zeros((8, 512), F32), unroll=8)
        line = jnp.sum(acc, axis=0, keepdims=True)
        for m in range(4):
            col_line[pl.ds(j * 4 + m, 1), :] = line[:, m * 128 : m * 128 + 128]

    pl.loop(0, 4)(some_columns)
    pl.semaphore_wait(barrier, NB - 1 + NP - 1)
    start_columns(0, 0)
    pl.loop(4, 8)(some_columns)
    start_columns(0, 1)

    start_rows(2 * ITERS, tot_acc, 0, 8)
    views_t[...] = views[...].astype(F32).T.astype(BF16)

    @pl.loop(0, R // 256)
    def _(i):
        rows = aligned(i, 256)
        v = pre[rows, :]
        t = jnp.tanh(gelu_a * (v + gelu_b * (v * v * v)))
        pre[rows, :] = 0.5 * (1.0 + t) + 0.5 * v * (1.0 - t * t) * (gelu_a * (1.0 + 3.0 * gelu_b * (v * v)))

    rows_of(0)
    for q in range(8):
        at = jnp.broadcast_to(pos[:, q * 128 : q * 128 + 128], (128, 128)).astype(F32).T
        for k in range(8):
            here = (iota((128, 128), 1) + k * 128).astype(F32)
            perm_t[q * 128 : q * 128 + 128, k * 128 : k * 128 + 128] = onehot(at == here)

    columns_of(1)
    own = perm[aligned(p, RC), :]
    r0 = raw[...]
    r1 = r0.astype(BF16)
    r0 = r0 - r1.astype(F32)
    r2 = r0.astype(BF16)
    r3 = (r0 - r2.astype(F32)).astype(BF16)
    raw_own[...] = dot(own, r1) + dot(own, r2) + dot(own, r3)
    spread(finish_rows(2 * ITERS) * loss_gain, tot_b, 0, 8)
    rows_of(1)
    columns_of(2)
    rows_of(2)

    def view_copy(k):
        return copy(vg_send.at[k], vg_recv.at[k], vg_sem, k, proto_peer(k))

    def one_chunk(q):
        @pl.loop(0, 4)
        def _(h):
            top, low = aligned(q * 8 + h, 16), aligned(q * 8 + h + 4, 16)
            t_top, t_low = tot_b[top, :], tot_b[low, :]
            r_top, r_low = row_b[top, :], row_b[low, :]
            for j in range(WV):
                cols = slice(j * 128, j * 128 + 128)
                c = c_ref[j : j + 1, :]
                e_top, e_low = eh[top, cols], eh[low, cols]
                dsc[top, cols] = (e_top * t_top - (e_low * e_low) * c * r_low).astype(BF16)
                dsc[low, cols] = (e_low * t_low - (e_top * e_top) * c * r_top).astype(BF16)

        part = dot(dsc[aligned(q, RC), :], unit[...])
        k = lax.rem(q + NP - p, NP)
        vg_send[k] = part.astype(BF16)

        @pl.when(k > 0)
        def _():
            view_copy(k).start()

        @pl.when(k == 0)
        def _():
            vg_own[...] = part

    for h in range(2):
        spread(finish_rows(2 * ITERS - 2 + h) * loss_gain, row_b, h * 4, 4)

        @pl.loop(1, 5)
        def _(m):
            one_chunk(lax.rem(p + m, 4) + h * 4)

    def y_peer(k):
        return (lax.rem(y + k, 4) * 4 + z, p)

    def z_peer(k):
        return (y * 4 + lax.rem(z + k, 4), p)

    def back(i, k):
        return lax.rem(i + 4 - k, 4)

    def first_a(k):
        return copy(ua_send.at[k], ua_recv.at[k], up_sem.at[0], k, y_peer(k))

    def first_b(k):
        return copy(ub_send.at[k], ub_recv.at[k], up_sem.at[1], k, z_peer(k))

    @pl.loop(1, 5)
    def _(kk):
        k = lax.rem(kk, 4)
        to_y = lax.rem(y + k, 4)

        @pl.loop(0, 4)
        def _(m):
            to_z = lax.rem(z + m, 4)
            part = dot(views_t[...], dsc[:, aligned(to_y * 4 + to_z, CC)])
            ua_send[k, to_z] = part[:, :Z].astype(BF16)
            ub_send[m, to_y] = part[:, Z:].astype(BF16)

            @pl.when(k == 0)
            def _():
                ua_own[to_z] = part[:, :Z]

            @pl.when(m == 0)
            def _():
                ub_own[to_y] = part[:, Z:]

        @pl.when(kk < 4)
        def _():
            first_a(kk).start()

    @pl.loop(1, 4)
    def _(k):
        first_b(k).start()

    view_grad = vg_own[...]
    for k in range(1, NP):
        view_copy(k).wait_recv()
        view_grad = view_grad + vg_recv[k].astype(F32)
    out = raw_own[...]
    inv = lax.rsqrt(jnp.sum(out * out, axis=1, keepdims=True) + norm_eps)
    along = jnp.sum(out * view_grad, axis=1, keepdims=True)
    mine = (inv * view_grad - out * (inv * inv * inv) * along).astype(BF16)
    dr_send[...] = mine
    dr_all[aligned(p, RC), :] = mine

    def raw_copy(k, owner):
        return copy(dr_send, dr_all.at[aligned(owner, RC), :], dr_sem, k, proto_peer(k))

    @pl.loop(1, NP)
    def _(k):
        raw_copy(k, p).start()

    @pl.loop(1, NP)
    def _(k):
        raw_copy(k, proto_source(k)).wait_recv()

    d_raw[...] = dot(perm_t[...], dr_all[...]).astype(BF16)

    @pl.loop(0, R // 256)
    def _(i):
        rows = aligned(i, 256)
        d_pre[rows, :] = (pre[rows, :] * dot_t(d_raw[rows, :], w_out[...])).astype(BF16)

    part_of = core * 4 + x
    gi = dot_tl(emb[:, aligned(part_of, 128)], d_pre[...]).reshape(8, 16, H)
    for m in range(2):
        gi_m = jnp.concatenate([gi[:, :, m * 128 : m * 128 + 128], gi[:, :, m * 128 + 256 : m * 128 + 384]], axis=2)
        gi_f[:, m] = gi_m
        gi_send[:, m] = gi_m.astype(BF16)

    def in_copy(k):
        q = lax.rem(b + k, NB)
        return copy(gi_send.at[q // 2, q % 2], gi_recv.at[k], gi_sem, k, batch_peer(k))

    @pl.loop(1, NB)
    def _(k):
        in_copy(k).start()

    def second_a(k):
        return copy(sa_send.at[k], sa_recv.at[k], up_sem.at[2], k, z_peer(k))

    def second_b(k):
        return copy(sb_send.at[k], sb_recv.at[k], up_sem.at[3], k, y_peer(k))

    @pl.loop(1, 4)
    def _(k):
        first_a(k).wait_recv()
        first_b(k).wait_recv()

    def sum_a(i):
        return (ua_own[i] + ua_recv[1, i].astype(F32)) + (ua_recv[2, i].astype(F32) + ua_recv[3, i].astype(F32))

    def sum_b(i):
        return (ub_own[i] + ub_recv[1, i].astype(F32)) + (ub_recv[2, i].astype(F32) + ub_recv[3, i].astype(F32))

    @pl.loop(1, 4)
    def _(k):
        sa_send[k] = sum_a(lax.rem(z + k, 4)).astype(BF16)
        second_a(k).start()
        sb_send[k] = sum_b(lax.rem(y + k, 4)).astype(BF16)
        second_b(k).start()

    ua_own[z] = sum_a(z)
    ub_own[y] = sum_b(y)

    go = dot_tl(hidden[...], d_raw[...]).reshape(NB, H // NB, Z)
    go_f[...] = go
    go_send[...] = go.astype(BF16)

    def out_copy(k):
        return copy(go_send.at[lax.rem(b + k, NB)], go_recv.at[k], go_sem, k, batch_peer(k))

    @pl.loop(1, NB)
    def _(k):
        out_copy(k).start()

    @pl.loop(1, NB)
    def _(k):
        in_copy(k).wait_recv()

    total = gi_f[b // 2, b % 2]
    for k in range(1, NB):
        total = total + gi_recv[k].astype(F32)
    total = total.astype(BF16)
    gx_send[...] = total

    def tile(q, h):
        return pl.ds(pl.multiple_of((q % 2 + 2 * h) * 128, 128), 128)

    gin[part_of, b // 2, :, tile(b, 0)] = total[:, :128]
    gin[part_of, b // 2, :, tile(b, 1)] = total[:, 128:]

    def x_peer(k):
        return (b, lax.rem(x + k, 4) * 2 + core)

    other_core = (b, x * 2 + 1 - core)

    def a_along_x(k, owner):
        return copy(gx_send.at[:, pl.ds(0, 128)], gin.at[core * 4 + owner, b // 2, :, tile(b, 0)], ax_sem, k, x_peer(k))

    def b_along_batch(k, q):
        return copy(gx_send.at[:, pl.ds(128, 128)], gin.at[part_of, q // 2, :, tile(q, 1)], bb_sem, k, batch_peer(k))

    @pl.loop(1, 4)
    def _(k):
        a_along_x(k, x).start()

    @pl.loop(1, NB)
    def _(k):
        b_along_batch(k, b).start()

    @pl.loop(1, 4)
    def _(k):
        second_a(k).wait_recv()
        second_b(k).wait_recv()

    def finish_proto(own, recv, h):
        grad = own
        for k in range(1, 4):
            grad = grad + recv[k].astype(F32)
        grad = grad.T
        f = proto[aligned(b * 2 + h, Z), :].astype(F32)
        inv = lax.rsqrt(jnp.sum(f * f, axis=1, keepdims=True) + norm_eps)
        along = jnp.sum(f * grad, axis=1, keepdims=True)
        gproto[y, z, h] = (inv * grad - f * (inv * inv * inv) * along).astype(BF16)

    finish_proto(ua_own[z], sa_recv, 0)
    finish_proto(ub_own[y], sb_recv, 1)

    def third_a(k, i):
        return copy(gproto.at[y, i, 0], gproto.at[y, i, 0], up_sem.at[4], k, z_peer(k))

    def third_b(k, i):
        return copy(gproto.at[i, z, 1], gproto.at[i, z, 1], up_sem.at[5], k, y_peer(k))

    @pl.loop(1, 4)
    def _(k):
        third_a(k, z).start()
        third_b(k, y).start()

    @pl.loop(1, 4)
    def _(k):
        a_along_x(k, back(x, k)).wait_recv()

    def a_plane(q, c):
        return gin.at[pl.ds(c * 4, 4), q // 2, :, tile(q, 0)]

    def a_along_batch(k, q):
        return copy(a_plane(q, core), a_plane(q, core), ab_sem, k, batch_peer(k))

    def a_to_core(k, c):
        q = batch_source(k)
        return copy(a_plane(q, c), a_plane(q, c), ac_sem, k, other_core)

    @pl.loop(1, NB)
    def _(k):
        a_along_batch(k, b).start()

    a_to_core(0, core).start()

    def b_slab(i, c):
        return gin.at[c * 4 + i, :, :, pl.ds(256, 256)]

    def b_along_x(k, i):
        return copy(b_slab(i, core), b_slab(i, core), bx_sem, k, x_peer(k))

    def b_to_core(k, c):
        return copy(b_slab(back(x, k), c), b_slab(back(x, k), c), bc_sem, k, other_core)

    @pl.loop(1, NB)
    def _(k):
        b_along_batch(k, batch_source(k)).wait_recv()

    @pl.loop(1, 4)
    def _(k):
        b_along_x(k, x).start()

    b_to_core(0, core).start()

    @pl.loop(1, 4)
    def _(k):
        third_a(k, back(z, k)).wait_recv()
        third_b(k, back(y, k)).wait_recv()

    def fourth_a(k, i):
        return copy(gproto.at[i, :, 0], gproto.at[i, :, 0], up_sem.at[6], k, y_peer(k))

    def fourth_b(k, i):
        return copy(gproto.at[:, i, 1], gproto.at[:, i, 1], up_sem.at[7], k, z_peer(k))

    @pl.loop(1, 4)
    def _(k):
        fourth_a(k, y).start()
        fourth_b(k, z).start()

    total = go_f[b]
    for k in range(1, NB):
        out_copy(k).wait_recv()
        total = total + go_recv[k].astype(F32)
    total = total.astype(BF16)
    goa_send[...] = total
    gout[b] = total

    def out_all(k, owner):
        return copy(goa_send, gout.at[owner], goa_sem, k, batch_peer(k))

    @pl.loop(1, NB)
    def _(k):
        out_all(k, b).start()

    @pl.loop(1, NB)
    def _(k):
        a_along_batch(k, batch_source(k)).wait_recv()
        a_to_core(k, core).start()

    @pl.loop(1, 4)
    def _(k):
        b_along_x(k, back(x, k)).wait_recv()
        b_to_core(k, core).start()

    @pl.loop(0, NB)
    def _(k):
        a_to_core(k, 1 - core).wait_recv()
        a_to_core(k, core).wait_send()

    @pl.loop(0, 4)
    def _(k):
        b_to_core(k, 1 - core).wait_recv()
        b_to_core(k, core).wait_send()

    @pl.loop(1, NB)
    def _(k):
        out_all(k, batch_source(k)).wait_recv()
        for it in range(ITERS):
            column_copy(it, 0, k).wait_send()
            column_copy(it, 1, k).wait_send()
        out_copy(k).wait_send()
        out_all(k, b).wait_send()
        in_copy(k).wait_send()
        a_along_batch(k, b).wait_send()
        b_along_batch(k, b).wait_send()

    @pl.loop(1, NP)
    def _(k):
        for slot in range(2 * ITERS + 1):
            row_copy(slot, k).wait_send()
        view_copy(k).wait_send()
        raw_copy(k, p).wait_send()

    @pl.loop(1, 4)
    def _(k):
        fourth_a(k, back(y, k)).wait_recv()
        fourth_b(k, back(z, k)).wait_recv()
        first_a(k).wait_send()
        first_b(k).wait_send()
        second_a(k).wait_send()
        second_b(k).wait_send()
        third_a(k, z).wait_send()
        third_b(k, y).wait_send()
        fourth_a(k, y).wait_send()
        fourth_b(k, z).wait_send()
        a_along_x(k, x).wait_send()
        b_along_x(k, x).wait_send()


def body(embeddings, pairing, w_in, w_out, prototypes):
    vmem = pl.BlockSpec(memory_space=pltpu.VMEM)
    hbm = pl.BlockSpec(memory_space=pl.ANY)
    out = lambda *shape: pltpu.VMEM(shape, BF16)
    dma = lambda *shape: pltpu.SemaphoreType.DMA(shape)
    v = pltpu.VMEM
    grad_in, grad_out, grad_proto = pl.pallas_call(
        kernel,
        name="swav_step",
        out_shape=(out(NP, 8, 16, H), out(NB, H // NB, Z), out(4, 4, 2, Z, Z)),
        in_specs=[hbm, vmem, hbm, hbm, vmem],
        out_specs=(vmem,) * 3,
        scratch_shapes=[
            v((R, E), BF16), v((E, H), BF16), v((H, Z), BF16), v((R, H), F32), v((R, H), BF16), v((R, Z), F32), v((R, R), BF16), v((R, R), BF16),
            v((R, Z), BF16), v((Z, R), BF16), v((W, Z), BF16), v((R, W), F32), v((R, W), BF16),
            v((R, 128), F32), v((R, 128), F32), v((R, 128), BF16), v((R, 128), F32), v((RC, Z), F32), v((WV, 128), F32),
            v((8, W), F32), v((WV, 128), F32), v((ITERS, 2, 16, 128), BF16), v((ITERS, 2, NB, 16, 128), BF16),
            v((2 * ITERS + 1, 8, 128), F32), v((2 * ITERS + 1, NP, 8, 128), F32),
            v((R, Z), BF16), v((NP, RC, Z), BF16), v((NP, RC, Z), BF16), v((RC, Z), F32),
            v((RC, Z), BF16), v((R, Z), BF16), v((R, Z), BF16), v((R, H), BF16),
            v((4, 4, Z, Z), BF16), v((4, 4, Z, Z), BF16), v((4, Z, Z), F32),
            v((4, 4, Z, Z), BF16), v((4, 4, Z, Z), BF16), v((4, Z, Z), F32),
            v((4, Z, Z), BF16), v((4, Z, Z), BF16), v((4, Z, Z), BF16), v((4, Z, Z), BF16),
            v((NB, H // NB, Z), F32), v((NB, H // NB, Z), BF16), v((NB, H // NB, Z), BF16), v((H // NB, Z), BF16),
            v((8, 2, 16, 256), F32), v((8, 2, 16, 256), BF16), v((NB, 16, 256), BF16), v((16, 256), BF16),
            dma(ITERS, 2, 2, NB), dma(2 * ITERS + 1, 2, NP), dma(2, NP), dma(2, NP), dma(8, 2, 4),
            dma(2, NB), dma(2, NB), dma(2, NB), dma(2, 4), dma(2, NB), dma(2, NB), dma(2, NB), dma(2, 4), dma(2, 4), dma(3),
        ],
        compiler_params=pltpu.CompilerParams(
            collective_id=0, has_side_effects=True, vmem_limit_bytes=60 << 20
        ),
    )(embeddings, pairing.reshape(8, 128), w_in, w_out, prototypes)
    return (
        grad_in.reshape(E, H).astype(F32),
        grad_out.reshape(H, Z).astype(F32),
        grad_proto.reshape(W, Z).astype(F32),
    )


def solution(mesh):
    return jax.shard_map(
        body,
        mesh=mesh,
        in_specs=(P("batch", None), P("batch"), P(), P(), P("proto", None)),
        out_specs=(P(), P(), P("proto", None)),
        check_vma=False,
    )
```

```python
import math

import jax
import jax.numpy as jnp
from jax import lax
from jax.experimental import pallas as pl
from jax.experimental.pallas import tpu as pltpu
from jax.sharding import PartitionSpec as P

ITERS = 3
norm_eps = 1e-06
loss_gain = 64.0 / 0.1
half_log2 = 10.0 * math.log2(math.e)
gelu_a = math.sqrt(2.0 / math.pi)
gelu_b = 0.044715

F32, BF16 = jnp.float32, jnp.bfloat16
MESH = pl.DeviceIdType.MESH
NB, NP = 16, 8
R, E, H, Z, W = 1024, 1024, 512, 128, 4096
RC = R // NP
CC = W // NB
WV = W // 128


def dot(a, b):
    return jnp.dot(a, b, preferred_element_type=F32)


def dot_t(a, b):
    return lax.dot_general(a, b, (((1,), (1,)), ((), ())), preferred_element_type=F32)


def dot_tl(a, b):
    return lax.dot_general(a, b, (((0,), (0,)), ((), ())), preferred_element_type=F32)


def iota(shape, dim):
    return lax.broadcasted_iota(jnp.int32, shape, dim)


def onehot(mask):
    return jnp.where(mask, 1.0, 0.0).astype(BF16)


def aligned(i, n):
    return pl.ds(pl.multiple_of(i * n, n), n)


def as_row(x):
    return jnp.concatenate([x[k : k + 1, :] for k in range(x.shape[0])], axis=1)


def kernel(
    emb_hbm, pairing, w_in_hbm, w_out_hbm, proto,
    gin, gout, gproto,
    emb, w_in, w_out, pre, hidden, raw, perm, perm_t, views, views_t, unit, eh, dsc,
    tot_acc, row_b, row_n, tot_b, raw_own, c_ref,
    col_acc, col_line, col_send, col_recv, row_send, row_recv,
    vun, vg_send, vg_recv, vg_own, dr_send, dr_all, d_raw, d_pre,
    ua_send, ua_recv, ua_own, ub_send, ub_recv, ub_own, sa_send, sa_recv, sb_send, sb_recv,
    go_f, go_send, go_recv, goa_send, gi_f, gi_send, gi_recv, gx_send,
    col_sem, row_sem, vg_sem, dr_sem, up_sem, go_sem, goa_sem, gi_sem, ax_sem, ab_sem, ac_sem, bb_sem, bx_sem, bc_sem, in_sem,
):
    b = lax.axis_index("batch")
    p = lax.axis_index("proto")
    x, core = p // 2, p % 2
    y, z = b // 4, b % 4

    def batch_peer(k):
        return (lax.rem(b + k, NB), p)

    def batch_source(k):
        return lax.rem(b + NB - k, NB)

    def proto_peer(k):
        return (b, lax.rem(p + k, NP))

    def proto_source(k):
        return lax.rem(p + NP - k, NP)

    def copy(src, dst, sem, k, device):
        return pltpu.make_async_remote_copy(
            src_ref=src, dst_ref=dst, send_sem=sem.at[0, k], recv_sem=sem.at[1, k],
            device_id=device, device_id_type=MESH,
        )

    loads = [
        pltpu.make_async_copy(src, dst, in_sem.at[i])
        for i, (src, dst) in enumerate(((emb_hbm, emb), (w_in_hbm, w_in), (w_out_hbm, w_out)))
    ]
    for load in loads:
        load.start()

    barrier = pltpu.get_barrier_semaphore()

    @pl.loop(1, NB)
    def _(k):
        pl.semaphore_signal(barrier, inc=1, device_id=batch_peer(k), device_id_type=MESH)

    @pl.loop(1, NP)
    def _(k):
        pl.semaphore_signal(barrier, inc=1, device_id=proto_peer(k), device_id_type=MESH)

    mate = pairing[...]
    lead = mate > iota((8, 128), 0) * 128 + iota((8, 128), 1)
    lead_f = jnp.where(lead, 1.0, 0.0)
    within = dot(lead_f, jnp.where(iota((128, 128), 0) < iota((128, 128), 1), 1.0, 0.0))
    chunk = dot(lead_f, jnp.ones((128, 128), F32))
    before = [jnp.zeros((1, 128), F32)]
    for k in range(7):
        before.append(before[-1] + chunk[k : k + 1, :])
    rank = within + jnp.concatenate(before, axis=0)
    high = jnp.floor(rank * (1.0 / 32.0))
    low = rank - 32.0 * high
    mate_row = as_row(mate)

    @pl.loop(0, 8)
    def _(i):
        perm[aligned(i, 128), :] = onehot(mate_row == iota((128, R), 0) + i * 128)

    halves = jnp.concatenate([as_row(high), as_row(low), jnp.zeros((14, R), F32)], axis=0).astype(BF16)
    of_mate = dot(halves, perm[...])
    lead_row = as_row(lead_f)
    rank_row = jnp.where(lead_row > 0.5, as_row(rank), 32.0 * of_mate[0:1, :] + of_mate[1:2, :])
    pos = rank_row + 64.0 * jnp.floor(rank_row * (1.0 / 64.0)) + jnp.where(lead_row > 0.5, 0.0, 64.0)
    pos = pos.astype(jnp.int32)

    @pl.loop(0, 8)
    def _(i):
        perm[aligned(i, 128), :] = onehot(pos == iota((128, R), 0) + i * 128)

    for load in loads:
        load.wait()

    @pl.loop(0, R // 256)
    def _(i):
        rows = aligned(i, 256)
        v = dot(emb[rows, :], w_in[...])
        pre[rows, :] = v
        hid = (0.5 * v * (1.0 + jnp.tanh(gelu_a * (v + gelu_b * (v * v * v))))).astype(BF16)
        hidden[rows, :] = hid
        out = dot(hid, w_out[...])
        raw[rows, :] = out
        inv = lax.rsqrt(jnp.sum(out * out, axis=1, keepdims=True) + norm_eps)
        vun[rows, :] = (out * inv).astype(BF16)
        for m in range(8):
            some = aligned(i * 8 + m, 128)
            f = proto[some, :].astype(F32)
            inv = lax.rsqrt(jnp.sum(f * f, axis=1, keepdims=True) + norm_eps)
            unit[some, :] = (f * inv).astype(BF16)

    views[...] = dot(perm[...], vun[...]).astype(BF16)

    def column_copy(it, h, k):
        return copy(col_send.at[it, h], col_recv.at[it, h, k], col_sem.at[it, h], k, batch_peer(k))

    def start_columns(it, h):
        col_send[it, h] = col_line[h * 16 : h * 16 + 16, :].astype(BF16)

        @pl.loop(1, NB)
        def _(k):
            column_copy(it, h, k).start()

    def finish_columns(it, h):
        @pl.loop(1, NB)
        def _(k):
            column_copy(it, h, k).wait_recv()

        total = col_send[it, h].astype(F32)
        for k in range(1, NB):
            total = total + col_recv[it, h, k].astype(F32)
        c_ref[h * 16 : h * 16 + 16, :] = 1.0 / total

    def row_copy(slot, k):
        return copy(row_send.at[slot], row_recv.at[slot, k], row_sem.at[slot], k, proto_peer(k))

    def start_rows(slot, src, first, count):
        for q in range(count):
            at = (first + q) * 128
            row_send[slot, q : q + 1, :] = jnp.sum(src[at : at + 128, :].T, axis=0, keepdims=True)

        @pl.loop(1, NP)
        def _(k):
            row_copy(slot, k).start()

    def finish_rows(slot):
        @pl.loop(1, NP)
        def _(k):
            row_copy(slot, k).wait_recv()

        total = row_send[slot]
        for k in range(1, NP):
            total = total + row_recv[slot, k]
        return 1.0 / total

    def spread(lines, dst, first, count):
        for q in range(count):
            at = (first + q) * 128
            dst[at : at + 128, :] = jnp.broadcast_to(lines[q : q + 1, :], (128, 128)).T.astype(dst.dtype)

    def pairwise(terms):
        while len(terms) > 1:
            terms = [terms[m] + terms[m + 1] for m in range(0, len(terms), 2)]
        return terms[0]

    def column_sweep(it, rows_half):
        for h in range(2):
            lines = range(h * 16, h * 16 + 16)

            def some_rows(i, acc):
                rows = [pl.ds(pl.multiple_of(i * 64 + m * 16, 16), 16) for m in range(4)]
                r = [row_n[at, :] for at in rows]
                out = []
                for j, a in zip(lines, acc):
                    part = pairwise([dsc[rows[m], j * 128 : j * 128 + 128] * r[m] for m in range(4)]).astype(F32)
                    out.append(a + (part[0:8] + part[8:16]))
                return tuple(out)

            if rows_half == 0:
                acc = tuple(jnp.zeros((8, 128), F32) for _ in lines)
            else:
                acc = tuple(col_acc[:, j * 128 : j * 128 + 128] for j in lines)
            acc = lax.fori_loop(rows_half * 8, rows_half * 8 + 8, some_rows, acc)
            if rows_half == 0:
                for j, a in zip(lines, acc):
                    col_acc[:, j * 128 : j * 128 + 128] = a
            else:
                for j, a in zip(lines, acc):
                    col_line[j : j + 1, :] = jnp.sum(a, axis=0, keepdims=True)
                start_columns(it, h)

    def row_sweep(h, first, last):
        lines = range(h * 16, h * 16 + 16)
        c = [jnp.broadcast_to(c_ref[j : j + 1, :], (16, 128)).astype(BF16) for j in lines]

        @pl.loop(first // 16, last // 16)
        def _(i):
            rows = aligned(i, 16)
            parts = []
            for g in range(0, 16, 4):
                some = [dsc[rows, (h * 16 + g + m) * 128 : (h * 16 + g + m + 1) * 128] * c[g + m] for m in range(4)]
                parts.append(pairwise(some).astype(F32))
            total = pairwise(parts)
            row_b[rows, :] = total if h == 0 else row_b[rows, :] + total

    def rows_of(it):
        finish_columns(it, 0)
        row_sweep(0, 0, R)
        finish_columns(it, 1)
        for h in range(2):
            row_sweep(1, h * 512, h * 512 + 512)
            start_rows(it * 2 + h, row_b, h * 4, 4)

    def columns_of(it):
        for h in range(2):
            spread(finish_rows(it * 2 - 2 + h), row_n, h * 4, 4)
            column_sweep(it, h)

    tot_acc[...] = jnp.zeros_like(tot_acc)
    row_send[...] = jnp.zeros_like(row_send)

    def some_columns(j):
        cols = aligned(j, 512)
        u = unit[cols, :]

        def some_rows(i, acc):
            rows = aligned(i, 128)
            e = jnp.exp2(dot_t(views[rows, :], u) * half_log2)
            eh[rows, cols] = e
            tot_acc[rows, :] += (e[:, 0:128] + e[:, 128:256]) + (e[:, 256:384] + e[:, 384:512])
            e = e * e
            dsc[rows, cols] = e.astype(BF16)
            return acc + jnp.sum(e.reshape(16, 8, 512), axis=0)

        acc = lax.fori_loop(0, R // 128, some_rows, jnp.zeros((8, 512), F32), unroll=8)
        line = jnp.sum(acc, axis=0, keepdims=True)
        for m in range(4):
            col_line[pl.ds(j * 4 + m, 1), :] = line[:, m * 128 : m * 128 + 128]

    pl.loop(0, 4)(some_columns)
    pl.semaphore_wait(barrier, NB - 1 + NP - 1)
    start_columns(0, 0)
    pl.loop(4, 8)(some_columns)
    start_columns(0, 1)

    start_rows(2 * ITERS, tot_acc, 0, 8)
    views_t[...] = views[...].astype(F32).T.astype(BF16)

    @pl.loop(0, R // 256)
    def _(i):
        rows = aligned(i, 256)
        v = pre[rows, :]
        t = jnp.tanh(gelu_a * (v + gelu_b * (v * v * v)))
        pre[rows, :] = 0.5 * (1.0 + t) + 0.5 * v * (1.0 - t * t) * (gelu_a * (1.0 + 3.0 * gelu_b * (v * v)))

    rows_of(0)
    for q in range(8):
        at = jnp.broadcast_to(pos[:, q * 128 : q * 128 + 128], (128, 128)).astype(F32).T
        for k in range(8):
            here = (iota((128, 128), 1) + k * 128).astype(F32)
            perm_t[q * 128 : q * 128 + 128, k * 128 : k * 128 + 128] = onehot(at == here)

    columns_of(1)
    own = perm[aligned(p, RC), :]
    r0 = raw[...]
    r1 = r0.astype(BF16)
    r0 = r0 - r1.astype(F32)
    r2 = r0.astype(BF16)
    r3 = (r0 - r2.astype(F32)).astype(BF16)
    raw_own[...] = dot(own, r1) + dot(own, r2) + dot(own, r3)
    spread(finish_rows(2 * ITERS) * loss_gain, tot_b, 0, 8)
    rows_of(1)
    columns_of(2)
    rows_of(2)

    def view_copy(k):
        return copy(vg_send.at[k], vg_recv.at[k], vg_sem, k, proto_peer(k))

    def one_chunk(q):
        @pl.loop(0, 4)
        def _(h):
            top, low = aligned(q * 8 + h, 16), aligned(q * 8 + h + 4, 16)
            t_top, t_low = tot_b[top, :], tot_b[low, :]
            r_top, r_low = row_b[top, :], row_b[low, :]
            for j in range(WV):
                cols = slice(j * 128, j * 128 + 128)
                c = c_ref[j : j + 1, :]
                e_top, e_low = eh[top, cols], eh[low, cols]
                dsc[top, cols] = (e_top * t_top - (e_low * e_low) * c * r_low).astype(BF16)
                dsc[low, cols] = (e_low * t_low - (e_top * e_top) * c * r_top).astype(BF16)

        part = dot(dsc[aligned(q, RC), :], unit[...])
        k = lax.rem(q + NP - p, NP)
        vg_send[k] = part.astype(BF16)

        @pl.when(k > 0)
        def _():
            view_copy(k).start()

        @pl.when(k == 0)
        def _():
            vg_own[...] = part

    for h in range(2):
        spread(finish_rows(2 * ITERS - 2 + h) * loss_gain, row_b, h * 4, 4)

        @pl.loop(1, 5)
        def _(m):
            one_chunk(lax.rem(p + m, 4) + h * 4)

    def y_peer(k):
        return (lax.rem(y + k, 4) * 4 + z, p)

    def z_peer(k):
        return (y * 4 + lax.rem(z + k, 4), p)

    def back(i, k):
        return lax.rem(i + 4 - k, 4)

    def first_a(k):
        return copy(ua_send.at[k], ua_recv.at[k], up_sem.at[0], k, y_peer(k))

    def first_b(k):
        return copy(ub_send.at[k], ub_recv.at[k], up_sem.at[1], k, z_peer(k))

    @pl.loop(1, 5)
    def _(kk):
        k = lax.rem(kk, 4)
        to_y = lax.rem(y + k, 4)

        parts = dot(views_t[...], dsc[:, aligned(to_y, 4 * CC)])
        for i in range(4):
            part = parts[:, i * CC : i * CC + CC]
            m = back(i, z)
            ua_send[k, i] = part[:, :Z].astype(BF16)
            ub_send[m, to_y] = part[:, Z:].astype(BF16)

            @pl.when(k == 0)
            def _():
                ua_own[i] = part[:, :Z]

            @pl.when(m == 0)
            def _():
                ub_own[to_y] = part[:, Z:]

        @pl.when(kk < 4)
        def _():
            first_a(kk).start()

    @pl.loop(1, 4)
    def _(k):
        first_b(k).start()

    view_grad = vg_own[...]
    for k in range(1, NP):
        view_copy(k).wait_recv()
        view_grad = view_grad + vg_recv[k].astype(F32)
    out = raw_own[...]
    inv = lax.rsqrt(jnp.sum(out * out, axis=1, keepdims=True) + norm_eps)
    along = jnp.sum(out * view_grad, axis=1, keepdims=True)
    mine = (inv * view_grad - out * (inv * inv * inv) * along).astype(BF16)
    dr_send[...] = mine
    dr_all[aligned(p, RC), :] = mine

    def raw_copy(k, owner):
        return copy(dr_send, dr_all.at[aligned(owner, RC), :], dr_sem, k, proto_peer(k))

    @pl.loop(1, NP)
    def _(k):
        raw_copy(k, p).start()

    @pl.loop(1, NP)
    def _(k):
        raw_copy(k, proto_source(k)).wait_recv()

    d_raw[...] = dot(perm_t[...], dr_all[...]).astype(BF16)

    @pl.loop(0, R // 256)
    def _(i):
        rows = aligned(i, 256)
        d_pre[rows, :] = (pre[rows, :] * dot_t(d_raw[rows, :], w_out[...])).astype(BF16)

    part_of = core * 4 + x
    gi = dot_tl(emb[:, aligned(part_of, 128)], d_pre[...]).reshape(8, 16, H)
    for m in range(2):
        gi_m = jnp.concatenate([gi[:, :, m * 128 : m * 128 + 128], gi[:, :, m * 128 + 256 : m * 128 + 384]], axis=2)
        gi_f[:, m] = gi_m
        gi_send[:, m] = gi_m.astype(BF16)

    def in_copy(k):
        q = lax.rem(b + k, NB)
        return copy(gi_send.at[q // 2, q % 2], gi_recv.at[k], gi_sem, k, batch_peer(k))

    @pl.loop(1, NB)
    def _(k):
        in_copy(k).start()

    go = dot_tl(hidden[...], d_raw[...]).reshape(NB, H // NB, Z)
    go_f[...] = go
    go_send[...] = go.astype(BF16)

    def out_copy(k):
        return copy(go_send.at[lax.rem(b + k, NB)], go_recv.at[k], go_sem, k, batch_peer(k))

    @pl.loop(1, NB)
    def _(k):
        out_copy(k).start()

    def second_a(k):
        return copy(sa_send.at[k], sa_recv.at[k], up_sem.at[2], k, z_peer(k))

    def second_b(k):
        return copy(sb_send.at[k], sb_recv.at[k], up_sem.at[3], k, y_peer(k))

    @pl.loop(1, 4)
    def _(k):
        first_a(k).wait_recv()
        first_b(k).wait_recv()

    def sum_a(i):
        return (ua_own[i] + ua_recv[1, i].astype(F32)) + (ua_recv[2, i].astype(F32) + ua_recv[3, i].astype(F32))

    def sum_b(i):
        return (ub_own[i] + ub_recv[1, i].astype(F32)) + (ub_recv[2, i].astype(F32) + ub_recv[3, i].astype(F32))

    @pl.loop(1, 4)
    def _(k):
        sa_send[k] = sum_a(lax.rem(z + k, 4)).astype(BF16)
        second_a(k).start()
        sb_send[k] = sum_b(lax.rem(y + k, 4)).astype(BF16)
        second_b(k).start()

    ua_own[z] = sum_a(z)
    ub_own[y] = sum_b(y)

    @pl.loop(1, NB)
    def _(k):
        in_copy(k).wait_recv()

    total = gi_f[b // 2, b % 2]
    for k in range(1, NB):
        total = total + gi_recv[k].astype(F32)
    total = total.astype(BF16)
    gx_send[...] = total

    def tile(q, h):
        return pl.ds(pl.multiple_of((q % 2 + 2 * h) * 128, 128), 128)

    gin[part_of, b // 2, :, tile(b, 0)] = total[:, :128]
    gin[part_of, b // 2, :, tile(b, 1)] = total[:, 128:]

    def x_peer(k):
        return (b, lax.rem(x + k, 4) * 2 + core)

    other_core = (b, x * 2 + 1 - core)

    def a_along_x(k, owner):
        return copy(gx_send.at[:, pl.ds(0, 128)], gin.at[core * 4 + owner, b // 2, :, tile(b, 0)], ax_sem, k, x_peer(k))

    def b_along_batch(k, q):
        return copy(gx_send.at[:, pl.ds(128, 128)], gin.at[part_of, q // 2, :, tile(q, 1)], bb_sem, k, batch_peer(k))

    @pl.loop(1, 4)
    def _(k):
        a_along_x(k, x).start()

    @pl.loop(1, NB)
    def _(k):
        b_along_batch(k, b).start()

    total = go_f[b]
    for k in range(1, NB):
        out_copy(k).wait_recv()
        total = total + go_recv[k].astype(F32)
    total = total.astype(BF16)
    goa_send[...] = total
    gout[b] = total

    def out_all(k, owner):
        return copy(goa_send, gout.at[owner], goa_sem, k, batch_peer(k))

    @pl.loop(1, NB)
    def _(k):
        out_all(k, b).start()

    @pl.loop(1, 4)
    def _(k):
        second_a(k).wait_recv()
        second_b(k).wait_recv()

    def finish_proto(own, recv, h):
        grad = own
        for k in range(1, 4):
            grad = grad + recv[k].astype(F32)
        grad = grad.T
        f = proto[aligned(b * 2 + h, Z), :].astype(F32)
        inv = lax.rsqrt(jnp.sum(f * f, axis=1, keepdims=True) + norm_eps)
        along = jnp.sum(f * grad, axis=1, keepdims=True)
        gproto[y, z, h] = (inv * grad - f * (inv * inv * inv) * along).astype(BF16)

    finish_proto(ua_own[z], sa_recv, 0)
    finish_proto(ub_own[y], sb_recv, 1)

    def third_a(k, i):
        return copy(gproto.at[y, i, 0], gproto.at[y, i, 0], up_sem.at[4], k, z_peer(k))

    def third_b(k, i):
        return copy(gproto.at[i, z, 1], gproto.at[i, z, 1], up_sem.at[5], k, y_peer(k))

    @pl.loop(1, 4)
    def _(k):
        third_a(k, z).start()
        third_b(k, y).start()

    @pl.loop(1, 4)
    def _(k):
        a_along_x(k, back(x, k)).wait_recv()

    def a_plane(q, c):
        return gin.at[pl.ds(c * 4, 4), q // 2, :, tile(q, 0)]

    def a_along_batch(k, q):
        return copy(a_plane(q, core), a_plane(q, core), ab_sem, k, batch_peer(k))

    def a_to_core(k, c):
        q = batch_source(k)
        return copy(a_plane(q, c), a_plane(q, c), ac_sem, k, other_core)

    @pl.loop(1, NB)
    def _(k):
        a_along_batch(k, b).start()

    a_to_core(0, core).start()

    def b_slab(i, c):
        return gin.at[c * 4 + i, :, :, pl.ds(256, 256)]

    def b_along_x(k, i):
        return copy(b_slab(i, core), b_slab(i, core), bx_sem, k, x_peer(k))

    def b_to_core(k, c):
        return copy(b_slab(back(x, k), c), b_slab(back(x, k), c), bc_sem, k, other_core)

    @pl.loop(1, NB)
    def _(k):
        b_along_batch(k, batch_source(k)).wait_recv()

    @pl.loop(1, 4)
    def _(k):
        b_along_x(k, x).start()

    b_to_core(0, core).start()

    @pl.loop(1, 4)
    def _(k):
        third_a(k, back(z, k)).wait_recv()
        third_b(k, back(y, k)).wait_recv()

    def fourth_a(k, i):
        return copy(gproto.at[i, :, 0], gproto.at[i, :, 0], up_sem.at[6], k, y_peer(k))

    def fourth_b(k, i):
        return copy(gproto.at[:, i, 1], gproto.at[:, i, 1], up_sem.at[7], k, z_peer(k))

    @pl.loop(1, 4)
    def _(k):
        fourth_a(k, y).start()
        fourth_b(k, z).start()

    @pl.loop(1, NB)
    def _(k):
        a_along_batch(k, batch_source(k)).wait_recv()
        a_to_core(k, core).start()

    @pl.loop(1, 4)
    def _(k):
        b_along_x(k, back(x, k)).wait_recv()
        b_to_core(k, core).start()

    @pl.loop(0, NB)
    def _(k):
        a_to_core(k, 1 - core).wait_recv()
        a_to_core(k, core).wait_send()

    @pl.loop(0, 4)
    def _(k):
        b_to_core(k, 1 - core).wait_recv()
        b_to_core(k, core).wait_send()

    @pl.loop(1, NB)
    def _(k):
        out_all(k, batch_source(k)).wait_recv()
        for it in range(ITERS):
            column_copy(it, 0, k).wait_send()
            column_copy(it, 1, k).wait_send()
        out_copy(k).wait_send()
        out_all(k, b).wait_send()
        in_copy(k).wait_send()
        a_along_batch(k, b).wait_send()
        b_along_batch(k, b).wait_send()

    @pl.loop(1, NP)
    def _(k):
        for slot in range(2 * ITERS + 1):
            row_copy(slot, k).wait_send()
        view_copy(k).wait_send()
        raw_copy(k, p).wait_send()

    @pl.loop(1, 4)
    def _(k):
        fourth_a(k, back(y, k)).wait_recv()
        fourth_b(k, back(z, k)).wait_recv()
        first_a(k).wait_send()
        first_b(k).wait_send()
        second_a(k).wait_send()
        second_b(k).wait_send()
        third_a(k, z).wait_send()
        third_b(k, y).wait_send()
        fourth_a(k, y).wait_send()
        fourth_b(k, z).wait_send()
        a_along_x(k, x).wait_send()
        b_along_x(k, x).wait_send()


def body(embeddings, pairing, w_in, w_out, prototypes):
    vmem = pl.BlockSpec(memory_space=pltpu.VMEM)
    hbm = pl.BlockSpec(memory_space=pl.ANY)
    out = lambda *shape: pltpu.VMEM(shape, BF16)
    dma = lambda *shape: pltpu.SemaphoreType.DMA(shape)
    v = pltpu.VMEM
    grad_in, grad_out, grad_proto = pl.pallas_call(
        kernel,
        name="swav_step",
        out_shape=(out(NP, 8, 16, H), out(NB, H // NB, Z), out(4, 4, 2, Z, Z)),
        in_specs=[hbm, vmem, hbm, hbm, vmem],
        out_specs=(vmem,) * 3,
        scratch_shapes=[
            v((R, E), BF16), v((E, H), BF16), v((H, Z), BF16), v((R, H), F32), v((R, H), BF16), v((R, Z), F32), v((R, R), BF16), v((R, R), BF16),
            v((R, Z), BF16), v((Z, R), BF16), v((W, Z), BF16), v((R, W), F32), v((R, W), BF16),
            v((R, 128), F32), v((R, 128), F32), v((R, 128), BF16), v((R, 128), F32), v((RC, Z), F32), v((WV, 128), F32),
            v((8, W), F32), v((WV, 128), F32), v((ITERS, 2, 16, 128), BF16), v((ITERS, 2, NB, 16, 128), BF16),
            v((2 * ITERS + 1, 8, 128), F32), v((2 * ITERS + 1, NP, 8, 128), F32),
            v((R, Z), BF16), v((NP, RC, Z), BF16), v((NP, RC, Z), BF16), v((RC, Z), F32),
            v((RC, Z), BF16), v((R, Z), BF16), v((R, Z), BF16), v((R, H), BF16),
            v((4, 4, Z, Z), BF16), v((4, 4, Z, Z), BF16), v((4, Z, Z), F32),
            v((4, 4, Z, Z), BF16), v((4, 4, Z, Z), BF16), v((4, Z, Z), F32),
            v((4, Z, Z), BF16), v((4, Z, Z), BF16), v((4, Z, Z), BF16), v((4, Z, Z), BF16),
            v((NB, H // NB, Z), F32), v((NB, H // NB, Z), BF16), v((NB, H // NB, Z), BF16), v((H // NB, Z), BF16),
            v((8, 2, 16, 256), F32), v((8, 2, 16, 256), BF16), v((NB, 16, 256), BF16), v((16, 256), BF16),
            dma(ITERS, 2, 2, NB), dma(2 * ITERS + 1, 2, NP), dma(2, NP), dma(2, NP), dma(8, 2, 4),
            dma(2, NB), dma(2, NB), dma(2, NB), dma(2, 4), dma(2, NB), dma(2, NB), dma(2, NB), dma(2, 4), dma(2, 4), dma(3),
        ],
        compiler_params=pltpu.CompilerParams(
            collective_id=0, has_side_effects=True, vmem_limit_bytes=60 << 20
        ),
    )(embeddings, pairing.reshape(8, 128), w_in, w_out, prototypes)
    return (
        grad_in.reshape(E, H).astype(F32),
        grad_out.reshape(H, Z).astype(F32),
        grad_proto.reshape(W, Z).astype(F32),
    )


def solution(mesh):
    return jax.shard_map(
        body,
        mesh=mesh,
        in_specs=(P("batch", None), P("batch"), P(), P(), P("proto", None)),
        out_specs=(P(), P(), P("proto", None)),
        check_vma=False,
    )
```

```python
import math

import jax
import jax.numpy as jnp
from jax import lax
from jax.experimental import pallas as pl
from jax.experimental.pallas import tpu as pltpu
from jax.sharding import PartitionSpec as P

ITERS = 3
norm_eps = 1e-06
loss_gain = 64.0 / 0.1
half_log2 = 10.0 * math.log2(math.e)
gelu_a = math.sqrt(2.0 / math.pi)
gelu_b = 0.044715

F32, BF16 = jnp.float32, jnp.bfloat16
MESH = pl.DeviceIdType.MESH
NB, NP = 16, 8
R, E, H, Z, W = 1024, 1024, 512, 128, 4096
RC = R // NP
CC = W // NB
WV = W // 128


def dot(a, b):
    return jnp.dot(a, b, preferred_element_type=F32)


def dot_t(a, b):
    return lax.dot_general(a, b, (((1,), (1,)), ((), ())), preferred_element_type=F32)


def dot_tl(a, b):
    return lax.dot_general(a, b, (((0,), (0,)), ((), ())), preferred_element_type=F32)


def iota(shape, dim):
    return lax.broadcasted_iota(jnp.int32, shape, dim)


def onehot(mask):
    return jnp.where(mask, 1.0, 0.0).astype(BF16)


def aligned(i, n):
    return pl.ds(pl.multiple_of(i * n, n), n)


def as_row(x):
    return jnp.concatenate([x[k : k + 1, :] for k in range(x.shape[0])], axis=1)


def kernel(
    emb_hbm, pairing, w_in_hbm, w_out_hbm, proto,
    gin, gout, gproto,
    emb, w_in, w_out, pre, hidden, raw, perm, perm_t, views, views_t, unit, eh, dsc,
    tot_acc, row_b, row_n, tot_b, raw_own, c_ref,
    col_acc, col_line, col_send, col_recv, row_send, row_recv,
    vun, vg_send, vg_recv, vg_own, dr_send, dr_all, d_raw, d_pre,
    ua_send, ua_recv, ua_own, ub_send, ub_recv, ub_own, sa_send, sa_recv, sb_send, sb_recv,
    go_f, go_send, go_recv, goa_send, gi_f, gi_send, gi_recv, gx_send,
    col_sem, row_sem, vg_sem, dr_sem, up_sem, go_sem, goa_sem, gi_sem, ax_sem, ab_sem, ac_sem, bb_sem, bx_sem, bc_sem, in_sem,
):
    b = lax.axis_index("batch")
    p = lax.axis_index("proto")
    x, core = p // 2, p % 2
    y, z = b // 4, b % 4

    def batch_peer(k):
        return (lax.rem(b + k, NB), p)

    def batch_source(k):
        return lax.rem(b + NB - k, NB)

    def proto_peer(k):
        return (b, lax.rem(p + k, NP))

    def proto_source(k):
        return lax.rem(p + NP - k, NP)

    def copy(src, dst, sem, k, device):
        return pltpu.make_async_remote_copy(
            src_ref=src, dst_ref=dst, send_sem=sem.at[0, k], recv_sem=sem.at[1, k],
            device_id=device, device_id_type=MESH,
        )

    loads = [
        pltpu.make_async_copy(src, dst, in_sem.at[i])
        for i, (src, dst) in enumerate(((emb_hbm, emb), (w_in_hbm, w_in), (w_out_hbm, w_out)))
    ]
    for load in loads:
        load.start()

    barrier = pltpu.get_barrier_semaphore()

    @pl.loop(1, NB)
    def _(k):
        pl.semaphore_signal(barrier, inc=1, device_id=batch_peer(k), device_id_type=MESH)

    @pl.loop(1, NP)
    def _(k):
        pl.semaphore_signal(barrier, inc=1, device_id=proto_peer(k), device_id_type=MESH)

    mate = pairing[...]
    lead = mate > iota((8, 128), 0) * 128 + iota((8, 128), 1)
    lead_f = jnp.where(lead, 1.0, 0.0)
    within = dot(lead_f, jnp.where(iota((128, 128), 0) < iota((128, 128), 1), 1.0, 0.0))
    chunk = dot(lead_f, jnp.ones((128, 128), F32))
    before = [jnp.zeros((1, 128), F32)]
    for k in range(7):
        before.append(before[-1] + chunk[k : k + 1, :])
    rank = within + jnp.concatenate(before, axis=0)
    high = jnp.floor(rank * (1.0 / 32.0))
    low = rank - 32.0 * high
    mate_row = as_row(mate)

    @pl.loop(0, 8)
    def _(i):
        perm[aligned(i, 128), :] = onehot(mate_row == iota((128, R), 0) + i * 128)

    halves = jnp.concatenate([as_row(high), as_row(low), jnp.zeros((14, R), F32)], axis=0).astype(BF16)
    of_mate = dot(halves, perm[...])
    lead_row = as_row(lead_f)
    rank_row = jnp.where(lead_row > 0.5, as_row(rank), 32.0 * of_mate[0:1, :] + of_mate[1:2, :])
    pos = rank_row + 64.0 * jnp.floor(rank_row * (1.0 / 64.0)) + jnp.where(lead_row > 0.5, 0.0, 64.0)
    pos = pos.astype(jnp.int32)

    @pl.loop(0, 8)
    def _(i):
        perm[aligned(i, 128), :] = onehot(pos == iota((128, R), 0) + i * 128)

    for load in loads:
        load.wait()

    @pl.loop(0, R // 256)
    def _(i):
        rows = aligned(i, 256)
        v = dot(emb[rows, :], w_in[...])
        pre[rows, :] = v
        hid = (0.5 * v * (1.0 + jnp.tanh(gelu_a * (v + gelu_b * (v * v * v))))).astype(BF16)
        hidden[rows, :] = hid
        out = dot(hid, w_out[...])
        raw[rows, :] = out
        inv = lax.rsqrt(jnp.sum(out * out, axis=1, keepdims=True) + norm_eps)
        vun[rows, :] = (out * inv).astype(BF16)
        for m in range(8):
            some = aligned(i * 8 + m, 128)
            f = proto[some, :].astype(F32)
            inv = lax.rsqrt(jnp.sum(f * f, axis=1, keepdims=True) + norm_eps)
            unit[some, :] = (f * inv).astype(BF16)

    views[...] = dot(perm[...], vun[...]).astype(BF16)

    def column_copy(it, h, k):
        return copy(col_send.at[it, h], col_recv.at[it, h, k], col_sem.at[it, h], k, batch_peer(k))

    def start_columns(it, h):
        col_send[it, h] = col_line[h * 16 : h * 16 + 16, :].astype(BF16)

        @pl.loop(1, NB)
        def _(k):
            column_copy(it, h, k).start()

    def finish_columns(it, h):
        @pl.loop(1, NB)
        def _(k):
            column_copy(it, h, k).wait_recv()

        total = col_send[it, h].astype(F32)
        for k in range(1, NB):
            total = total + col_recv[it, h, k].astype(F32)
        c_ref[h * 16 : h * 16 + 16, :] = 1.0 / total

    def row_copy(slot, k):
        return copy(row_send.at[slot], row_recv.at[slot, k], row_sem.at[slot], k, proto_peer(k))

    def start_rows(slot, src, first, count):
        for q in range(count):
            at = (first + q) * 128
            row_send[slot, q : q + 1, :] = jnp.sum(src[at : at + 128, :].T, axis=0, keepdims=True)

        @pl.loop(1, NP)
        def _(k):
            row_copy(slot, k).start()

    def finish_rows(slot):
        @pl.loop(1, NP)
        def _(k):
            row_copy(slot, k).wait_recv()

        total = row_send[slot]
        for k in range(1, NP):
            total = total + row_recv[slot, k]
        return 1.0 / total

    def spread(lines, dst, first, count):
        for q in range(count):
            at = (first + q) * 128
            dst[at : at + 128, :] = jnp.broadcast_to(lines[q : q + 1, :], (128, 128)).T.astype(dst.dtype)

    def pairwise(terms):
        while len(terms) > 1:
            terms = [terms[m] + terms[m + 1] for m in range(0, len(terms), 2)]
        return terms[0]

    def column_sweep(it, rows_half):
        for h in range(2):
            lines = range(h * 16, h * 16 + 16)

            def some_rows(i, acc):
                rows = [pl.ds(pl.multiple_of(i * 64 + m * 16, 16), 16) for m in range(4)]
                r = [row_n[at, :] for at in rows]
                out = []
                for j, a in zip(lines, acc):
                    part = pairwise([dsc[rows[m], j * 128 : j * 128 + 128] * r[m] for m in range(4)]).astype(F32)
                    out.append(a + (part[0:8] + part[8:16]))
                return tuple(out)

            if rows_half == 0:
                acc = tuple(jnp.zeros((8, 128), F32) for _ in lines)
            else:
                acc = tuple(col_acc[:, j * 128 : j * 128 + 128] for j in lines)
            acc = lax.fori_loop(rows_half * 8, rows_half * 8 + 8, some_rows, acc)
            if rows_half == 0:
                for j, a in zip(lines, acc):
                    col_acc[:, j * 128 : j * 128 + 128] = a
            else:
                for j, a in zip(lines, acc):
                    col_line[j : j + 1, :] = jnp.sum(a, axis=0, keepdims=True)
                start_columns(it, h)

    def row_sweep(h, first, last):
        lines = range(h * 16, h * 16 + 16)
        c = [jnp.broadcast_to(c_ref[j : j + 1, :], (16, 128)).astype(BF16) for j in lines]

        @pl.loop(first // 16, last // 16)
        def _(i):
            rows = aligned(i, 16)
            parts = []
            for g in range(0, 16, 4):
                some = [dsc[rows, (h * 16 + g + m) * 128 : (h * 16 + g + m + 1) * 128] * c[g + m] for m in range(4)]
                parts.append(pairwise(some).astype(F32))
            total = pairwise(parts)
            row_b[rows, :] = total if h == 0 else row_b[rows, :] + total

    def rows_of(it):
        finish_columns(it, 0)
        row_sweep(0, 0, R)
        finish_columns(it, 1)
        for h in range(2):
            row_sweep(1, h * 512, h * 512 + 512)
            start_rows(it * 2 + h, row_b, h * 4, 4)

    def columns_of(it):
        for h in range(2):
            spread(finish_rows(it * 2 - 2 + h), row_n, h * 4, 4)
            column_sweep(it, h)

    tot_acc[...] = jnp.zeros_like(tot_acc)
    row_send[...] = jnp.zeros_like(row_send)

    def some_columns(j):
        cols = aligned(j, 512)
        u = unit[cols, :]

        def some_rows(i, acc):
            rows = aligned(i, 128)
            e = jnp.exp2(dot_t(views[rows, :], u) * half_log2)
            eh[rows, cols] = e
            tot_acc[rows, :] += (e[:, 0:128] + e[:, 128:256]) + (e[:, 256:384] + e[:, 384:512])
            e = e * e
            dsc[rows, cols] = e.astype(BF16)
            return acc + jnp.sum(e.reshape(16, 8, 512), axis=0)

        acc = lax.fori_loop(0, R // 128, some_rows, jnp.zeros((8, 512), F32), unroll=8)
        line = jnp.sum(acc, axis=0, keepdims=True)
        for m in range(4):
            col_line[pl.ds(j * 4 + m, 1), :] = line[:, m * 128 : m * 128 + 128]

    pl.loop(0, 4)(some_columns)
    pl.semaphore_wait(barrier, NB - 1 + NP - 1)
    start_columns(0, 0)
    pl.loop(4, 8)(some_columns)
    start_columns(0, 1)

    start_rows(2 * ITERS, tot_acc, 0, 8)
    views_t[...] = views[...].astype(F32).T.astype(BF16)

    @pl.loop(0, R // 256)
    def _(i):
        rows = aligned(i, 256)
        v = pre[rows, :]
        t = jnp.tanh(gelu_a * (v + gelu_b * (v * v * v)))
        pre[rows, :] = 0.5 * (1.0 + t) + 0.5 * v * (1.0 - t * t) * (gelu_a * (1.0 + 3.0 * gelu_b * (v * v)))

    rows_of(0)
    for q in range(8):
        at = jnp.broadcast_to(pos[:, q * 128 : q * 128 + 128], (128, 128)).astype(F32).T
        for k in range(8):
            here = (iota((128, 128), 1) + k * 128).astype(F32)
            perm_t[q * 128 : q * 128 + 128, k * 128 : k * 128 + 128] = onehot(at == here)

    columns_of(1)
    own = perm[aligned(p, RC), :]
    r0 = raw[...]
    r1 = r0.astype(BF16)
    r0 = r0 - r1.astype(F32)
    r2 = r0.astype(BF16)
    r3 = (r0 - r2.astype(F32)).astype(BF16)
    raw_own[...] = dot(own, r1) + dot(own, r2) + dot(own, r3)
    spread(finish_rows(2 * ITERS) * loss_gain, tot_b, 0, 8)
    rows_of(1)
    columns_of(2)
    rows_of(2)

    def view_copy(k):
        return copy(vg_send.at[k], vg_recv.at[k], vg_sem, k, proto_peer(k))

    def one_chunk(q):
        @pl.loop(0, 4)
        def _(h):
            top, low = aligned(q * 8 + h, 16), aligned(q * 8 + h + 4, 16)
            t_top, t_low = tot_b[top, :], tot_b[low, :]
            r_top, r_low = row_b[top, :], row_b[low, :]
            for j in range(WV):
                cols = slice(j * 128, j * 128 + 128)
                c = c_ref[j : j + 1, :]
                e_top, e_low = eh[top, cols], eh[low, cols]
                dsc[top, cols] = (e_top * t_top - (e_low * e_low) * c * r_low).astype(BF16)
                dsc[low, cols] = (e_low * t_low - (e_top * e_top) * c * r_top).astype(BF16)

        part = dot(dsc[aligned(q, RC), :], unit[...])
        k = lax.rem(q + NP - p, NP)
        vg_send[k] = part.astype(BF16)

        @pl.when(k > 0)
        def _():
            view_copy(k).start()

        @pl.when(k == 0)
        def _():
            vg_own[...] = part

    for h in range(2):
        spread(finish_rows(2 * ITERS - 2 + h) * loss_gain, row_b, h * 4, 4)

        @pl.loop(1, 5)
        def _(m):
            one_chunk(lax.rem(p + m, 4) + h * 4)

    def y_peer(k):
        return (lax.rem(y + k, 4) * 4 + z, p)

    def z_peer(k):
        return (y * 4 + lax.rem(z + k, 4), p)

    def back(i, k):
        return lax.rem(i + 4 - k, 4)

    def first_a(k):
        return copy(ua_send.at[k], ua_recv.at[k], up_sem.at[0], k, y_peer(k))

    def first_b(k):
        return copy(ub_send.at[k], ub_recv.at[k], up_sem.at[1], k, z_peer(k))

    @pl.loop(1, 5)
    def _(kk):
        k = lax.rem(kk, 4)
        to_y = lax.rem(y + k, 4)

        parts = dot(views_t[...], dsc[:, aligned(to_y, 4 * CC)])
        for i in range(4):
            part = parts[:, i * CC : i * CC + CC]
            m = back(i, z)
            ua_send[k, i] = part[:, :Z].astype(BF16)
            ub_send[m, to_y] = part[:, Z:].astype(BF16)

            @pl.when(k == 0)
            def _():
                ua_own[i] = part[:, :Z]

            @pl.when(m == 0)
            def _():
                ub_own[to_y] = part[:, Z:]

        @pl.when(kk < 4)
        def _():
            first_a(kk).start()

    @pl.loop(1, 4)
    def _(k):
        first_b(k).start()

    view_grad = vg_own[...]
    for k in range(1, NP):
        view_copy(k).wait_recv()
        view_grad = view_grad + vg_recv[k].astype(F32)
    out = raw_own[...]
    inv = lax.rsqrt(jnp.sum(out * out, axis=1, keepdims=True) + norm_eps)
    along = jnp.sum(out * view_grad, axis=1, keepdims=True)
    mine = (inv * view_grad - out * (inv * inv * inv) * along).astype(BF16)
    dr_send[...] = mine
    dr_all[aligned(p, RC), :] = mine

    def raw_copy(k, owner):
        return copy(dr_send, dr_all.at[aligned(owner, RC), :], dr_sem, k, proto_peer(k))

    @pl.loop(1, NP)
    def _(k):
        raw_copy(k, p).start()

    def second_a(k):
        return copy(sa_send.at[k], sa_recv.at[k], up_sem.at[2], k, z_peer(k))

    def second_b(k):
        return copy(sb_send.at[k], sb_recv.at[k], up_sem.at[3], k, y_peer(k))

    @pl.loop(1, 4)
    def _(k):
        first_a(k).wait_recv()
        first_b(k).wait_recv()

    def sum_a(i):
        return (ua_own[i] + ua_recv[1, i].astype(F32)) + (ua_recv[2, i].astype(F32) + ua_recv[3, i].astype(F32))

    def sum_b(i):
        return (ub_own[i] + ub_recv[1, i].astype(F32)) + (ub_recv[2, i].astype(F32) + ub_recv[3, i].astype(F32))

    @pl.loop(1, 4)
    def _(k):
        sa_send[k] = sum_a(lax.rem(z + k, 4)).astype(BF16)
        second_a(k).start()
        sb_send[k] = sum_b(lax.rem(y + k, 4)).astype(BF16)
        second_b(k).start()

    ua_own[z] = sum_a(z)
    ub_own[y] = sum_b(y)

    @pl.loop(1, NP)
    def _(k):
        raw_copy(k, proto_source(k)).wait_recv()

    d_raw[...] = dot(perm_t[...], dr_all[...]).astype(BF16)

    @pl.loop(0, R // 256)
    def _(i):
        rows = aligned(i, 256)
        d_pre[rows, :] = (pre[rows, :] * dot_t(d_raw[rows, :], w_out[...])).astype(BF16)

    part_of = core * 4 + x
    gi = dot_tl(emb[:, aligned(part_of, 128)], d_pre[...]).reshape(8, 16, H)
    for m in range(2):
        gi_m = jnp.concatenate([gi[:, :, m * 128 : m * 128 + 128], gi[:, :, m * 128 + 256 : m * 128 + 384]], axis=2)
        gi_f[:, m] = gi_m
        gi_send[:, m] = gi_m.astype(BF16)

    def in_copy(k):
        q = lax.rem(b + k, NB)
        return copy(gi_send.at[q // 2, q % 2], gi_recv.at[k], gi_sem, k, batch_peer(k))

    @pl.loop(1, NB)
    def _(k):
        in_copy(k).start()

    go = dot_tl(hidden[...], d_raw[...]).reshape(NB, H // NB, Z)
    go_f[...] = go
    go_send[...] = go.astype(BF16)

    def out_copy(k):
        return copy(go_send.at[lax.rem(b + k, NB)], go_recv.at[k], go_sem, k, batch_peer(k))

    @pl.loop(1, NB)
    def _(k):
        out_copy(k).start()

    @pl.loop(1, 4)
    def _(k):
        second_a(k).wait_recv()
        second_b(k).wait_recv()

    def finish_proto(own, recv, h):
        grad = own
        for k in range(1, 4):
            grad = grad + recv[k].astype(F32)
        grad = grad.T
        f = proto[aligned(b * 2 + h, Z), :].astype(F32)
        inv = lax.rsqrt(jnp.sum(f * f, axis=1, keepdims=True) + norm_eps)
        along = jnp.sum(f * grad, axis=1, keepdims=True)
        gproto[y, z, h] = (inv * grad - f * (inv * inv * inv) * along).astype(BF16)

    finish_proto(ua_own[z], sa_recv, 0)
    finish_proto(ub_own[y], sb_recv, 1)

    def third_a(k, i):
        return copy(gproto.at[y, i, 0], gproto.at[y, i, 0], up_sem.at[4], k, z_peer(k))

    def third_b(k, i):
        return copy(gproto.at[i, z, 1], gproto.at[i, z, 1], up_sem.at[5], k, y_peer(k))

    @pl.loop(1, 4)
    def _(k):
        third_a(k, z).start()
        third_b(k, y).start()

    @pl.loop(1, NB)
    def _(k):
        in_copy(k).wait_recv()

    total = gi_f[b // 2, b % 2]
    for k in range(1, NB):
        total = total + gi_recv[k].astype(F32)
    total = total.astype(BF16)
    gx_send[...] = total

    def tile(q, h):
        return pl.ds(pl.multiple_of((q % 2 + 2 * h) * 128, 128), 128)

    gin[part_of, b // 2, :, tile(b, 0)] = total[:, :128]
    gin[part_of, b // 2, :, tile(b, 1)] = total[:, 128:]

    def x_peer(k):
        return (b, lax.rem(x + k, 4) * 2 + core)

    other_core = (b, x * 2 + 1 - core)

    def a_along_x(k, owner):
        return copy(gx_send.at[:, pl.ds(0, 128)], gin.at[core * 4 + owner, b // 2, :, tile(b, 0)], ax_sem, k, x_peer(k))

    def b_along_batch(k, q):
        return copy(gx_send.at[:, pl.ds(128, 128)], gin.at[part_of, q // 2, :, tile(q, 1)], bb_sem, k, batch_peer(k))

    @pl.loop(1, 4)
    def _(k):
        a_along_x(k, x).start()

    @pl.loop(1, NB)
    def _(k):
        b_along_batch(k, b).start()

    total = go_f[b]
    for k in range(1, NB):
        out_copy(k).wait_recv()
        total = total + go_recv[k].astype(F32)
    total = total.astype(BF16)
    goa_send[...] = total
    gout[b] = total

    def out_all(k, owner):
        return copy(goa_send, gout.at[owner], goa_sem, k, batch_peer(k))

    @pl.loop(1, NB)
    def _(k):
        out_all(k, b).start()

    @pl.loop(1, 4)
    def _(k):
        a_along_x(k, back(x, k)).wait_recv()

    def a_plane(q, c):
        return gin.at[pl.ds(c * 4, 4), q // 2, :, tile(q, 0)]

    def a_along_batch(k, q):
        return copy(a_plane(q, core), a_plane(q, core), ab_sem, k, batch_peer(k))

    def a_to_core(k, c):
        q = batch_source(k)
        return copy(a_plane(q, c), a_plane(q, c), ac_sem, k, other_core)

    @pl.loop(1, NB)
    def _(k):
        a_along_batch(k, b).start()

    a_to_core(0, core).start()

    @pl.loop(1, 4)
    def _(k):
        third_a(k, back(z, k)).wait_recv()
        third_b(k, back(y, k)).wait_recv()

    def fourth_a(k, i):
        return copy(gproto.at[i, :, 0], gproto.at[i, :, 0], up_sem.at[6], k, y_peer(k))

    def fourth_b(k, i):
        return copy(gproto.at[:, i, 1], gproto.at[:, i, 1], up_sem.at[7], k, z_peer(k))

    @pl.loop(1, 4)
    def _(k):
        fourth_a(k, y).start()
        fourth_b(k, z).start()

    def b_slab(i, c):
        return gin.at[c * 4 + i, :, :, pl.ds(256, 256)]

    def b_along_x(k, i):
        return copy(b_slab(i, core), b_slab(i, core), bx_sem, k, x_peer(k))

    def b_to_core(k, c):
        return copy(b_slab(back(x, k), c), b_slab(back(x, k), c), bc_sem, k, other_core)

    @pl.loop(1, NB)
    def _(k):
        b_along_batch(k, batch_source(k)).wait_recv()

    @pl.loop(1, 4)
    def _(k):
        b_along_x(k, x).start()

    b_to_core(0, core).start()

    @pl.loop(1, NB)
    def _(k):
        a_along_batch(k, batch_source(k)).wait_recv()
        a_to_core(k, core).start()

    @pl.loop(1, 4)
    def _(k):
        b_along_x(k, back(x, k)).wait_recv()
        b_to_core(k, core).start()

    @pl.loop(0, NB)
    def _(k):
        a_to_core(k, 1 - core).wait_recv()
        a_to_core(k, core).wait_send()

    @pl.loop(0, 4)
    def _(k):
        b_to_core(k, 1 - core).wait_recv()
        b_to_core(k, core).wait_send()

    @pl.loop(1, NB)
    def _(k):
        out_all(k, batch_source(k)).wait_recv()
        for it in range(ITERS):
            column_copy(it, 0, k).wait_send()
            column_copy(it, 1, k).wait_send()
        out_copy(k).wait_send()
        out_all(k, b).wait_send()
        in_copy(k).wait_send()
        a_along_batch(k, b).wait_send()
        b_along_batch(k, b).wait_send()

    @pl.loop(1, NP)
    def _(k):
        for slot in range(2 * ITERS + 1):
            row_copy(slot, k).wait_send()
        view_copy(k).wait_send()
        raw_copy(k, p).wait_send()

    @pl.loop(1, 4)
    def _(k):
        fourth_a(k, back(y, k)).wait_recv()
        fourth_b(k, back(z, k)).wait_recv()
        first_a(k).wait_send()
        first_b(k).wait_send()
        second_a(k).wait_send()
        second_b(k).wait_send()
        third_a(k, z).wait_send()
        third_b(k, y).wait_send()
        fourth_a(k, y).wait_send()
        fourth_b(k, z).wait_send()
        a_along_x(k, x).wait_send()
        b_along_x(k, x).wait_send()


def body(embeddings, pairing, w_in, w_out, prototypes):
    vmem = pl.BlockSpec(memory_space=pltpu.VMEM)
    hbm = pl.BlockSpec(memory_space=pl.ANY)
    out = lambda *shape: pltpu.VMEM(shape, BF16)
    dma = lambda *shape: pltpu.SemaphoreType.DMA(shape)
    v = pltpu.VMEM
    grad_in, grad_out, grad_proto = pl.pallas_call(
        kernel,
        name="swav_step",
        out_shape=(out(NP, 8, 16, H), out(NB, H // NB, Z), out(4, 4, 2, Z, Z)),
        in_specs=[hbm, vmem, hbm, hbm, vmem],
        out_specs=(vmem,) * 3,
        scratch_shapes=[
            v((R, E), BF16), v((E, H), BF16), v((H, Z), BF16), v((R, H), F32), v((R, H), BF16), v((R, Z), F32), v((R, R), BF16), v((R, R), BF16),
            v((R, Z), BF16), v((Z, R), BF16), v((W, Z), BF16), v((R, W), F32), v((R, W), BF16),
            v((R, 128), F32), v((R, 128), F32), v((R, 128), BF16), v((R, 128), F32), v((RC, Z), F32), v((WV, 128), F32),
            v((8, W), F32), v((WV, 128), F32), v((ITERS, 2, 16, 128), BF16), v((ITERS, 2, NB, 16, 128), BF16),
            v((2 * ITERS + 1, 8, 128), F32), v((2 * ITERS + 1, NP, 8, 128), F32),
            v((R, Z), BF16), v((NP, RC, Z), BF16), v((NP, RC, Z), BF16), v((RC, Z), F32),
            v((RC, Z), BF16), v((R, Z), BF16), v((R, Z), BF16), v((R, H), BF16),
            v((4, 4, Z, Z), BF16), v((4, 4, Z, Z), BF16), v((4, Z, Z), F32),
            v((4, 4, Z, Z), BF16), v((4, 4, Z, Z), BF16), v((4, Z, Z), F32),
            v((4, Z, Z), BF16), v((4, Z, Z), BF16), v((4, Z, Z), BF16), v((4, Z, Z), BF16),
            v((NB, H // NB, Z), F32), v((NB, H // NB, Z), BF16), v((NB, H // NB, Z), BF16), v((H // NB, Z), BF16),
            v((8, 2, 16, 256), F32), v((8, 2, 16, 256), BF16), v((NB, 16, 256), BF16), v((16, 256), BF16),
            dma(ITERS, 2, 2, NB), dma(2 * ITERS + 1, 2, NP), dma(2, NP), dma(2, NP), dma(8, 2, 4),
            dma(2, NB), dma(2, NB), dma(2, NB), dma(2, 4), dma(2, NB), dma(2, NB), dma(2, NB), dma(2, 4), dma(2, 4), dma(3),
        ],
        compiler_params=pltpu.CompilerParams(
            collective_id=0, has_side_effects=True, vmem_limit_bytes=60 << 20
        ),
    )(embeddings, pairing.reshape(8, 128), w_in, w_out, prototypes)
    return (
        grad_in.reshape(E, H).astype(F32),
        grad_out.reshape(H, Z).astype(F32),
        grad_proto.reshape(W, Z).astype(F32),
    )


def solution(mesh):
    return jax.shard_map(
        body,
        mesh=mesh,
        in_specs=(P("batch", None), P("batch"), P(), P(), P("proto", None)),
        out_specs=(P(), P(), P("proto", None)),
        check_vma=False,
    )
```

```python
import math

import jax
import jax.numpy as jnp
from jax import lax
from jax.experimental import pallas as pl
from jax.experimental.pallas import tpu as pltpu
from jax.sharding import PartitionSpec as P

ITERS = 3
norm_eps = 1e-06
loss_gain = 64.0 / 0.1
half_log2 = 10.0 * math.log2(math.e)
gelu_a = math.sqrt(2.0 / math.pi)
gelu_b = 0.044715

F32, BF16 = jnp.float32, jnp.bfloat16
MESH = pl.DeviceIdType.MESH
NB, NP = 16, 8
R, E, H, Z, W = 1024, 1024, 512, 128, 4096
RC = R // NP
CC = W // NB
WV = W // 128


def dot(a, b):
    return jnp.dot(a, b, preferred_element_type=F32)


def dot_t(a, b):
    return lax.dot_general(a, b, (((1,), (1,)), ((), ())), preferred_element_type=F32)


def dot_tl(a, b):
    return lax.dot_general(a, b, (((0,), (0,)), ((), ())), preferred_element_type=F32)


def iota(shape, dim):
    return lax.broadcasted_iota(jnp.int32, shape, dim)


def onehot(mask):
    return jnp.where(mask, 1.0, 0.0).astype(BF16)


def aligned(i, n):
    return pl.ds(pl.multiple_of(i * n, n), n)


def as_row(x):
    return jnp.concatenate([x[k : k + 1, :] for k in range(x.shape[0])], axis=1)


def kernel(
    emb_hbm, pairing, w_in_hbm, w_out_hbm, proto,
    gin, gout, gproto,
    emb, w_in, w_out, pre, hidden, raw, perm, perm_t, views, views_t, emb_t, unit, eh, low_d, high_d,
    tot_acc, row_b, row_n, tot_b, raw_own, c_ref,
    col_acc, col_line, col_send, col_recv, row_send, row_recv,
    vun, vg_send, vg_recv, vg_own, dr_send, dr_all, d_raw, d_pre,
    ua_send, ua_recv, ua_own, ub_send, ub_recv, ub_own, sa_send, sa_recv, sb_send, sb_recv,
    go_f, go_send, go_recv, goa_send, gi_f, gi_send, gi_recv, gx_send,
    col_sem, row_sem, vg_sem, dr_sem, up_sem, go_sem, goa_sem, gi_sem, ax_sem, ab_sem, ac_sem, bb_sem, bx_sem, bc_sem, in_sem,
):
    dsc = (low_d, high_d)
    b = lax.axis_index("batch")
    p = lax.axis_index("proto")
    x, core = p // 2, p % 2
    part_of = core * 4 + x
    y, z = b // 4, b % 4

    def batch_peer(k):
        return (lax.rem(b + k, NB), p)

    def batch_source(k):
        return lax.rem(b + NB - k, NB)

    def proto_peer(k):
        return (b, lax.rem(p + k, NP))

    def proto_source(k):
        return lax.rem(p + NP - k, NP)

    def copy(src, dst, sem, k, device):
        return pltpu.make_async_remote_copy(
            src_ref=src, dst_ref=dst, send_sem=sem.at[0, k], recv_sem=sem.at[1, k],
            device_id=device, device_id_type=MESH,
        )

    loads = [
        pltpu.make_async_copy(src, dst, in_sem.at[i])
        for i, (src, dst) in enumerate(((emb_hbm, emb), (w_in_hbm, w_in), (w_out_hbm, w_out)))
    ]
    for load in loads:
        load.start()

    barrier = pltpu.get_barrier_semaphore()

    @pl.loop(1, NB)
    def _(k):
        pl.semaphore_signal(barrier, inc=1, device_id=batch_peer(k), device_id_type=MESH)

    @pl.loop(1, NP)
    def _(k):
        pl.semaphore_signal(barrier, inc=1, device_id=proto_peer(k), device_id_type=MESH)

    mate = pairing[...]
    lead = mate > iota((8, 128), 0) * 128 + iota((8, 128), 1)
    lead_f = jnp.where(lead, 1.0, 0.0)
    within = dot(lead_f, jnp.where(iota((128, 128), 0) < iota((128, 128), 1), 1.0, 0.0))
    chunk = dot(lead_f, jnp.ones((128, 128), F32))
    before = [jnp.zeros((1, 128), F32)]
    for k in range(7):
        before.append(before[-1] + chunk[k : k + 1, :])
    rank = within + jnp.concatenate(before, axis=0)
    high = jnp.floor(rank * (1.0 / 32.0))
    low = rank - 32.0 * high
    mate_row = as_row(mate)

    @pl.loop(0, 8)
    def _(i):
        perm[aligned(i, 128), :] = onehot(mate_row == iota((128, R), 0) + i * 128)

    halves = jnp.concatenate([as_row(high), as_row(low), jnp.zeros((14, R), F32)], axis=0).astype(BF16)
    of_mate = dot(halves, perm[...])
    lead_row = as_row(lead_f)
    rank_row = jnp.where(lead_row > 0.5, as_row(rank), 32.0 * of_mate[0:1, :] + of_mate[1:2, :])
    pos = rank_row + 64.0 * jnp.floor(rank_row * (1.0 / 64.0)) + jnp.where(lead_row > 0.5, 0.0, 64.0)
    pos = pos.astype(jnp.int32)

    @pl.loop(0, 8)
    def _(i):
        perm[aligned(i, 128), :] = onehot(pos == iota((128, R), 0) + i * 128)

    for load in loads:
        load.wait()

    @pl.loop(0, R // 256)
    def _(i):
        rows = aligned(i, 256)
        v = dot(emb[rows, :], w_in[...])
        pre[rows, :] = v
        hid = (0.5 * v * (1.0 + jnp.tanh(gelu_a * (v + gelu_b * (v * v * v))))).astype(BF16)
        hidden[rows, :] = hid
        out = dot(hid, w_out[...])
        raw[rows, :] = out
        inv = lax.rsqrt(jnp.sum(out * out, axis=1, keepdims=True) + norm_eps)
        vun[rows, :] = (out * inv).astype(BF16)
        for m in range(8):
            some = aligned(i * 8 + m, 128)
            f = proto[some, :].astype(F32)
            inv = lax.rsqrt(jnp.sum(f * f, axis=1, keepdims=True) + norm_eps)
            unit[some, :] = (f * inv).astype(BF16)

    views[...] = dot(perm[...], vun[...]).astype(BF16)

    def column_copy(it, h, k):
        return copy(col_send.at[it, h], col_recv.at[it, h, k], col_sem.at[it, h], k, batch_peer(k))

    def start_columns(it, h):
        col_send[it, h] = col_line[h * 16 : h * 16 + 16, :].astype(BF16)

        @pl.loop(1, NB)
        def _(k):
            column_copy(it, h, k).start()

    def finish_columns(it, h):
        @pl.loop(1, NB)
        def _(k):
            column_copy(it, h, k).wait_recv()

        total = col_send[it, h].astype(F32)
        for k in range(1, NB):
            total = total + col_recv[it, h, k].astype(F32)
        c_ref[h * 16 : h * 16 + 16, :] = 1.0 / total

    def row_copy(slot, k):
        return copy(row_send.at[slot], row_recv.at[slot, k], row_sem.at[slot], k, proto_peer(k))

    def start_rows(slot, src, first, count):
        for q in range(count):
            at = (first + q) * 128
            row_send[slot, q : q + 1, :] = jnp.sum(src[at : at + 128, :].T, axis=0, keepdims=True)

        @pl.loop(1, NP)
        def _(k):
            row_copy(slot, k).start()

    def finish_rows(slot):
        @pl.loop(1, NP)
        def _(k):
            row_copy(slot, k).wait_recv()

        total = row_send[slot]
        for k in range(1, NP):
            total = total + row_recv[slot, k]
        return 1.0 / total

    def spread(lines, dst, first, count):
        for q in range(count):
            at = (first + q) * 128
            dst[at : at + 128, :] = jnp.broadcast_to(lines[q : q + 1, :], (128, 128)).T.astype(dst.dtype)

    def pairwise(terms):
        while len(terms) > 1:
            terms = [terms[m] + terms[m + 1] for m in range(0, len(terms), 2)]
        return terms[0]

    def column_sweep(it, rows_half):
        for h in range(2):
            lines = range(h * 16, h * 16 + 16)

            def some_rows(i, acc):
                rows = [pl.ds(pl.multiple_of(i * 64 + m * 16, 16), 16) for m in range(4)]
                r = [row_n[pl.ds(pl.multiple_of(rows_half * 512 + i * 64 + m * 16, 16), 16), :] for m in range(4)]
                out = []
                for j, a in zip(lines, acc):
                    part = pairwise([dsc[rows_half][rows[m], j * 128 : j * 128 + 128] * r[m] for m in range(4)]).astype(F32)
                    out.append(a + (part[0:8] + part[8:16]))
                return tuple(out)

            if rows_half == 0:
                acc = tuple(jnp.zeros((8, 128), F32) for _ in lines)
            else:
                acc = tuple(col_acc[:, j * 128 : j * 128 + 128] for j in lines)
            acc = lax.fori_loop(0, 8, some_rows, acc)
            if rows_half == 0:
                for j, a in zip(lines, acc):
                    col_acc[:, j * 128 : j * 128 + 128] = a
            else:
                for j, a in zip(lines, acc):
                    col_line[j : j + 1, :] = jnp.sum(a, axis=0, keepdims=True)
                start_columns(it, h)

    def row_sweep(h, rows_half):
        lines = range(h * 16, h * 16 + 16)
        c = [jnp.broadcast_to(c_ref[j : j + 1, :], (16, 128)).astype(BF16) for j in lines]

        @pl.loop(0, 32)
        def _(i):
            near, rows = aligned(i, 16), aligned(i + rows_half * 32, 16)
            parts = []
            for g in range(0, 16, 4):
                some = [dsc[rows_half][near, (h * 16 + g + m) * 128 : (h * 16 + g + m + 1) * 128] * c[g + m] for m in range(4)]
                parts.append(pairwise(some).astype(F32))
            total = pairwise(parts)
            row_b[rows, :] = total if h == 0 else row_b[rows, :] + total

    def rows_of(it):
        finish_columns(it, 0)
        row_sweep(0, 0)
        row_sweep(0, 1)
        finish_columns(it, 1)
        for h in range(2):
            row_sweep(1, h)
            start_rows(it * 2 + h, row_b, h * 4, 4)

    def columns_of(it):
        for h in range(2):
            spread(finish_rows(it * 2 - 2 + h), row_n, h * 4, 4)
            column_sweep(it, h)

    tot_acc[...] = jnp.zeros_like(tot_acc)
    row_send[...] = jnp.zeros_like(row_send)

    def some_columns(j):
        cols = aligned(j, 512)
        u = unit[cols, :]

        acc = jnp.zeros((8, 512), F32)
        for i in range(8):
            rows = slice(i * 128, i * 128 + 128)
            e = jnp.exp2(dot_t(views[rows, :], u) * half_log2)
            eh[rows, cols] = e
            tot_acc[rows, :] += (e[:, 0:128] + e[:, 128:256]) + (e[:, 256:384] + e[:, 384:512])
            e = e * e
            dsc[i // 4][i % 4 * 128 : i % 4 * 128 + 128, cols] = e.astype(BF16)
            acc = acc + jnp.sum(e.reshape(16, 8, 512), axis=0)
        line = jnp.sum(acc, axis=0, keepdims=True)
        for m in range(4):
            col_line[pl.ds(j * 4 + m, 1), :] = line[:, m * 128 : m * 128 + 128]

    pl.loop(0, 4)(some_columns)
    pl.semaphore_wait(barrier, NB - 1 + NP - 1)
    start_columns(0, 0)
    pl.loop(4, 8)(some_columns)
    start_columns(0, 1)

    start_rows(2 * ITERS, tot_acc, 0, 8)
    views_t[...] = views[...].astype(F32).T.astype(BF16)

    @pl.loop(0, R // 256)
    def _(i):
        rows = aligned(i, 256)
        v = pre[rows, :]
        t = jnp.tanh(gelu_a * (v + gelu_b * (v * v * v)))
        pre[rows, :] = 0.5 * (1.0 + t) + 0.5 * v * (1.0 - t * t) * (gelu_a * (1.0 + 3.0 * gelu_b * (v * v)))

    rows_of(0)
    for q in range(8):
        at = jnp.broadcast_to(pos[:, q * 128 : q * 128 + 128], (128, 128)).astype(F32).T
        for k in range(8):
            here = (iota((128, 128), 1) + k * 128).astype(F32)
            perm_t[q * 128 : q * 128 + 128, k * 128 : k * 128 + 128] = onehot(at == here)

    columns_of(1)
    emb_t[...] = emb[:, aligned(part_of, 128)].astype(F32).T.astype(BF16)
    own = perm[aligned(p, RC), :]
    r0 = raw[...]
    r1 = r0.astype(BF16)
    r0 = r0 - r1.astype(F32)
    r2 = r0.astype(BF16)
    r3 = (r0 - r2.astype(F32)).astype(BF16)
    raw_own[...] = dot(own, r1) + dot(own, r2) + dot(own, r3)
    spread(finish_rows(2 * ITERS) * loss_gain, tot_b, 0, 8)
    rows_of(1)
    columns_of(2)
    rows_of(2)

    def view_copy(k):
        return copy(vg_send.at[k], vg_recv.at[k], vg_sem, k, proto_peer(k))

    def some_scores(h, m, part):
        q = m + h * 4
        top, low = aligned(q * 8 + part, 16), aligned(q * 8 + part + 4, 16)
        d_top, d_low = aligned(m * 8 + part, 16), aligned(m * 8 + part + 4, 16)
        t_top, t_low = tot_b[top, :], tot_b[low, :]
        r_top, r_low = row_b[top, :], row_b[low, :]
        for j in range(WV):
            cols = slice(j * 128, j * 128 + 128)
            c = c_ref[j : j + 1, :]
            e_top, e_low = eh[top, cols], eh[low, cols]
            dsc[h][d_top, cols] = (e_top * t_top - (e_low * e_low) * c * r_low).astype(BF16)
            dsc[h][d_low, cols] = (e_low * t_low - (e_top * e_top) * c * r_top).astype(BF16)

    def view_part(h, m):
        return dot(dsc[h][aligned(m, RC), :], unit[...])

    def send_part(h, m, part):
        k = lax.rem(m + h * 4 + NP - p, NP)
        vg_send[k] = part.astype(BF16)

        @pl.when(k > 0)
        def _():
            view_copy(k).start()

        @pl.when(k == 0)
        def _():
            vg_own[...] = part

    spread(finish_rows(2 * ITERS - 2) * loss_gain, row_b, 0, 4)

    @pl.loop(0, 16)
    def _(i):
        some_scores(0, i // 4, i % 4)

    spread(finish_rows(2 * ITERS - 1) * loss_gain, row_b, 4, 4)

    @pl.loop(1, 5)
    def _(i):
        m = lax.rem(p + i, 4)
        part = view_part(0, m)
        for n in range(4):
            some_scores(1, m, n)
        send_part(0, m, part)

    @pl.loop(1, 5)
    def _(i):
        m = lax.rem(p + i, 4)
        send_part(1, m, view_part(1, m))

    def y_peer(k):
        return (lax.rem(y + k, 4) * 4 + z, p)

    def z_peer(k):
        return (y * 4 + lax.rem(z + k, 4), p)

    def back(i, k):
        return lax.rem(i + 4 - k, 4)

    def first_a(k):
        return copy(ua_send.at[k], ua_recv.at[k], up_sem.at[0], k, y_peer(k))

    def first_b(k):
        return copy(ub_send.at[k], ub_recv.at[k], up_sem.at[1], k, z_peer(k))

    @pl.loop(1, 5)
    def _(kk):
        k = lax.rem(kk, 4)
        to_y = lax.rem(y + k, 4)

        cols = aligned(to_y, 4 * CC)
        parts = dot(views_t[:, :512], dsc[0][:, cols]) + dot(views_t[:, 512:], dsc[1][:, cols])
        for i in range(4):
            part = parts[:, i * CC : i * CC + CC]
            m = back(i, z)
            ua_send[k, i] = part[:, :Z].astype(BF16)
            ub_send[m, to_y] = part[:, Z:].astype(BF16)

            @pl.when(k == 0)
            def _():
                ua_own[i] = part[:, :Z]

            @pl.when(m == 0)
            def _():
                ub_own[to_y] = part[:, Z:]

        @pl.when(kk < 4)
        def _():
            first_a(kk).start()

    @pl.loop(1, 4)
    def _(k):
        first_b(k).start()

    view_grad = vg_own[...]
    for k in range(1, NP):
        view_copy(k).wait_recv()
        view_grad = view_grad + vg_recv[k].astype(F32)
    out = raw_own[...]
    inv = lax.rsqrt(jnp.sum(out * out, axis=1, keepdims=True) + norm_eps)
    along = jnp.sum(out * view_grad, axis=1, keepdims=True)
    mine = (inv * view_grad - out * (inv * inv * inv) * along).astype(BF16)
    dr_send[...] = mine
    dr_all[aligned(p, RC), :] = mine

    def raw_copy(k, owner):
        return copy(dr_send, dr_all.at[aligned(owner, RC), :], dr_sem, k, proto_peer(k))

    @pl.loop(1, NP)
    def _(k):
        raw_copy(k, p).start()

    def second_a(k):
        return copy(sa_send.at[k], sa_recv.at[k], up_sem.at[2], k, z_peer(k))

    def second_b(k):
        return copy(sb_send.at[k], sb_recv.at[k], up_sem.at[3], k, y_peer(k))

    @pl.loop(1, 4)
    def _(k):
        first_a(k).wait_recv()
        first_b(k).wait_recv()

    def sum_a(i):
        return (ua_own[i] + ua_recv[1, i].astype(F32)) + (ua_recv[2, i].astype(F32) + ua_recv[3, i].astype(F32))

    def sum_b(i):
        return (ub_own[i] + ub_recv[1, i].astype(F32)) + (ub_recv[2, i].astype(F32) + ub_recv[3, i].astype(F32))

    @pl.loop(1, 4)
    def _(k):
        sa_send[k] = sum_a(lax.rem(z + k, 4)).astype(BF16)
        second_a(k).start()
        sb_send[k] = sum_b(lax.rem(y + k, 4)).astype(BF16)
        second_b(k).start()

    ua_own[z] = sum_a(z)
    ub_own[y] = sum_b(y)

    @pl.loop(1, NP)
    def _(k):
        raw_copy(k, proto_source(k)).wait_recv()

    d_raw[...] = dot(perm_t[...], dr_all[...]).astype(BF16)

    @pl.loop(0, R // 256)
    def _(i):
        rows = aligned(i, 256)
        d_pre[rows, :] = (pre[rows, :] * dot_t(d_raw[rows, :], w_out[...])).astype(BF16)

    gi = dot(emb_t[...], d_pre[...]).reshape(8, 16, H)
    for m in range(2):
        gi_m = jnp.concatenate([gi[:, :, m * 128 : m * 128 + 128], gi[:, :, m * 128 + 256 : m * 128 + 384]], axis=2)
        gi_f[:, m] = gi_m
        gi_send[:, m] = gi_m.astype(BF16)

    def in_copy(k):
        q = lax.rem(b + k, NB)
        return copy(gi_send.at[q // 2, q % 2], gi_recv.at[k], gi_sem, k, batch_peer(k))

    @pl.loop(1, NB)
    def _(k):
        in_copy(k).start()

    go = dot_tl(hidden[...], d_raw[...]).reshape(NB, H // NB, Z)
    go_f[...] = go
    go_send[...] = go.astype(BF16)

    def out_copy(k):
        return copy(go_send.at[lax.rem(b + k, NB)], go_recv.at[k], go_sem, k, batch_peer(k))

    @pl.loop(1, NB)
    def _(k):
        out_copy(k).start()

    @pl.loop(1, 4)
    def _(k):
        second_a(k).wait_recv()
        second_b(k).wait_recv()

    def finish_proto(own, recv, h):
        grad = own
        for k in range(1, 4):
            grad = grad + recv[k].astype(F32)
        grad = grad.T
        f = proto[aligned(b * 2 + h, Z), :].astype(F32)
        inv = lax.rsqrt(jnp.sum(f * f, axis=1, keepdims=True) + norm_eps)
        along = jnp.sum(f * grad, axis=1, keepdims=True)
        gproto[y, z, h] = (inv * grad - f * (inv * inv * inv) * along).astype(BF16)

    finish_proto(ua_own[z], sa_recv, 0)
    finish_proto(ub_own[y], sb_recv, 1)

    def third_a(k, i):
        return copy(gproto.at[y, i, 0], gproto.at[y, i, 0], up_sem.at[4], k, z_peer(k))

    def third_b(k, i):
        return copy(gproto.at[i, z, 1], gproto.at[i, z, 1], up_sem.at[5], k, y_peer(k))

    @pl.loop(1, 4)
    def _(k):
        third_a(k, z).start()
        third_b(k, y).start()

    @pl.loop(1, NB)
    def _(k):
        in_copy(k).wait_recv()

    total = gi_f[b // 2, b % 2]
    for k in range(1, NB):
        total = total + gi_recv[k].astype(F32)
    total = total.astype(BF16)
    gx_send[...] = total

    def tile(q, h):
        return pl.ds(pl.multiple_of((q % 2 + 2 * h) * 128, 128), 128)

    gin[part_of, b // 2, :, tile(b, 0)] = total[:, :128]
    gin[part_of, b // 2, :, tile(b, 1)] = total[:, 128:]

    def x_peer(k):
        return (b, lax.rem(x + k, 4) * 2 + core)

    other_core = (b, x * 2 + 1 - core)

    def a_along_x(k, owner):
        return copy(gx_send.at[:, pl.ds(0, 128)], gin.at[core * 4 + owner, b // 2, :, tile(b, 0)], ax_sem, k, x_peer(k))

    def b_along_batch(k, q):
        return copy(gx_send.at[:, pl.ds(128, 128)], gin.at[part_of, q // 2, :, tile(q, 1)], bb_sem, k, batch_peer(k))

    @pl.loop(1, 4)
    def _(k):
        a_along_x(k, x).start()

    @pl.loop(1, NB)
    def _(k):
        b_along_batch(k, b).start()

    total = go_f[b]
    for k in range(1, NB):
        out_copy(k).wait_recv()
        total = total + go_recv[k].astype(F32)
    total = total.astype(BF16)
    goa_send[...] = total
    gout[b] = total

    def out_all(k, owner):
        return copy(goa_send, gout.at[owner], goa_sem, k, batch_peer(k))

    @pl.loop(1, NB)
    def _(k):
        out_all(k, b).start()

    @pl.loop(1, 4)
    def _(k):
        a_along_x(k, back(x, k)).wait_recv()

    def a_plane(q, c):
        return gin.at[pl.ds(c * 4, 4), q // 2, :, tile(q, 0)]

    def a_along_batch(k, q):
        return copy(a_plane(q, core), a_plane(q, core), ab_sem, k, batch_peer(k))

    def a_to_core(k, c):
        q = batch_source(k)
        return copy(a_plane(q, c), a_plane(q, c), ac_sem, k, other_core)

    @pl.loop(1, NB)
    def _(k):
        a_along_batch(k, b).start()

    a_to_core(0, core).start()

    @pl.loop(1, 4)
    def _(k):
        third_a(k, back(z, k)).wait_recv()
        third_b(k, back(y, k)).wait_recv()

    def fourth_a(k, i):
        return copy(gproto.at[i, :, 0], gproto.at[i, :, 0], up_sem.at[6], k, y_peer(k))

    def fourth_b(k, i):
        return copy(gproto.at[:, i, 1], gproto.at[:, i, 1], up_sem.at[7], k, z_peer(k))

    @pl.loop(1, 4)
    def _(k):
        fourth_a(k, y).start()
        fourth_b(k, z).start()

    def b_slab(i, c):
        return gin.at[c * 4 + i, :, :, pl.ds(256, 256)]

    def b_along_x(k, i):
        return copy(b_slab(i, core), b_slab(i, core), bx_sem, k, x_peer(k))

    def b_to_core(k, c):
        return copy(b_slab(back(x, k), c), b_slab(back(x, k), c), bc_sem, k, other_core)

    @pl.loop(1, NB)
    def _(k):
        b_along_batch(k, batch_source(k)).wait_recv()

    @pl.loop(1, 4)
    def _(k):
        b_along_x(k, x).start()

    b_to_core(0, core).start()

    @pl.loop(1, NB)
    def _(k):
        a_along_batch(k, batch_source(k)).wait_recv()
        a_to_core(k, core).start()

    @pl.loop(1, 4)
    def _(k):
        b_along_x(k, back(x, k)).wait_recv()
        b_to_core(k, core).start()

    @pl.loop(0, NB)
    def _(k):
        a_to_core(k, 1 - core).wait_recv()
        a_to_core(k, core).wait_send()

    @pl.loop(0, 4)
    def _(k):
        b_to_core(k, 1 - core).wait_recv()
        b_to_core(k, core).wait_send()

    @pl.loop(1, NB)
    def _(k):
        out_all(k, batch_source(k)).wait_recv()
        for it in range(ITERS):
            column_copy(it, 0, k).wait_send()
            column_copy(it, 1, k).wait_send()
        out_copy(k).wait_send()
        out_all(k, b).wait_send()
        in_copy(k).wait_send()
        a_along_batch(k, b).wait_send()
        b_along_batch(k, b).wait_send()

    @pl.loop(1, NP)
    def _(k):
        for slot in range(2 * ITERS + 1):
            row_copy(slot, k).wait_send()
        view_copy(k).wait_send()
        raw_copy(k, p).wait_send()

    @pl.loop(1, 4)
    def _(k):
        fourth_a(k, back(y, k)).wait_recv()
        fourth_b(k, back(z, k)).wait_recv()
        first_a(k).wait_send()
        first_b(k).wait_send()
        second_a(k).wait_send()
        second_b(k).wait_send()
        third_a(k, z).wait_send()
        third_b(k, y).wait_send()
        fourth_a(k, y).wait_send()
        fourth_b(k, z).wait_send()
        a_along_x(k, x).wait_send()
        b_along_x(k, x).wait_send()


def body(embeddings, pairing, w_in, w_out, prototypes):
    vmem = pl.BlockSpec(memory_space=pltpu.VMEM)
    hbm = pl.BlockSpec(memory_space=pl.ANY)
    out = lambda *shape: pltpu.VMEM(shape, BF16)
    dma = lambda *shape: pltpu.SemaphoreType.DMA(shape)
    v = pltpu.VMEM
    grad_in, grad_out, grad_proto = pl.pallas_call(
        kernel,
        name="swav_step",
        out_shape=(out(NP, 8, 16, H), out(NB, H // NB, Z), out(4, 4, 2, Z, Z)),
        in_specs=[hbm, vmem, hbm, hbm, vmem],
        out_specs=(vmem,) * 3,
        scratch_shapes=[
            v((R, E), BF16), v((E, H), BF16), v((H, Z), BF16), v((R, H), F32), v((R, H), BF16), v((R, Z), F32), v((R, R), BF16), v((R, R), BF16),
            v((R, Z), BF16), v((Z, R), BF16), v((128, R), BF16), v((W, Z), BF16), v((R, W), F32), v((R // 2, W), BF16), v((R // 2, W), BF16),
            v((R, 128), F32), v((R, 128), F32), v((R, 128), BF16), v((R, 128), F32), v((RC, Z), F32), v((WV, 128), F32),
            v((8, W), F32), v((WV, 128), F32), v((ITERS, 2, 16, 128), BF16), v((ITERS, 2, NB, 16, 128), BF16),
            v((2 * ITERS + 1, 8, 128), F32), v((2 * ITERS + 1, NP, 8, 128), F32),
            v((R, Z), BF16), v((NP, RC, Z), BF16), v((NP, RC, Z), BF16), v((RC, Z), F32),
            v((RC, Z), BF16), v((R, Z), BF16), v((R, Z), BF16), v((R, H), BF16),
            v((4, 4, Z, Z), BF16), v((4, 4, Z, Z), BF16), v((4, Z, Z), F32),
            v((4, 4, Z, Z), BF16), v((4, 4, Z, Z), BF16), v((4, Z, Z), F32),
            v((4, Z, Z), BF16), v((4, Z, Z), BF16), v((4, Z, Z), BF16), v((4, Z, Z), BF16),
            v((NB, H // NB, Z), F32), v((NB, H // NB, Z), BF16), v((NB, H // NB, Z), BF16), v((H // NB, Z), BF16),
            v((8, 2, 16, 256), F32), v((8, 2, 16, 256), BF16), v((NB, 16, 256), BF16), v((16, 256), BF16),
            dma(ITERS, 2, 2, NB), dma(2 * ITERS + 1, 2, NP), dma(2, NP), dma(2, NP), dma(8, 2, 4),
            dma(2, NB), dma(2, NB), dma(2, NB), dma(2, 4), dma(2, NB), dma(2, NB), dma(2, NB), dma(2, 4), dma(2, 4), dma(3),
        ],
        compiler_params=pltpu.CompilerParams(
            collective_id=0, has_side_effects=True, vmem_limit_bytes=60 << 20
        ),
    )(embeddings, pairing.reshape(8, 128), w_in, w_out, prototypes)
    return (
        grad_in.reshape(E, H).astype(F32),
        grad_out.reshape(H, Z).astype(F32),
        grad_proto.reshape(W, Z).astype(F32),
    )


def solution(mesh):
    return jax.shard_map(
        body,
        mesh=mesh,
        in_specs=(P("batch", None), P("batch"), P(), P(), P("proto", None)),
        out_specs=(P(), P(), P("proto", None)),
        check_vma=False,
    )
```

```python
import math

import jax
import jax.numpy as jnp
from jax import lax
from jax.experimental import pallas as pl
from jax.experimental.pallas import tpu as pltpu
from jax.sharding import PartitionSpec as P

ITERS = 3
norm_eps = 1e-06
loss_gain = 64.0 / 0.1
half_log2 = 10.0 * math.log2(math.e)
gelu_a = math.sqrt(2.0 / math.pi)
gelu_b = 0.044715

F32, BF16 = jnp.float32, jnp.bfloat16
MESH = pl.DeviceIdType.MESH
NB, NP = 16, 8
R, E, H, Z, W = 1024, 1024, 512, 128, 4096
RC = R // NP
CC = W // NB
WV = W // 128


def dot(a, b):
    return jnp.dot(a, b, preferred_element_type=F32)


def dot_t(a, b):
    return lax.dot_general(a, b, (((1,), (1,)), ((), ())), preferred_element_type=F32)


def dot_tl(a, b):
    return lax.dot_general(a, b, (((0,), (0,)), ((), ())), preferred_element_type=F32)


def iota(shape, dim):
    return lax.broadcasted_iota(jnp.int32, shape, dim)


def onehot(mask):
    return jnp.where(mask, 1.0, 0.0).astype(BF16)


def aligned(i, n):
    return pl.ds(pl.multiple_of(i * n, n), n)


def as_row(x):
    return jnp.concatenate([x[k : k + 1, :] for k in range(x.shape[0])], axis=1)


def kernel(
    emb_hbm, pairing, w_in_hbm, w_out_hbm, proto,
    gin, gout, gproto,
    emb, w_in, w_out, pre, hidden, raw, perm, perm_t, views, views_t, emb_t, unit, eh, low_d, high_d,
    tot_acc, row_b, row_n, tot_b, raw_own, c_ref,
    col_acc, col_line, col_send, col_recv, row_send, row_recv,
    vun, vg_send, vg_recv, vg_own, dr_send, dr_all, d_raw, d_pre,
    ua_send, ua_recv, ua_own, ub_send, ub_recv, ub_own, sa_send, sa_recv, sb_send, sb_recv,
    go_f, go_send, go_recv, goa_send, gi_f, gi_send, gi_recv, gx_send,
    col_sem, row_sem, vg_sem, dr_sem, up_sem, go_sem, goa_sem, gi_sem, ax_sem, ab_sem, ac_sem, bb_sem, bx_sem, bc_sem, in_sem,
):
    dsc = (low_d, high_d)
    b = lax.axis_index("batch")
    p = lax.axis_index("proto")
    x, core = p // 2, p % 2
    part_of = core * 4 + x
    y, z = b // 4, b % 4

    def batch_peer(k):
        return (lax.rem(b + k, NB), p)

    def batch_source(k):
        return lax.rem(b + NB - k, NB)

    def proto_peer(k):
        return (b, lax.rem(p + k, NP))

    def proto_source(k):
        return lax.rem(p + NP - k, NP)

    def copy(src, dst, sem, k, device):
        return pltpu.make_async_remote_copy(
            src_ref=src, dst_ref=dst, send_sem=sem.at[0, k], recv_sem=sem.at[1, k],
            device_id=device, device_id_type=MESH,
        )

    loads = [
        pltpu.make_async_copy(src, dst, in_sem.at[i])
        for i, (src, dst) in enumerate(((emb_hbm, emb), (w_in_hbm, w_in), (w_out_hbm, w_out)))
    ]
    for load in loads:
        load.start()

    barrier = pltpu.get_barrier_semaphore()

    @pl.loop(1, NB)
    def _(k):
        pl.semaphore_signal(barrier, inc=1, device_id=batch_peer(k), device_id_type=MESH)

    @pl.loop(1, NP)
    def _(k):
        pl.semaphore_signal(barrier, inc=1, device_id=proto_peer(k), device_id_type=MESH)

    mate = pairing[...]
    lead = mate > iota((8, 128), 0) * 128 + iota((8, 128), 1)
    lead_f = jnp.where(lead, 1.0, 0.0)
    within = dot(lead_f, jnp.where(iota((128, 128), 0) < iota((128, 128), 1), 1.0, 0.0))
    chunk = dot(lead_f, jnp.ones((128, 128), F32))
    before = [jnp.zeros((1, 128), F32)]
    for k in range(7):
        before.append(before[-1] + chunk[k : k + 1, :])
    rank = within + jnp.concatenate(before, axis=0)
    high = jnp.floor(rank * (1.0 / 32.0))
    low = rank - 32.0 * high
    mate_row = as_row(mate)

    @pl.loop(0, 8)
    def _(i):
        perm[aligned(i, 128), :] = onehot(mate_row == iota((128, R), 0) + i * 128)

    halves = jnp.concatenate([as_row(high), as_row(low), jnp.zeros((14, R), F32)], axis=0).astype(BF16)
    of_mate = dot(halves, perm[...])
    lead_row = as_row(lead_f)
    rank_row = jnp.where(lead_row > 0.5, as_row(rank), 32.0 * of_mate[0:1, :] + of_mate[1:2, :])
    pos = rank_row + 64.0 * jnp.floor(rank_row * (1.0 / 64.0)) + jnp.where(lead_row > 0.5, 0.0, 64.0)
    pos = pos.astype(jnp.int32)

    @pl.loop(0, 8)
    def _(i):
        perm[aligned(i, 128), :] = onehot(pos == iota((128, R), 0) + i * 128)

    for load in loads:
        load.wait()

    @pl.loop(0, R // 256)
    def _(i):
        rows = aligned(i, 256)
        v = dot(emb[rows, :], w_in[...])
        pre[rows, :] = v
        hid = (0.5 * v * (1.0 + jnp.tanh(gelu_a * (v + gelu_b * (v * v * v))))).astype(BF16)
        hidden[rows, :] = hid
        out = dot(hid, w_out[...])
        raw[rows, :] = out
        inv = lax.rsqrt(jnp.sum(out * out, axis=1, keepdims=True) + norm_eps)
        vun[rows, :] = (out * inv).astype(BF16)
        for m in range(8):
            some = aligned(i * 8 + m, 128)
            f = proto[some, :].astype(F32)
            inv = lax.rsqrt(jnp.sum(f * f, axis=1, keepdims=True) + norm_eps)
            unit[some, :] = (f * inv).astype(BF16)

    views[...] = dot(perm[...], vun[...]).astype(BF16)

    def column_copy(it, h, k):
        return copy(col_send.at[it, h], col_recv.at[it, h, k], col_sem.at[it, h], k, batch_peer(k))

    def start_columns(it, h):
        col_send[it, h] = col_line[h * 16 : h * 16 + 16, :].astype(BF16)

        @pl.loop(1, NB)
        def _(k):
            column_copy(it, h, k).start()

    def finish_columns(it, h):
        @pl.loop(1, NB)
        def _(k):
            column_copy(it, h, k).wait_recv()

        total = col_send[it, h].astype(F32)
        for k in range(1, NB):
            total = total + col_recv[it, h, k].astype(F32)
        c_ref[h * 16 : h * 16 + 16, :] = 1.0 / total

    def row_copy(slot, k):
        return copy(row_send.at[slot], row_recv.at[slot, k], row_sem.at[slot], k, proto_peer(k))

    def start_rows(slot, src, first, count):
        for q in range(count):
            at = (first + q) * 128
            row_send[slot, q : q + 1, :] = jnp.sum(src[at : at + 128, :].T, axis=0, keepdims=True)

        @pl.loop(1, NP)
        def _(k):
            row_copy(slot, k).start()

    def finish_rows(slot):
        @pl.loop(1, NP)
        def _(k):
            row_copy(slot, k).wait_recv()

        total = row_send[slot]
        for k in range(1, NP):
            total = total + row_recv[slot, k]
        return 1.0 / total

    def spread(lines, dst, first, count):
        for q in range(count):
            at = (first + q) * 128
            dst[at : at + 128, :] = jnp.broadcast_to(lines[q : q + 1, :], (128, 128)).T.astype(dst.dtype)

    def pairwise(terms):
        while len(terms) > 1:
            terms = [terms[m] + terms[m + 1] for m in range(0, len(terms), 2)]
        return terms[0]

    def column_sweep(it, rows_half):
        for h in range(2):
            lines = range(h * 16, h * 16 + 16)

            def some_rows(i, acc):
                rows = [pl.ds(pl.multiple_of(i * 64 + m * 16, 16), 16) for m in range(4)]
                r = [row_n[pl.ds(pl.multiple_of(rows_half * 512 + i * 64 + m * 16, 16), 16), :] for m in range(4)]
                out = []
                for j, a in zip(lines, acc):
                    part = pairwise([dsc[rows_half][rows[m], j * 128 : j * 128 + 128] * r[m] for m in range(4)]).astype(F32)
                    out.append(a + (part[0:8] + part[8:16]))
                return tuple(out)

            if rows_half == 0:
                acc = tuple(jnp.zeros((8, 128), F32) for _ in lines)
            else:
                acc = tuple(col_acc[:, j * 128 : j * 128 + 128] for j in lines)
            acc = lax.fori_loop(0, 8, some_rows, acc)
            if rows_half == 0:
                for j, a in zip(lines, acc):
                    col_acc[:, j * 128 : j * 128 + 128] = a
            else:
                for j, a in zip(lines, acc):
                    col_line[j : j + 1, :] = jnp.sum(a, axis=0, keepdims=True)
                start_columns(it, h)

    def row_sweep(h, rows_half):
        lines = range(h * 16, h * 16 + 16)
        c = [jnp.broadcast_to(c_ref[j : j + 1, :], (16, 128)).astype(BF16) for j in lines]

        @pl.loop(0, 32)
        def _(i):
            near, rows = aligned(i, 16), aligned(i + rows_half * 32, 16)
            parts = []
            for g in range(0, 16, 4):
                some = [dsc[rows_half][near, (h * 16 + g + m) * 128 : (h * 16 + g + m + 1) * 128] * c[g + m] for m in range(4)]
                parts.append(pairwise(some).astype(F32))
            total = pairwise(parts)
            row_b[rows, :] = total if h == 0 else row_b[rows, :] + total

    def rows_of(it):
        finish_columns(it, 0)
        row_sweep(0, 0)
        row_sweep(0, 1)
        finish_columns(it, 1)
        for h in range(2):
            row_sweep(1, h)
            start_rows(it * 2 + h, row_b, h * 4, 4)

    def columns_of(it):
        for h in range(2):
            spread(finish_rows(it * 2 - 2 + h), row_n, h * 4, 4)
            column_sweep(it, h)

    tot_acc[...] = jnp.zeros_like(tot_acc)
    row_send[...] = jnp.zeros_like(row_send)

    def some_columns(j):
        cols = aligned(j, 512)
        u = unit[cols, :]

        acc = jnp.zeros((8, 512), F32)
        for i in range(8):
            rows = slice(i * 128, i * 128 + 128)
            e = jnp.exp2(dot_t(views[rows, :], u) * half_log2)
            eh[rows, cols] = e
            tot_acc[rows, :] += (e[:, 0:128] + e[:, 128:256]) + (e[:, 256:384] + e[:, 384:512])
            e = e * e
            dsc[i // 4][i % 4 * 128 : i % 4 * 128 + 128, cols] = e.astype(BF16)
            acc = acc + jnp.sum(e.reshape(16, 8, 512), axis=0)
        line = jnp.sum(acc, axis=0, keepdims=True)
        for m in range(4):
            col_line[pl.ds(j * 4 + m, 1), :] = line[:, m * 128 : m * 128 + 128]

    pl.loop(0, 5)(some_columns)
    pl.semaphore_wait(barrier, NB - 1 + NP - 1)
    start_columns(0, 0)
    pl.loop(5, 8)(some_columns)
    start_columns(0, 1)

    start_rows(2 * ITERS, tot_acc, 0, 8)
    views_t[...] = views[...].astype(F32).T.astype(BF16)

    @pl.loop(0, R // 256)
    def _(i):
        rows = aligned(i, 256)
        v = pre[rows, :]
        t = jnp.tanh(gelu_a * (v + gelu_b * (v * v * v)))
        pre[rows, :] = 0.5 * (1.0 + t) + 0.5 * v * (1.0 - t * t) * (gelu_a * (1.0 + 3.0 * gelu_b * (v * v)))

    rows_of(0)
    for q in range(8):
        at = jnp.broadcast_to(pos[:, q * 128 : q * 128 + 128], (128, 128)).astype(F32).T
        for k in range(8):
            here = (iota((128, 128), 1) + k * 128).astype(F32)
            perm_t[q * 128 : q * 128 + 128, k * 128 : k * 128 + 128] = onehot(at == here)

    columns_of(1)
    emb_t[...] = emb[:, aligned(part_of, 128)].astype(F32).T.astype(BF16)
    own = perm[aligned(p, RC), :]
    r0 = raw[...]
    r1 = r0.astype(BF16)
    r0 = r0 - r1.astype(F32)
    r2 = r0.astype(BF16)
    r3 = (r0 - r2.astype(F32)).astype(BF16)
    raw_own[...] = dot(own, r1) + dot(own, r2) + dot(own, r3)
    spread(finish_rows(2 * ITERS) * loss_gain, tot_b, 0, 8)
    rows_of(1)
    columns_of(2)
    rows_of(2)

    def view_copy(k):
        return copy(vg_send.at[k], vg_recv.at[k], vg_sem, k, proto_peer(k))

    def some_scores(h, m, part):
        q = m + h * 4
        top, low = aligned(q * 8 + part, 16), aligned(q * 8 + part + 4, 16)
        d_top, d_low = aligned(m * 8 + part, 16), aligned(m * 8 + part + 4, 16)
        t_top, t_low = tot_b[top, :], tot_b[low, :]
        r_top, r_low = row_b[top, :], row_b[low, :]
        for j in range(WV):
            cols = slice(j * 128, j * 128 + 128)
            c = c_ref[j : j + 1, :]
            e_top, e_low = eh[top, cols], eh[low, cols]
            dsc[h][d_top, cols] = (e_top * t_top - (e_low * e_low) * c * r_low).astype(BF16)
            dsc[h][d_low, cols] = (e_low * t_low - (e_top * e_top) * c * r_top).astype(BF16)

    def view_part(h, m):
        return dot(dsc[h][aligned(m, RC), :], unit[...])

    def send_part(h, m, part):
        k = lax.rem(m + h * 4 + NP - p, NP)
        vg_send[k] = part.astype(BF16)

        @pl.when(k > 0)
        def _():
            view_copy(k).start()

        @pl.when(k == 0)
        def _():
            vg_own[...] = part

    spread(finish_rows(2 * ITERS - 2) * loss_gain, row_b, 0, 4)

    @pl.loop(0, 16)
    def _(i):
        some_scores(0, i // 4, i % 4)

    spread(finish_rows(2 * ITERS - 1) * loss_gain, row_b, 4, 4)

    @pl.loop(1, 5)
    def _(i):
        m = lax.rem(p + i, 4)
        part = view_part(0, m)
        for n in range(4):
            some_scores(1, m, n)
        send_part(0, m, part)

    @pl.loop(1, 5)
    def _(i):
        m = lax.rem(p + i, 4)
        send_part(1, m, view_part(1, m))

    def y_peer(k):
        return (lax.rem(y + k, 4) * 4 + z, p)

    def z_peer(k):
        return (y * 4 + lax.rem(z + k, 4), p)

    def back(i, k):
        return lax.rem(i + 4 - k, 4)

    def first_a(k):
        return copy(ua_send.at[k], ua_recv.at[k], up_sem.at[0], k, y_peer(k))

    def first_b(k):
        return copy(ub_send.at[k], ub_recv.at[k], up_sem.at[1], k, z_peer(k))

    @pl.loop(1, 5)
    def _(kk):
        k = lax.rem(kk, 4)
        to_y = lax.rem(y + k, 4)

        cols = aligned(to_y, 4 * CC)
        parts = dot(views_t[:, :512], dsc[0][:, cols]) + dot(views_t[:, 512:], dsc[1][:, cols])
        for i in range(4):
            part = parts[:, i * CC : i * CC + CC]
            m = back(i, z)
            ua_send[k, i] = part[:, :Z].astype(BF16)
            ub_send[m, to_y] = part[:, Z:].astype(BF16)

            @pl.when(k == 0)
            def _():
                ua_own[i] = part[:, :Z]

            @pl.when(m == 0)
            def _():
                ub_own[to_y] = part[:, Z:]

        @pl.when(kk < 4)
        def _():
            first_a(kk).start()

    @pl.loop(1, 4)
    def _(k):
        first_b(k).start()

    view_grad = vg_own[...]
    for k in range(1, NP):
        view_copy(k).wait_recv()
        view_grad = view_grad + vg_recv[k].astype(F32)
    out = raw_own[...]
    inv = lax.rsqrt(jnp.sum(out * out, axis=1, keepdims=True) + norm_eps)
    along = jnp.sum(out * view_grad, axis=1, keepdims=True)
    mine = (inv * view_grad - out * (inv * inv * inv) * along).astype(BF16)
    dr_send[...] = mine
    dr_all[aligned(p, RC), :] = mine

    def raw_copy(k, owner):
        return copy(dr_send, dr_all.at[aligned(owner, RC), :], dr_sem, k, proto_peer(k))

    @pl.loop(1, NP)
    def _(k):
        raw_copy(k, p).start()

    def second_a(k):
        return copy(sa_send.at[k], sa_recv.at[k], up_sem.at[2], k, z_peer(k))

    def second_b(k):
        return copy(sb_send.at[k], sb_recv.at[k], up_sem.at[3], k, y_peer(k))

    @pl.loop(1, 4)
    def _(k):
        first_a(k).wait_recv()
        first_b(k).wait_recv()

    def sum_a(i):
        return (ua_own[i] + ua_recv[1, i].astype(F32)) + (ua_recv[2, i].astype(F32) + ua_recv[3, i].astype(F32))

    def sum_b(i):
        return (ub_own[i] + ub_recv[1, i].astype(F32)) + (ub_recv[2, i].astype(F32) + ub_recv[3, i].astype(F32))

    @pl.loop(1, 4)
    def _(k):
        sa_send[k] = sum_a(lax.rem(z + k, 4)).astype(BF16)
        second_a(k).start()
        sb_send[k] = sum_b(lax.rem(y + k, 4)).astype(BF16)
        second_b(k).start()

    ua_own[z] = sum_a(z)
    ub_own[y] = sum_b(y)

    @pl.loop(1, NP)
    def _(k):
        raw_copy(k, proto_source(k)).wait_recv()

    d_raw[...] = dot(perm_t[...], dr_all[...]).astype(BF16)

    @pl.loop(0, R // 256)
    def _(i):
        rows = aligned(i, 256)
        d_pre[rows, :] = (pre[rows, :] * dot_t(d_raw[rows, :], w_out[...])).astype(BF16)

    gi = dot(emb_t[...], d_pre[...]).reshape(8, 16, H)
    for m in range(2):
        gi_m = jnp.concatenate([gi[:, :, m * 128 : m * 128 + 128], gi[:, :, m * 128 + 256 : m * 128 + 384]], axis=2)
        gi_f[:, m] = gi_m
        gi_send[:, m] = gi_m.astype(BF16)

    def in_copy(k):
        q = lax.rem(b + k, NB)
        return copy(gi_send.at[q // 2, q % 2], gi_recv.at[k], gi_sem, k, batch_peer(k))

    @pl.loop(1, NB)
    def _(k):
        in_copy(k).start()

    go = dot_tl(hidden[...], d_raw[...]).reshape(NB, H // NB, Z)
    go_f[...] = go
    go_send[...] = go.astype(BF16)

    def out_copy(k):
        return copy(go_send.at[lax.rem(b + k, NB)], go_recv.at[k], go_sem, k, batch_peer(k))

    @pl.loop(1, NB)
    def _(k):
        out_copy(k).start()

    @pl.loop(1, 4)
    def _(k):
        second_a(k).wait_recv()
        second_b(k).wait_recv()

    def finish_proto(own, recv, h):
        grad = own
        for k in range(1, 4):
            grad = grad + recv[k].astype(F32)
        grad = grad.T
        f = proto[aligned(b * 2 + h, Z), :].astype(F32)
        inv = lax.rsqrt(jnp.sum(f * f, axis=1, keepdims=True) + norm_eps)
        along = jnp.sum(f * grad, axis=1, keepdims=True)
        gproto[y, z, h] = (inv * grad - f * (inv * inv * inv) * along).astype(BF16)

    finish_proto(ua_own[z], sa_recv, 0)
    finish_proto(ub_own[y], sb_recv, 1)

    def third_a(k, i):
        return copy(gproto.at[y, i, 0], gproto.at[y, i, 0], up_sem.at[4], k, z_peer(k))

    def third_b(k, i):
        return copy(gproto.at[i, z, 1], gproto.at[i, z, 1], up_sem.at[5], k, y_peer(k))

    @pl.loop(1, 4)
    def _(k):
        third_a(k, z).start()
        third_b(k, y).start()

    @pl.loop(1, NB)
    def _(k):
        in_copy(k).wait_recv()

    total = gi_f[b // 2, b % 2]
    for k in range(1, NB):
        total = total + gi_recv[k].astype(F32)
    total = total.astype(BF16)
    gx_send[...] = total

    def tile(q, h):
        return pl.ds(pl.multiple_of((q % 2 + 2 * h) * 128, 128), 128)

    gin[part_of, b // 2, :, tile(b, 0)] = total[:, :128]
    gin[part_of, b // 2, :, tile(b, 1)] = total[:, 128:]

    def x_peer(k):
        return (b, lax.rem(x + k, 4) * 2 + core)

    other_core = (b, x * 2 + 1 - core)

    def a_along_x(k, owner):
        return copy(gx_send.at[:, pl.ds(0, 128)], gin.at[core * 4 + owner, b // 2, :, tile(b, 0)], ax_sem, k, x_peer(k))

    def b_along_batch(k, q):
        return copy(gx_send.at[:, pl.ds(128, 128)], gin.at[part_of, q // 2, :, tile(q, 1)], bb_sem, k, batch_peer(k))

    @pl.loop(1, 4)
    def _(k):
        a_along_x(k, x).start()

    @pl.loop(1, NB)
    def _(k):
        b_along_batch(k, b).start()

    total = go_f[b]
    for k in range(1, NB):
        out_copy(k).wait_recv()
        total = total + go_recv[k].astype(F32)
    total = total.astype(BF16)
    goa_send[...] = total
    gout[b] = total

    def out_all(k, owner):
        return copy(goa_send, gout.at[owner], goa_sem, k, batch_peer(k))

    @pl.loop(1, NB)
    def _(k):
        out_all(k, b).start()

    @pl.loop(1, 4)
    def _(k):
        a_along_x(k, back(x, k)).wait_recv()

    def a_plane(q, c):
        return gin.at[pl.ds(c * 4, 4), q // 2, :, tile(q, 0)]

    def a_along_batch(k, q):
        return copy(a_plane(q, core), a_plane(q, core), ab_sem, k, batch_peer(k))

    def a_to_core(k, c):
        q = batch_source(k)
        return copy(a_plane(q, c), a_plane(q, c), ac_sem, k, other_core)

    @pl.loop(1, NB)
    def _(k):
        a_along_batch(k, b).start()

    a_to_core(0, core).start()

    @pl.loop(1, 4)
    def _(k):
        third_a(k, back(z, k)).wait_recv()
        third_b(k, back(y, k)).wait_recv()

    def fourth_a(k, i):
        return copy(gproto.at[i, :, 0], gproto.at[i, :, 0], up_sem.at[6], k, y_peer(k))

    def fourth_b(k, i):
        return copy(gproto.at[:, i, 1], gproto.at[:, i, 1], up_sem.at[7], k, z_peer(k))

    @pl.loop(1, 4)
    def _(k):
        fourth_a(k, y).start()
        fourth_b(k, z).start()

    def b_slab(i, c):
        return gin.at[c * 4 + i, :, :, pl.ds(256, 256)]

    def b_along_x(k, i):
        return copy(b_slab(i, core), b_slab(i, core), bx_sem, k, x_peer(k))

    def b_to_core(k, c):
        return copy(b_slab(back(x, k), c), b_slab(back(x, k), c), bc_sem, k, other_core)

    @pl.loop(1, NB)
    def _(k):
        b_along_batch(k, batch_source(k)).wait_recv()

    @pl.loop(1, 4)
    def _(k):
        b_along_x(k, x).start()

    b_to_core(0, core).start()

    @pl.loop(1, NB)
    def _(k):
        a_along_batch(k, batch_source(k)).wait_recv()
        a_to_core(k, core).start()

    @pl.loop(1, 4)
    def _(k):
        b_along_x(k, back(x, k)).wait_recv()
        b_to_core(k, core).start()

    @pl.loop(0, NB)
    def _(k):
        a_to_core(k, 1 - core).wait_recv()
        a_to_core(k, core).wait_send()

    @pl.loop(0, 4)
    def _(k):
        b_to_core(k, 1 - core).wait_recv()
        b_to_core(k, core).wait_send()

    @pl.loop(1, NB)
    def _(k):
        out_all(k, batch_source(k)).wait_recv()
        for it in range(ITERS):
            column_copy(it, 0, k).wait_send()
            column_copy(it, 1, k).wait_send()
        out_copy(k).wait_send()
        out_all(k, b).wait_send()
        in_copy(k).wait_send()
        a_along_batch(k, b).wait_send()
        b_along_batch(k, b).wait_send()

    @pl.loop(1, NP)
    def _(k):
        for slot in range(2 * ITERS + 1):
            row_copy(slot, k).wait_send()
        view_copy(k).wait_send()
        raw_copy(k, p).wait_send()

    @pl.loop(1, 4)
    def _(k):
        fourth_a(k, back(y, k)).wait_recv()
        fourth_b(k, back(z, k)).wait_recv()
        first_a(k).wait_send()
        first_b(k).wait_send()
        second_a(k).wait_send()
        second_b(k).wait_send()
        third_a(k, z).wait_send()
        third_b(k, y).wait_send()
        fourth_a(k, y).wait_send()
        fourth_b(k, z).wait_send()
        a_along_x(k, x).wait_send()
        b_along_x(k, x).wait_send()


def body(embeddings, pairing, w_in, w_out, prototypes):
    vmem = pl.BlockSpec(memory_space=pltpu.VMEM)
    hbm = pl.BlockSpec(memory_space=pl.ANY)
    out = lambda *shape: pltpu.VMEM(shape, BF16)
    dma = lambda *shape: pltpu.SemaphoreType.DMA(shape)
    v = pltpu.VMEM
    grad_in, grad_out, grad_proto = pl.pallas_call(
        kernel,
        name="swav_step",
        out_shape=(out(NP, 8, 16, H), out(NB, H // NB, Z), out(4, 4, 2, Z, Z)),
        in_specs=[hbm, vmem, hbm, hbm, vmem],
        out_specs=(vmem,) * 3,
        scratch_shapes=[
            v((R, E), BF16), v((E, H), BF16), v((H, Z), BF16), v((R, H), F32), v((R, H), BF16), v((R, Z), F32), v((R, R), BF16), v((R, R), BF16),
            v((R, Z), BF16), v((Z, R), BF16), v((128, R), BF16), v((W, Z), BF16), v((R, W), F32), v((R // 2, W), BF16), v((R // 2, W), BF16),
            v((R, 128), F32), v((R, 128), F32), v((R, 128), BF16), v((R, 128), F32), v((RC, Z), F32), v((WV, 128), F32),
            v((8, W), F32), v((WV, 128), F32), v((ITERS, 2, 16, 128), BF16), v((ITERS, 2, NB, 16, 128), BF16),
            v((2 * ITERS + 1, 8, 128), F32), v((2 * ITERS + 1, NP, 8, 128), F32),
            v((R, Z), BF16), v((NP, RC, Z), BF16), v((NP, RC, Z), BF16), v((RC, Z), F32),
            v((RC, Z), BF16), v((R, Z), BF16), v((R, Z), BF16), v((R, H), BF16),
            v((4, 4, Z, Z), BF16), v((4, 4, Z, Z), BF16), v((4, Z, Z), F32),
            v((4, 4, Z, Z), BF16), v((4, 4, Z, Z), BF16), v((4, Z, Z), F32),
            v((4, Z, Z), BF16), v((4, Z, Z), BF16), v((4, Z, Z), BF16), v((4, Z, Z), BF16),
            v((NB, H // NB, Z), F32), v((NB, H // NB, Z), BF16), v((NB, H // NB, Z), BF16), v((H // NB, Z), BF16),
            v((8, 2, 16, 256), F32), v((8, 2, 16, 256), BF16), v((NB, 16, 256), BF16), v((16, 256), BF16),
            dma(ITERS, 2, 2, NB), dma(2 * ITERS + 1, 2, NP), dma(2, NP), dma(2, NP), dma(8, 2, 4),
            dma(2, NB), dma(2, NB), dma(2, NB), dma(2, 4), dma(2, NB), dma(2, NB), dma(2, NB), dma(2, 4), dma(2, 4), dma(3),
        ],
        compiler_params=pltpu.CompilerParams(
            collective_id=0, has_side_effects=True, vmem_limit_bytes=60 << 20
        ),
    )(embeddings, pairing.reshape(8, 128), w_in, w_out, prototypes)
    return (
        grad_in.reshape(E, H).astype(F32),
        grad_out.reshape(H, Z).astype(F32),
        grad_proto.reshape(W, Z).astype(F32),
    )


def solution(mesh):
    return jax.shard_map(
        body,
        mesh=mesh,
        in_specs=(P("batch", None), P("batch"), P(), P(), P("proto", None)),
        out_specs=(P(), P(), P("proto", None)),
        check_vma=False,
    )
```
